256 devices in a mesh: rep: 32 (over y, z), shard: 8 (over x, core).
Axes of the slice: x: 4, y: 4, z: 8, core: 2. Of those that a mesh axis runs over, the one named last changes fastest.
Arguments:
- gradient: bfloat16 [32, 1024, 4096], P('rep', None, 'shard'), may hold values from -16 to 16
- feedback: bfloat16 [32, 1024, 4096], P('rep', None, 'shard'), may hold values from -4 to 4
- warm_start: float32 [1024, 64], replicated, may hold values from -6 to 6
- master: float32 [1024, 4096], P('rep', 'shard'), may hold values from -4 to 4
- moment: float32 [1024, 4096], P('rep', 'shard'), may hold values from -1.5 to 1.5
- second: float32 [1024, 4096], P('rep', 'shard'), may hold values from 0.005 to 0.5
Outputs:
- new_feedback: bfloat16 [32, 1024, 4096], P('rep', None, 'shard')
- weights: bfloat16 [1024, 4096], P(None, 'shard')
- master_out: float32 [1024, 4096], P('rep', 'shard')
- moment_out: float32 [1024, 4096], P('rep', 'shard')
- second_out: float32 [1024, 4096], P('rep', 'shard')
- right_factor: float32 [1024, 64], replicated
The draws below stay inside these ranges and needn't reach their ends.
All inputs are finite; a program needn't handle non-finite values.
Results may differ from the reference program's by a relative error of at most 0.001.
Values may be sent and summed in bfloat16 or wider, within the bound.
No kernel may reach another device: no remote copies, remote signals or barrier semaphores. Data moves between devices by JAX's collectives and lax.ppermute only.
A program may use at most 64 MiB of HBM per device.

```python
import math
import jax
import jax.numpy as jnp
from jax import lax

FF = 4096
DW = 1024
RANK = 64
REPLICAS = 32


def draw_gradient(key, part):
    key_cols, key_rows, key_own = jax.random.split(key, 3)
    column_pos = jnp.arange(FF, dtype=jnp.float32) / FF
    replica_pos = jnp.arange(REPLICAS, dtype=jnp.float32) / REPLICAS
    column_scale = jnp.exp(jax.random.uniform(key_cols, (FF,), jnp.float32, 0.0, math.log(10.0)))
    row_scale = jnp.exp(jax.random.uniform(key_rows, (DW,), jnp.float32, 0.0, math.log(4.0)))
    values = jax.random.truncated_normal(key_own, -4.0, 4.0, (REPLICAS, DW, FF), jnp.float32)
    rising = jnp.power(3.0, 0.5 * column_pos)
    base_scale = 0.06
    scale_all = base_scale * (column_scale * rising)[None, None, :] * row_scale[None, :, None]
    scale_all = scale_all * jnp.power(3.0, 0.5 * replica_pos)[:, None, None]
    return jnp.clip(values * scale_all, -16.0, 16.0).astype(jnp.bfloat16)


def block_levels(stream_key, extent, cuts, least, high):
    def one(position, shards_of):
        draws = jax.random.uniform(jax.random.fold_in(jax.random.fold_in(stream_key, 6), position), (shards_of,), jnp.float32, least / len(cuts), high / len(cuts))
        return jnp.repeat(jnp.exp(draws), extent[position] // shards_of).reshape((-1,) + (1,) * (len(extent) - position - 1))

    factor_of = one(*cuts[0])
    for cut in cuts[1:]:
        factor_of = factor_of * one(*cut)
    return factor_of


def gaussian(stream_key, dims, width, most, shards=(), kind=jnp.bfloat16):
    entries = width * jax.random.normal(stream_key, dims, jnp.float32)
    if shards:
        entries = entries * block_levels(stream_key, dims, shards, -0.22, 0.18)
    return jnp.clip(entries, -most, most).astype(kind)


def setup_inputs(seed: int = 0) -> dict:
    keys = jax.random.split(jax.random.key(seed), 7)
    return {
        "gradient": draw_gradient(jax.random.fold_in(keys[6], 71), 0),
        "feedback": gaussian(keys[1], (REPLICAS, DW, FF), 0.5, 4.0, ((0, 32), (2, 8))),
        "warm_start": gaussian(keys[2], (DW, RANK), 1.0, 6.0, (), jnp.float32),
        "master": gaussian(keys[3], (DW, FF), 1.0, 4.0, ((0, 32), (1, 8)), jnp.float32),
        "moment": gaussian(keys[4], (DW, FF), 0.1, 1.5, ((0, 32), (1, 8)), jnp.float32),
        "second": jnp.clip(jnp.exp(math.log(0.5) - 4.6051702 * jax.random.uniform(keys[5], (DW, FF), jnp.float32) ** block_levels(keys[5], (DW, FF), ((0, 32), (1, 8)), -0.2, 0.2)), 0.005, 0.5),
    }


HIGHEST = lax.Precision.HIGHEST
beta_one = 0.9
beta_two = 0.95
learn_rate = 0.02
decay_rate = 0.1
adam_eps = 1e-08
ridge_rate = 1e-06

def lower_inverse(gram):
    matrix_order = gram.shape[0]
    identity = jnp.eye(matrix_order, dtype=jnp.float32)
    ridge_term = ridge_rate * jnp.trace(gram) / matrix_order
    cholesky_lower = jnp.linalg.cholesky(gram + ridge_term * identity)
    return jax.scipy.linalg.solve_triangular(cholesky_lower, identity, lower=True)

def contract_first(left, right):
    return lax.dot_general(left.astype(jnp.float32), right.astype(jnp.float32), (((0,), (0,)), ((), ())), precision=HIGHEST, preferred_element_type=jnp.float32)

def reference(gradient, feedback, warm_start, master, moment, second):
    replicas = gradient.shape[0]

    def factor_step(running, slices):
        merged = slices[0].astype(jnp.float32) + slices[1].astype(jnp.float32)
        return (running + contract_first(merged, warm_start), None)
    zero_factor = jnp.zeros((gradient.shape[2], warm_start.shape[1]), jnp.float32)
    factor, _ = lax.scan(factor_step, zero_factor, (gradient, feedback))
    factor = factor / replicas
    gram = contract_first(factor, factor)
    inverse = lower_inverse(gram)
    unit_basis = jnp.dot(factor.astype(jnp.float32), inverse.T.astype(jnp.float32), precision=HIGHEST, preferred_element_type=jnp.float32)

    def project_step(running, slices):
        merged = slices[0].astype(jnp.float32) + slices[1].astype(jnp.float32)
        return (running + jnp.dot(merged.astype(jnp.float32), unit_basis.astype(jnp.float32), precision=HIGHEST, preferred_element_type=jnp.float32), None)
    zero_right = jnp.zeros(warm_start.shape, jnp.float32)
    right_factor, _ = lax.scan(project_step, zero_right, (gradient, feedback))
    right_factor = right_factor / replicas
    approx = lax.dot_general(right_factor.astype(jnp.float32), unit_basis.astype(jnp.float32), (((1,), (1,)), ((), ())), precision=HIGHEST, preferred_element_type=jnp.float32)

    def residue(slices):
        merged = slices[0].astype(jnp.float32) + slices[1].astype(jnp.float32)
        return (merged - approx).astype(jnp.bfloat16)
    new_feedback = lax.map(residue, (gradient, feedback))
    moment_out = beta_one * moment + (1.0 - beta_one) * approx
    second_out = beta_two * second + (1.0 - beta_two) * approx * approx
    master_out = master - learn_rate * (moment_out / (jnp.sqrt(second_out) + adam_eps) + decay_rate * master)
    return (new_feedback, master_out.astype(jnp.bfloat16), master_out, moment_out, second_out, right_factor)
```

```python
import jax
import jax.numpy as jnp
from jax import lax
from jax.sharding import PartitionSpec as P

HIGHEST = lax.Precision.HIGHEST
beta_one = 0.9
beta_two = 0.95
learn_rate = 0.02
decay_rate = 0.1
adam_eps = 1e-08
ridge_rate = 1e-06


def lower_inverse(gram):
    matrix_order = gram.shape[0]
    identity = jnp.eye(matrix_order, dtype=jnp.float32)
    ridge_term = ridge_rate * jnp.trace(gram) / matrix_order
    cholesky_lower = jnp.linalg.cholesky(gram + ridge_term * identity)
    return jax.scipy.linalg.solve_triangular(cholesky_lower, identity, lower=True)


def contract(left, right, left_dim, right_dim):
    return lax.dot_general(
        left,
        right,
        (((left_dim,), (right_dim,)), ((), ())),
        precision=HIGHEST,
        preferred_element_type=jnp.float32,
    )


def exchange(value, axis, distance):
    return lax.ppermute(value, axis, [(i, i ^ distance) for i in range(lax.axis_size(axis))])


def sum_by_doubling(value, axis):
    distance = 1
    while distance < lax.axis_size(axis):
        value = value + exchange(value, axis, distance)
        distance *= 2
    return value


def start_sum(value, axis):
    return [value] + [exchange(value, axis, d) for d in range(1, lax.axis_size(axis))]


def finish_sum(terms):
    while len(terms) > 1:
        terms = [a + b for a, b in zip(terms[::2], terms[1::2])]
    return terms[0]


def on_device(gradient, feedback, warm_start, master, moment, second):
    replicas = lax.axis_size("rep")
    merged = gradient[0].astype(jnp.float32) + feedback[0].astype(jnp.float32)
    rows, columns = merged.shape
    rank = warm_start.shape[1]
    own_rows = master.shape[0]
    half = own_rows // 2

    factor_t = sum_by_doubling(contract(warm_start, merged, 0, 0), "rep") / replicas
    gram_terms = start_sum(contract(factor_t, factor_t, 1, 1), "shard")

    projected = contract(merged, factor_t, 1, 1)
    packed = projected.reshape(replicas, 2, half, rank).transpose(0, 2, 1, 3)
    packed = packed.reshape(replicas, half, 2 * rank)
    received = lax.all_to_all(packed, "rep", 0, 0, tiled=True)
    own_terms = start_sum(received.sum(0), "shard")

    inverse = lower_inverse(finish_sum(gram_terms))
    unit_t = contract(inverse, factor_t, 1, 0)

    own_packed = finish_sum(own_terms)
    own_projected = jnp.concatenate([own_packed[:, :rank], own_packed[:, rank:]], 0)
    own_right = contract(own_projected, inverse, 1, 1) / replicas
    grad_rows = contract(own_right, unit_t, 1, 0)

    moment_out = beta_one * moment + (1.0 - beta_one) * grad_rows
    second_out = beta_two * second + (1.0 - beta_two) * grad_rows * grad_rows
    master_out = master - learn_rate * (
        moment_out / (jnp.sqrt(second_out) + adam_eps) + decay_rate * master
    )

    high = lax.reduce_precision(own_right, 8, 7)
    low = (own_right - high).astype(jnp.bfloat16)
    extra = own_rows * rank // columns
    block = jnp.concatenate(
        [
            master_out.astype(jnp.bfloat16),
            high.astype(jnp.bfloat16).reshape(extra, columns),
            low.reshape(extra, columns),
        ],
        0,
    )
    blocks = lax.all_to_all(
        jnp.broadcast_to(block[None], (replicas,) + block.shape), "rep", 0, 0, tiled=True
    )
    weights = blocks[:, :own_rows].reshape(rows, columns)
    high_all = blocks[:, own_rows : own_rows + extra].reshape(rows, rank).astype(jnp.float32)
    low_all = blocks[:, own_rows + extra :].reshape(rows, rank).astype(jnp.float32)
    right_factor = high_all + low_all
    approx = contract(right_factor, unit_t, 1, 0)
    new_feedback = (merged - approx).astype(jnp.bfloat16)[None]
    return (new_feedback, weights, master_out, moment_out, second_out, right_factor)


def solution(mesh):
    return jax.shard_map(
        on_device,
        mesh=mesh,
        in_specs=(
            P("rep", None, "shard"),
            P("rep", None, "shard"),
            P(),
            P("rep", "shard"),
            P("rep", "shard"),
            P("rep", "shard"),
        ),
        out_specs=(
            P("rep", None, "shard"),
            P(None, "shard"),
            P("rep", "shard"),
            P("rep", "shard"),
            P("rep", "shard"),
            P(),
        ),
        check_vma=False,
    )
```

```python
import jax
import jax.numpy as jnp
from jax import lax
from jax.experimental import pallas as pl
from jax.experimental.pallas import tpu as pltpu
from jax.sharding import PartitionSpec as P

HIGHEST = lax.Precision.HIGHEST
beta_one = 0.9
beta_two = 0.95
learn_rate = 0.02
decay_rate = 0.1
adam_eps = 1e-08
ridge_rate = 1e-06

F32 = jnp.float32
BF16 = jnp.bfloat16
Y_SIZE, Z_SIZE = 4, 8
Y_STEPS = (8, 16, 24)
X_STEPS = (2, 4, 6)


def exact(left, right, left_dim, right_dim):
    return lax.dot_general(
        left,
        right,
        (((left_dim,), (right_dim,)), ((), ())),
        precision=HIGHEST,
        preferred_element_type=F32,
    )


def native(left, right, left_dim, right_dim):
    return lax.dot_general(
        left, right, (((left_dim,), (right_dim,)), ((), ())), preferred_element_type=F32
    )


def three_parts(value):
    high = value.astype(BF16)
    rest = value - high.astype(F32)
    middle = rest.astype(BF16)
    return high, middle, (rest - middle.astype(F32)).astype(BF16)


def exchange(value, axis, distance):
    return lax.ppermute(value, axis, [(i, i ^ distance) for i in range(lax.axis_size(axis))])


def sum_four(terms):
    return (terms[0] + terms[1]) + (terms[2] + terms[3])


def shard_sum(value):
    value = value + exchange(value, "shard", 1)
    return sum_four([value] + [exchange(value, "shard", d) for d in X_STEPS])


def whole(shape):
    return pl.BlockSpec(shape, lambda *_: (0,) * len(shape))


def near(*values):
    return [pltpu.with_memory_space_constraint(v, pltpu.VMEM) for v in values]


def factor_kernel(rep_ref, warm_ref, grad_ref, feed_ref, *refs):
    outs, parts_ref = refs[:-1], refs[-1]
    rank = warm_ref.shape[0]
    step = pl.program_id(0)

    @pl.when(step == 0)
    def _():
        for i, part in enumerate(three_parts(warm_ref[...])):
            parts_ref[i * rank : (i + 1) * rank, :] = part

    total = native(parts_ref[...], grad_ref[...], 1, 0) + native(parts_ref[...], feed_ref[...], 1, 0)
    total = (total[2 * rank :] + total[rank : 2 * rank]) + total[:rank]
    for i, out in enumerate(outs):

        @pl.when(step == i)
        def _(out=out):
            out[...] = total


def local_factor(rep, warm_t, gradient, feedback):
    rank, rows = warm_t.shape
    quarter = gradient.shape[1] // Y_SIZE
    column_block = pl.BlockSpec((rows, quarter), lambda d, rep: (0, (rep[0] // Z_SIZE) ^ d))
    return pl.pallas_call(
        factor_kernel,
        out_shape=[pltpu.VMEM((rank, quarter), F32)] * Y_SIZE,
        grid_spec=pltpu.PrefetchScalarGridSpec(
            num_scalar_prefetch=1,
            grid=(Y_SIZE,),
            in_specs=[whole((rank, rows)), column_block, column_block],
            out_specs=[whole((rank, quarter))] * Y_SIZE,
            scratch_shapes=[pltpu.VMEM((3 * rank, rows), BF16)],
        ),
        cost_estimate=pl.CostEstimate(flops=2_000_000_000, bytes_accessed=2_500_000, transcendentals=0),
        name="local_factor",
    )(rep, warm_t, gradient, feedback)


def assemble_kernel(rep_ref, *refs):
    quarters, (factor_ref, parts_ref, gram_ref) = refs[:Y_SIZE], refs[Y_SIZE:]
    rank, quarter = quarters[0].shape
    own = rep_ref[0] // Z_SIZE
    for d, block in enumerate(quarters):
        at = pl.ds(pl.multiple_of((own ^ d) * quarter, quarter), quarter)
        factor_ref[:, at] = block[...]
    factor = factor_ref[...]
    for i, part in enumerate(three_parts(factor)):
        parts_ref[i * rank : (i + 1) * rank, :] = part
    gram_ref[...] = exact(factor, factor, 1, 1)


def assemble(rep, quarters):
    rank, quarter = quarters[0].shape
    columns = quarter * Y_SIZE
    shapes = [(rank, columns), (3 * rank, columns), (rank, rank)]
    types = [F32, BF16, F32]
    return pl.pallas_call(
        assemble_kernel,
        out_shape=[pltpu.VMEM(s, t) for s, t in zip(shapes, types)],
        grid_spec=pltpu.PrefetchScalarGridSpec(
            num_scalar_prefetch=1,
            grid=(1,),
            in_specs=[whole((rank, quarter))] * Y_SIZE,
            out_specs=[whole(s) for s in shapes],
        ),
        cost_estimate=pl.CostEstimate(flops=100_000_000, bytes_accessed=500_000, transcendentals=0),
        name="assemble_factor",
    )(rep, *near(*quarters))


def project_kernel(grad_ref, feed_ref, parts_ref, out_ref):
    groups, half, _ = out_ref.shape
    rank = parts_ref.shape[0] // 3
    parts = parts_ref[...]
    total = native(grad_ref[...], parts, 1, 1) + native(feed_ref[...], parts, 1, 1)
    value = (total[:, 2 * rank :] + total[:, rank : 2 * rank]) + total[:, :rank]
    value = value.reshape(groups, 2, half, rank)
    out_ref[...] = jnp.concatenate([value[:, 0], value[:, 1]], axis=-1)


def project(gradient, feedback, parts, replicas):
    rows, columns = gradient.shape
    rank = parts.shape[0] // 3
    half = rows // replicas // 2
    steps = 4
    row_block = pl.BlockSpec((rows // steps, columns), lambda i: (i, 0))
    return pl.pallas_call(
        project_kernel,
        out_shape=jax.ShapeDtypeStruct((replicas, half, 2 * rank), F32),
        grid=(steps,),
        in_specs=[row_block, row_block, whole(parts.shape)],
        out_specs=pl.BlockSpec((replicas // steps, half, 2 * rank), lambda i: (i, 0, 0)),
        cost_estimate=pl.CostEstimate(flops=2_000_000_000, bytes_accessed=2_500_000, transcendentals=0),
        name="project",
    )(gradient, feedback, *near(parts))


def inverse_kernel(gram_ref, factor_ref, inverse_ref, unit_ref):
    rank = gram_ref.shape[0]
    row = lax.broadcasted_iota(jnp.int32, (rank, rank), 0)
    column = lax.broadcasted_iota(jnp.int32, (rank, rank), 1)
    diagonal = row == column
    gram = gram_ref[...]
    trace = jnp.sum(jnp.where(diagonal, gram, 0.0))
    gram = gram + jnp.where(diagonal, ridge_rate * trace / rank, 0.0)
    table = jnp.concatenate([gram, jnp.where(diagonal, 1.0, 0.0)], axis=1)
    row_index = lax.broadcasted_iota(jnp.int32, (rank, 1), 0)
    pivots = jnp.zeros((rank, 1), F32)
    for k in range(rank):
        pivot_row = table[k : k + 1, :]
        pivot_column = table[:, k : k + 1]
        pivot = table[k : k + 1, k : k + 1]
        scale = jnp.where(row_index > k, pivot_column / pivot, 0.0)
        pivots = jnp.where(row_index == k, pivot, pivots)
        table = table - scale * pivot_row
    inverse = table[:, rank:] / jnp.sqrt(pivots)
    inverse_ref[...] = inverse
    unit_ref[...] = exact(inverse, factor_ref[...], 1, 0)


def invert(gram, factor_t):
    return pl.pallas_call(
        inverse_kernel,
        out_shape=[
            pltpu.VMEM(gram.shape, F32),
            pltpu.VMEM(factor_t.shape, F32),
        ],
        cost_estimate=pl.CostEstimate(flops=4_000_000_000, bytes_accessed=300_000, transcendentals=0),
        name="invert",
    )(*near(gram, factor_t))


def update_kernel(replicas, sum_ref, inverse_ref, unit_ref, master_ref, moment_ref, second_ref,
                  send_ref, master_out, moment_out, second_out):
    rank = inverse_ref.shape[0]
    columns = master_ref.shape[1]
    packed = sum_ref[...]
    own = jnp.concatenate([packed[:, :rank], packed[:, rank:]], axis=0)
    right = exact(own, inverse_ref[...], 1, 1) / replicas
    grad = exact(right, unit_ref[...], 1, 0)
    moment = beta_one * moment_ref[...] + (1.0 - beta_one) * grad
    second = beta_two * second_ref[...] + (1.0 - beta_two) * grad * grad
    master = master_ref[...]
    master = master - learn_rate * (
        moment / (jnp.sqrt(second) + adam_eps) + decay_rate * master
    )
    moment_out[...] = moment
    second_out[...] = second
    master_out[...] = master
    high = right.astype(BF16).astype(F32)
    send_ref[:, :columns] = master.astype(BF16)
    send_ref[:, columns:] = jnp.concatenate([high, right - high], axis=1).astype(BF16)


def update(replicas, own_sum, inverse, unit_t, master, moment, second):
    rows, columns = master.shape
    rank = inverse.shape[0]
    block = jax.ShapeDtypeStruct(master.shape, F32)
    return pl.pallas_call(
        lambda *refs: update_kernel(replicas, *refs),
        out_shape=[pltpu.VMEM((rows, columns + 2 * rank), BF16), block, block, block],
        cost_estimate=pl.CostEstimate(flops=50_000_000, bytes_accessed=600_000, transcendentals=0),
        name="update",
    )(*near(own_sum, inverse, unit_t, master, moment, second))


def finish_kernel(rep_ref, *refs):
    blocks, (unit_ref, grad_ref, feed_ref) = refs[:Y_SIZE], refs[Y_SIZE : Y_SIZE + 3]
    new_ref, weights_ref, right_ref, parts_ref, right_rows = refs[Y_SIZE + 3 :]
    rank, columns = unit_ref.shape
    own_rows = blocks[0].shape[1]
    rep = rep_ref[0]
    own_y, own_z = rep // Z_SIZE, rep % Z_SIZE
    step = pl.program_id(0)

    @pl.when(step == 0)
    def _():
        for i, part in enumerate(three_parts(unit_ref[...])):
            parts_ref[i, :rank, :] = part
            parts_ref[i, rank:, :] = part

    for d, block in enumerate(blocks):

        @pl.when(step == d)
        def _(d=d, block=block):
            first = (own_y ^ d) * (Z_SIZE * own_rows)
            for j in range(Z_SIZE):
                at = pl.multiple_of((own_z ^ j) * own_rows, own_rows)
                rows = pl.ds(at, own_rows)
                right = block[j, :, columns:]
                approx = native(right, parts_ref[2], 1, 0) + native(right, parts_ref[1], 1, 0)
                approx = approx + native(right, parts_ref[0], 1, 0)
                merged = grad_ref[rows, :].astype(F32) + feed_ref[rows, :].astype(F32)
                new_ref[rows, :] = (merged - approx).astype(BF16)
                weights_ref[rows, :] = block[j, :, :columns]
                wide = right.astype(F32)
                all_rows = pl.ds(pl.multiple_of(first + at, own_rows), own_rows)
                right_rows[all_rows, :] = wide[:, :rank] + wide[:, rank:]

    @pl.when(step == Y_SIZE - 1)
    def _():
        right_ref[...] = right_rows[...].T


def finish(rep, blocks, unit_t, gradient, feedback):
    rows, columns = gradient.shape
    rank = unit_t.shape[0]
    quarter = rows // Y_SIZE
    row_block = pl.BlockSpec((quarter, columns), lambda d, rep: ((rep[0] // Z_SIZE) ^ d, 0))
    return pl.pallas_call(
        finish_kernel,
        out_shape=[
            jax.ShapeDtypeStruct((rows, columns), BF16),
            jax.ShapeDtypeStruct((rows, columns), BF16),
            jax.ShapeDtypeStruct((rank, rows), F32),
        ],
        grid_spec=pltpu.PrefetchScalarGridSpec(
            num_scalar_prefetch=1,
            grid=(Y_SIZE,),
            in_specs=[whole(b.shape) for b in blocks] + [whole(unit_t.shape), row_block, row_block],
            out_specs=[row_block, row_block, whole((rank, rows))],
            scratch_shapes=[
                pltpu.VMEM((3, 2 * rank, columns), BF16),
                pltpu.VMEM((rows, rank), F32),
            ],
        ),
        cost_estimate=pl.CostEstimate(flops=1_000_000_000, bytes_accessed=6_000_000, transcendentals=0),
        name="finish",
    )(rep, *near(*blocks, unit_t), gradient, feedback)


def on_device(gradient, feedback, warm_start, master, moment, second):
    replicas = lax.axis_size("rep")
    gradient, feedback = gradient[0], feedback[0]
    rep = lax.axis_index("rep").astype(jnp.int32).reshape(1)

    pieces = local_factor(rep, warm_start.T, gradient, feedback)
    quarter = sum_four([pieces[0]] + [exchange(p, "rep", d) for p, d in zip(pieces[1:], Y_STEPS)])
    for distance in (1, 2, 4):
        quarter = quarter + exchange(quarter, "rep", distance)
    quarter = quarter / replicas
    quarters = [quarter] + [exchange(quarter, "rep", d) for d in Y_STEPS]
    factor_t, parts, gram_term = assemble(rep, quarters)

    packed = project(gradient, feedback, parts, replicas)
    received = lax.all_to_all(packed, "rep", 0, 0, tiled=True)
    inverse, unit_t = invert(shard_sum(gram_term), factor_t)
    received, inverse, unit_t = lax.optimization_barrier((received, inverse, unit_t))
    own_sum = shard_sum(received.sum(0))

    send, master_out, moment_out, second_out = update(
        replicas, own_sum, inverse, unit_t, master, moment, second
    )
    pair = jnp.stack([send, exchange(send, "rep", 1)])
    column = jnp.concatenate([pair] + [exchange(pair, "rep", d) for d in (2, 4, 6)])
    blocks = [column] + [exchange(column, "rep", d) for d in Y_STEPS]
    new_feedback, weights, right_t = finish(rep, blocks, unit_t, gradient, feedback)
    return (new_feedback[None], weights, master_out, moment_out, second_out, right_t.T)


def solution(mesh):
    return jax.shard_map(
        on_device,
        mesh=mesh,
        in_specs=(
            P("rep", None, "shard"),
            P("rep", None, "shard"),
            P(),
            P("rep", "shard"),
            P("rep", "shard"),
            P("rep", "shard"),
        ),
        out_specs=(
            P("rep", None, "shard"),
            P(None, "shard"),
            P("rep", "shard"),
            P("rep", "shard"),
            P("rep", "shard"),
            P(),
        ),
        check_vma=False,
    )
```

```python
import jax
import jax.numpy as jnp
from jax import lax
from jax.experimental import pallas as pl
from jax.experimental.pallas import tpu as pltpu
from jax.sharding import PartitionSpec as P

HIGHEST = lax.Precision.HIGHEST
beta_one = 0.9
beta_two = 0.95
learn_rate = 0.02
decay_rate = 0.1
adam_eps = 1e-08
ridge_rate = 1e-06

F32 = jnp.float32
BF16 = jnp.bfloat16
Y_SIZE, Z_SIZE = 4, 8
Y_STEPS = (8, 16, 24)
X_STEPS = (2, 4, 6)


def exact(left, right, left_dim, right_dim):
    return lax.dot_general(
        left,
        right,
        (((left_dim,), (right_dim,)), ((), ())),
        precision=HIGHEST,
        preferred_element_type=F32,
    )


def native(left, right, left_dim, right_dim):
    return lax.dot_general(
        left, right, (((left_dim,), (right_dim,)), ((), ())), preferred_element_type=F32
    )


def three_parts(value):
    high = value.astype(BF16)
    rest = value - high.astype(F32)
    middle = rest.astype(BF16)
    return high, middle, (rest - middle.astype(F32)).astype(BF16)


def exchange(value, axis, distance):
    return lax.ppermute(value, axis, [(i, i ^ distance) for i in range(lax.axis_size(axis))])


def sum_four(terms):
    return (terms[0] + terms[1]) + (terms[2] + terms[3])


def shard_sum(value):
    value = value + exchange(value, "shard", 1)
    return sum_four([value] + [exchange(value, "shard", d) for d in X_STEPS])


def whole(shape):
    return pl.BlockSpec(shape, lambda *_: (0,) * len(shape))


def call(kernel, outs, args, cost, name, aliases=None, grid=None, out_specs=None, spare=(),
         scratch=()):
    specs = [pl.BlockSpec(memory_space=pltpu.VMEM)] * (len(args) - 1)
    specs += [pl.BlockSpec(memory_space=pl.ANY)] * len(spare)
    flops, traffic = cost
    return pl.pallas_call(
        kernel,
        out_shape=outs,
        grid_spec=pltpu.PrefetchScalarGridSpec(
            num_scalar_prefetch=1,
            grid=grid or (1,),
            in_specs=specs,
            out_specs=out_specs or [pl.BlockSpec(memory_space=pltpu.VMEM)] * len(outs),
            scratch_shapes=scratch,
        ),
        input_output_aliases=aliases or {},
        compiler_params=pltpu.CompilerParams(vmem_limit_bytes=16 * 2**20),
        cost_estimate=pl.CostEstimate(flops=flops, bytes_accessed=traffic, transcendentals=0),
        name=name,
    )(
        args[0],
        *[pltpu.with_memory_space_constraint(v, pltpu.VMEM) for v in args[1:]],
        *spare,
    )


def factor_kernel(rep_ref, warm_ref, grad_ref, feed_ref, *refs):
    outs, parts_ref, total_ref = refs[:-2], refs[-2], refs[-1]
    rank = warm_ref.shape[0]
    width = grad_ref.shape[1]
    quarter = outs[0].shape[1]
    step = pl.program_id(0)

    @pl.when(step == 0)
    def _():
        for i, part in enumerate(three_parts(warm_ref[...])):
            parts_ref[i * rank : (i + 1) * rank, :] = part

    total = native(parts_ref[...], grad_ref[...], 1, 0) + native(parts_ref[...], feed_ref[...], 1, 0)
    total = (total[2 * rank :] + total[rank : 2 * rank]) + total[:rank]
    total_ref[:, pl.ds(pl.multiple_of(step * width, width), width)] = total

    @pl.when(step == pl.num_programs(0) - 1)
    def _():
        own = rep_ref[0] // Z_SIZE
        for d, out in enumerate(outs):
            out[...] = total_ref[:, pl.ds(pl.multiple_of((own ^ d) * quarter, quarter), quarter)]


def local_factor(rep, warm_t, gradient, feedback):
    rank, rows = warm_t.shape
    columns = gradient.shape[1]
    quarter = columns // Y_SIZE
    steps = 2
    column_block = pl.BlockSpec((rows, columns // steps), lambda i, rep: (0, i))
    return pl.pallas_call(
        factor_kernel,
        out_shape=[pltpu.VMEM((rank, quarter), F32)] * Y_SIZE,
        grid_spec=pltpu.PrefetchScalarGridSpec(
            num_scalar_prefetch=1,
            grid=(steps,),
            in_specs=[whole((rank, rows)), column_block, column_block],
            out_specs=[whole((rank, quarter))] * Y_SIZE,
            scratch_shapes=[pltpu.VMEM((3 * rank, rows), BF16), pltpu.VMEM((rank, columns), F32)],
        ),
        compiler_params=pltpu.CompilerParams(vmem_limit_bytes=16 * 2**20),
        cost_estimate=pl.CostEstimate(flops=10**9, bytes_accessed=2_500_000, transcendentals=0),
        name="local_factor",
    )(rep, warm_t, gradient, feedback)


def assemble_kernel(rep_ref, *refs):
    quarters, (factor_ref, parts_ref, gram_ref) = refs[:Y_SIZE], refs[Y_SIZE:]
    rank, quarter = quarters[0].shape
    own = rep_ref[0] // Z_SIZE
    for d, block in enumerate(quarters):
        at = pl.ds(pl.multiple_of((own ^ d) * quarter, quarter), quarter)
        factor_ref[:, at] = block[...]
    factor = factor_ref[...]
    for i, part in enumerate(three_parts(factor)):
        parts_ref[i * rank : (i + 1) * rank, :] = part
    gram_ref[...] = exact(factor, factor, 1, 1)


def assemble(rep, quarters):
    rank, quarter = quarters[0].shape
    columns = quarter * Y_SIZE
    outs = [
        pltpu.VMEM((rank, columns), F32),
        pltpu.VMEM((3 * rank, columns), BF16),
        pltpu.VMEM((rank, rank), F32),
    ]
    return call(assemble_kernel, outs, (rep, *quarters), (10**8, 500_000), "assemble_factor")


def project_kernel(rep_ref, grad_ref, feed_ref, parts_ref, out_ref):
    replicas, half, _ = out_ref.shape
    rows = grad_ref.shape[0]
    rank = parts_ref.shape[0] // 3
    parts = parts_ref[...]
    groups = 8
    size = rows // replicas * groups

    for i in range(replicas // groups):
        at = slice(i * size, (i + 1) * size)
        total = native(grad_ref[at, :], parts, 1, 1) + native(feed_ref[at, :], parts, 1, 1)
        value = (total[:, 2 * rank :] + total[:, rank : 2 * rank]) + total[:, :rank]
        value = value.reshape(groups, 2, half, rank)
        out_ref[i * groups : (i + 1) * groups] = jnp.concatenate([value[:, 0], value[:, 1]], axis=-1)


def project(rep, gradient, feedback, parts, replicas):
    rank = parts.shape[0] // 3
    half = gradient.shape[0] // replicas // 2
    outs = [pltpu.VMEM((replicas, half, 2 * rank), F32)]
    return call(
        project_kernel, outs, (rep, gradient, feedback, parts), (10**9, 2_500_000), "project"
    )[0]


def inverse_kernel(rep_ref, gram_ref, factor_ref, inverse_ref, unit_ref, parts_ref):
    rank = gram_ref.shape[0]
    width = 8
    row = lax.broadcasted_iota(jnp.int32, (rank, rank), 0)
    column = lax.broadcasted_iota(jnp.int32, (rank, rank), 1)
    diagonal = row == column
    gram = gram_ref[...]
    trace = jnp.sum(jnp.where(diagonal, gram, 0.0))
    gram = gram + jnp.where(diagonal, ridge_rate * trace / rank, 0.0)
    table = jnp.concatenate([gram, jnp.where(diagonal, 1.0, 0.0)], axis=1)
    row = lax.broadcasted_iota(jnp.int32, table.shape, 0)
    pivots = jnp.ones(table.shape, F32)
    for k in range(0, rank, width):
        ahead = [jnp.broadcast_to(table[:, c : c + 1], table.shape) for c in range(k, k + width)]
        lines = [table[c : c + 1, :] for c in range(k, k + width)]
        for i in range(width):
            at = k + i
            pivot = ahead[i][at : at + 1, :]
            pivots = jnp.where(row == at, pivot, pivots)
            scale = jnp.where(row > at, ahead[i] * (1.0 / pivot), 0.0)
            for j in range(i + 1, width):
                entry = ahead[j][at : at + 1, :]
                ahead[j] = ahead[j] - scale * entry
                lines[j] = lines[j] - scale[k + j : k + j + 1, :] * lines[i]
            table = table - scale * lines[i]
    inverse = table[:, rank:] / jnp.sqrt(pivots[:, rank:])
    inverse_ref[...] = inverse
    unit = exact(inverse, factor_ref[...], 1, 0)
    unit_ref[...] = unit
    for i, part in enumerate(three_parts(unit)):
        parts_ref[2 * i * rank : (2 * i + 1) * rank, :] = part
        parts_ref[(2 * i + 1) * rank : (2 * i + 2) * rank, :] = part


def invert(rep, gram, factor_t):
    rank, columns = factor_t.shape
    outs = [
        pltpu.VMEM((rank, rank), F32),
        pltpu.VMEM((rank, columns), F32),
        pltpu.VMEM((6 * rank, columns), BF16),
    ]
    return call(inverse_kernel, outs, (rep, gram, factor_t), (2 * 10**9, 500_000), "invert")


def update_kernel(replicas, rep_ref, sum_ref, inverse_ref, unit_ref, master_ref, moment_ref,
                  second_ref, send_ref, master_out, moment_out, second_out):
    rank = inverse_ref.shape[0]
    columns = master_ref.shape[1]
    packed = sum_ref[...]
    own = jnp.concatenate([packed[:, :rank], packed[:, rank:]], axis=0)
    right = exact(own, inverse_ref[...], 1, 1) / replicas
    grad = exact(right, unit_ref[...], 1, 0)
    moment = beta_one * moment_ref[...] + (1.0 - beta_one) * grad
    second = beta_two * second_ref[...] + (1.0 - beta_two) * grad * grad
    master = master_ref[...]
    master = master - learn_rate * (
        moment / (jnp.sqrt(second) + adam_eps) + decay_rate * master
    )
    moment_out[...] = moment
    second_out[...] = second
    master_out[...] = master
    high = right.astype(BF16).astype(F32)
    send_ref[:, :columns] = master.astype(BF16)
    send_ref[:, columns:] = jnp.concatenate([high, right - high], axis=1).astype(BF16)


def update(replicas, rep, own_sum, inverse, unit_t, master, moment, second):
    rows, columns = master.shape
    rank = inverse.shape[0]
    block = pltpu.VMEM(master.shape, F32)
    outs = [pltpu.VMEM((rows, columns + 2 * rank), BF16), block, block, block]
    args = (rep, own_sum, inverse, unit_t, master, moment, second)
    kernel = lambda *refs: update_kernel(replicas, *refs)
    return call(kernel, outs, args, (5 * 10**7, 600_000), "update")


def finish_rows(own_y, own_z, d, block, parts_ref, grad_ref, feed_ref, new_ref, weights_ref):
    columns = grad_ref.shape[1]
    groups, own_rows, width = block.shape
    right = block[:, :, columns:].reshape(groups * own_rows, width - columns)
    approx = native(jnp.concatenate([right] * 3, axis=1), parts_ref[...], 1, 0)
    first = (own_y ^ d) * (groups * own_rows)
    for j in range(groups):
        at = pl.multiple_of((own_z ^ j) * own_rows, own_rows)
        source = pl.ds(pl.multiple_of(first + at, own_rows), own_rows)
        merged = grad_ref[source, :].astype(F32) + feed_ref[source, :].astype(F32)
        rows = pl.ds(at, own_rows)
        piece = approx[j * own_rows : (j + 1) * own_rows]
        new_ref[rows, :] = (merged - piece).astype(BF16)
        weights_ref[rows, :] = block[j, :, :columns]


def finish_own_kernel(rep_ref, block, parts_ref, grad_ref, feed_ref, new_ref, weights_ref):
    own_y, own_z = rep_ref[0] // Z_SIZE, rep_ref[0] % Z_SIZE
    finish_rows(own_y, own_z, 0, block, parts_ref, grad_ref, feed_ref, new_ref, weights_ref)


def finish_rest_kernel(rep_ref, *refs):
    blocks, (parts_ref, grad_ref, feed_ref) = refs[:Y_SIZE], refs[Y_SIZE : Y_SIZE + 3]
    new_ref, weights_ref, right_ref, right_rows = refs[Y_SIZE + 5 :]
    columns = grad_ref.shape[1]
    groups, own_rows, width = blocks[0].shape
    rank = (width - columns) // 2
    own_y, own_z = rep_ref[0] // Z_SIZE, rep_ref[0] % Z_SIZE
    step = pl.program_id(0)
    for d in range(1, Y_SIZE):

        @pl.when(step == d - 1)
        def _(d=d):
            finish_rows(
                own_y, own_z, d, blocks[d], parts_ref, grad_ref, feed_ref, new_ref, weights_ref
            )

    @pl.when(step == 0)
    def _():
        for d, block in enumerate(blocks):
            for j in range(groups):
                at = (own_y ^ d) * (groups * own_rows) + (own_z ^ j) * own_rows
                wide = block[j, :, columns:].astype(F32)
                rows = pl.ds(pl.multiple_of(at, own_rows), own_rows)
                right_rows[rows, :] = wide[:, :rank] + wide[:, rank:]
        right_ref[...] = right_rows[...].T


def finish_own(rep, block, parts, gradient, feedback):
    rows, columns = gradient.shape
    row_block = pl.BlockSpec((rows // Y_SIZE, columns), lambda i, rep: (rep[0] // Z_SIZE, 0))
    return call(
        finish_own_kernel,
        [jax.ShapeDtypeStruct((rows, columns), BF16)] * 2,
        (rep, block, parts, gradient, feedback),
        (10**9, 1_500_000),
        "finish_own",
        out_specs=[row_block, row_block],
    )


def finish_rest(rep, blocks, parts, gradient, feedback, begun):
    rows, columns = gradient.shape
    rank = (blocks[0].shape[2] - columns) // 2
    row_block = pl.BlockSpec(
        (rows // Y_SIZE, columns), lambda i, rep: ((rep[0] // Z_SIZE) ^ (i + 1), 0)
    )
    return call(
        finish_rest_kernel,
        [jax.ShapeDtypeStruct((rows, columns), BF16)] * 2
        + [jax.ShapeDtypeStruct((rank, rows), F32)],
        (rep, *blocks, parts, gradient, feedback),
        (10**9, 4_500_000),
        "finish_rest",
        aliases={Y_SIZE + 4: 0, Y_SIZE + 5: 1},
        grid=(Y_SIZE - 1,),
        out_specs=[row_block, row_block, whole((rank, rows))],
        spare=begun,
        scratch=[pltpu.VMEM((rows, rank), F32)],
    )


def on_device(gradient, feedback, warm_start, master, moment, second):
    replicas = lax.axis_size("rep")
    gradient, feedback = gradient[0], feedback[0]
    rep = lax.axis_index("rep").astype(jnp.int32).reshape(1)

    pieces = local_factor(rep, warm_start.T, gradient, feedback)
    quarter = sum_four([pieces[0]] + [exchange(p, "rep", d) for p, d in zip(pieces[1:], Y_STEPS)])
    for distance in (1, 2, 4):
        quarter = quarter + exchange(quarter, "rep", distance)
    quarter = quarter / replicas
    quarters = [quarter] + [exchange(quarter, "rep", d) for d in Y_STEPS]
    factor_t, parts, gram_term = assemble(rep, quarters)

    gram_pair = gram_term + exchange(gram_term, "shard", 1)
    packed = project(rep, gradient, feedback, parts, replicas)
    gram_pair, packed = lax.optimization_barrier((gram_pair, packed))
    received = lax.all_to_all(packed, "rep", 0, 0, tiled=True)
    gram = sum_four([gram_pair] + [exchange(gram_pair, "shard", d) for d in X_STEPS])
    inverse, unit_t, unit_parts = invert(rep, gram, factor_t)
    received, inverse, unit_t, unit_parts = lax.optimization_barrier(
        (received, inverse, unit_t, unit_parts)
    )
    own_sum = shard_sum(received.sum(0))

    send, master_out, moment_out, second_out = update(
        replicas, rep, own_sum, inverse, unit_t, master, moment, second
    )
    pair = jnp.stack([send, exchange(send, "rep", 1)])
    column = jnp.concatenate([pair] + [exchange(pair, "rep", d) for d in (2, 4, 6)])
    others = [exchange(column, "rep", d) for d in Y_STEPS]
    begun = finish_own(rep, column, unit_parts, gradient, feedback)
    new_feedback, weights, right_t = finish_rest(
        rep, [column] + others, unit_parts, gradient, feedback, begun
    )
    return (new_feedback[None], weights, master_out, moment_out, second_out, right_t.T)


def solution(mesh):
    return jax.shard_map(
        on_device,
        mesh=mesh,
        in_specs=(
            P("rep", None, "shard"),
            P("rep", None, "shard"),
            P(),
            P("rep", "shard"),
            P("rep", "shard"),
            P("rep", "shard"),
        ),
        out_specs=(
            P("rep", None, "shard"),
            P(None, "shard"),
            P("rep", "shard"),
            P("rep", "shard"),
            P("rep", "shard"),
            P(),
        ),
        check_vma=False,
    )
```

```python
import jax
import jax.numpy as jnp
from jax import lax
from jax.experimental import pallas as pl
from jax.experimental.pallas import tpu as pltpu
from jax.sharding import PartitionSpec as P

HIGHEST = lax.Precision.HIGHEST
beta_one = 0.9
beta_two = 0.95
learn_rate = 0.02
decay_rate = 0.1
adam_eps = 1e-08
ridge_rate = 1e-06

F32 = jnp.float32
BF16 = jnp.bfloat16
Y_SIZE, Z_SIZE = 4, 8
Y_STEPS = (8, 16, 24)
X_STEPS = (2, 4, 6)
ROW_BLOCKS = 4


def exact(left, right, left_dim, right_dim):
    return lax.dot_general(
        left,
        right,
        (((left_dim,), (right_dim,)), ((), ())),
        precision=HIGHEST,
        preferred_element_type=F32,
    )


def native(left, right, left_dim, right_dim):
    return lax.dot_general(
        left, right, (((left_dim,), (right_dim,)), ((), ())), preferred_element_type=F32
    )


def three_parts(value):
    high = value.astype(BF16)
    rest = value - high.astype(F32)
    middle = rest.astype(BF16)
    return high, middle, (rest - middle.astype(F32)).astype(BF16)


def exchange(value, axis, distance):
    return lax.ppermute(value, axis, [(i, i ^ distance) for i in range(lax.axis_size(axis))])


def sum_four(terms):
    return (terms[0] + terms[1]) + (terms[2] + terms[3])


def shard_sum(value):
    value = value + exchange(value, "shard", 1)
    return sum_four([value] + [exchange(value, "shard", d) for d in X_STEPS])


def whole(shape):
    return pl.BlockSpec(shape, lambda *_: (0,) * len(shape))


def call(kernel, outs, args, cost, name, aliases=None, grid=None, out_specs=None, spare=(),
         scratch=()):
    specs = [pl.BlockSpec(memory_space=pltpu.VMEM)] * (len(args) - 1)
    specs += [pl.BlockSpec(memory_space=pl.ANY)] * len(spare)
    flops, traffic = cost
    return pl.pallas_call(
        kernel,
        out_shape=outs,
        grid_spec=pltpu.PrefetchScalarGridSpec(
            num_scalar_prefetch=1,
            grid=grid or (1,),
            in_specs=specs,
            out_specs=out_specs or [pl.BlockSpec(memory_space=pltpu.VMEM)] * len(outs),
            scratch_shapes=scratch,
        ),
        input_output_aliases=aliases or {},
        compiler_params=pltpu.CompilerParams(vmem_limit_bytes=16 * 2**20),
        cost_estimate=pl.CostEstimate(flops=flops, bytes_accessed=traffic, transcendentals=0),
        name=name,
    )(
        args[0],
        *[pltpu.with_memory_space_constraint(v, pltpu.VMEM) for v in args[1:]],
        *spare,
    )


def factor_kernel(rep_ref, warm_far, grad_far, feed_far, *refs):
    outs, (grad_ref, feed_ref, warm_ref, parts_ref, total_ref, sems) = refs[:Y_SIZE], refs[Y_SIZE:]
    rank, rows = warm_ref.shape
    quarter = outs[0].shape[1]
    size = rows // ROW_BLOCKS
    warm_copy = pltpu.make_async_copy(warm_far, warm_ref, sems.at[2 * ROW_BLOCKS])
    warm_copy.start()
    copies = []
    for i in range(ROW_BLOCKS):
        at = pl.ds(i * size, size)
        for k, (far, ref) in enumerate([(grad_far, grad_ref), (feed_far, feed_ref)]):
            copies.append(pltpu.make_async_copy(far.at[at], ref.at[at], sems.at[2 * i + k]))
            copies[-1].start()
    warm_copy.wait()
    for i, part in enumerate(three_parts(warm_ref[...])):
        parts_ref[i * rank : (i + 1) * rank, :] = part
    total = None
    for i in range(ROW_BLOCKS):
        at = slice(i * size, (i + 1) * size)
        copies[2 * i].wait()
        copies[2 * i + 1].wait()
        parts = parts_ref[:, at]
        term = native(parts, grad_ref[at, :], 1, 0) + native(parts, feed_ref[at, :], 1, 0)
        total = term if total is None else total + term
    total_ref[...] = (total[2 * rank :] + total[rank : 2 * rank]) + total[:rank]
    own = rep_ref[0] // Z_SIZE
    for d, out in enumerate(outs):
        out[...] = total_ref[:, pl.ds(pl.multiple_of((own ^ d) * quarter, quarter), quarter)]


def local_factor(rep, warm_t, gradient, feedback):
    rank, rows = warm_t.shape
    columns = gradient.shape[1]
    near = pltpu.VMEM((rows, columns), BF16)
    args = [pltpu.with_memory_space_constraint(v, pltpu.HBM) for v in (warm_t, gradient, feedback)]
    outs = pl.pallas_call(
        factor_kernel,
        out_shape=[pltpu.VMEM((rank, columns // Y_SIZE), F32)] * Y_SIZE + [near] * 2,
        grid_spec=pltpu.PrefetchScalarGridSpec(
            num_scalar_prefetch=1,
            grid=(1,),
            in_specs=[pl.BlockSpec(memory_space=pl.ANY)] * 3,
            out_specs=[pl.BlockSpec(memory_space=pltpu.VMEM)] * (Y_SIZE + 2),
            scratch_shapes=[
                pltpu.VMEM((rank, rows), F32),
                pltpu.VMEM((3 * rank, rows), BF16),
                pltpu.VMEM((rank, columns), F32),
                pltpu.SemaphoreType.DMA((2 * ROW_BLOCKS + 1,)),
            ],
        ),
        compiler_params=pltpu.CompilerParams(vmem_limit_bytes=16 * 2**20),
        cost_estimate=pl.CostEstimate(flops=10**9, bytes_accessed=2_500_000, transcendentals=0),
        name="local_factor",
    )(rep, *args)
    return outs[:Y_SIZE], outs[Y_SIZE], outs[Y_SIZE + 1]


def assemble_kernel(rep_ref, *refs):
    quarters, (factor_ref, parts_ref, gram_ref) = refs[:Y_SIZE], refs[Y_SIZE:]
    rank, quarter = quarters[0].shape
    own = rep_ref[0] // Z_SIZE
    for d, block in enumerate(quarters):
        at = pl.ds(pl.multiple_of((own ^ d) * quarter, quarter), quarter)
        factor_ref[:, at] = block[...]
    factor = factor_ref[...]
    for i, part in enumerate(three_parts(factor)):
        parts_ref[i * rank : (i + 1) * rank, :] = part
    gram_ref[...] = exact(factor, factor, 1, 1)


def assemble(rep, quarters):
    rank, quarter = quarters[0].shape
    columns = quarter * Y_SIZE
    outs = [
        pltpu.VMEM((rank, columns), F32),
        pltpu.VMEM((3 * rank, columns), BF16),
        pltpu.VMEM((rank, rank), F32),
    ]
    return call(assemble_kernel, outs, (rep, *quarters), (10**8, 500_000), "assemble_factor")


def project_kernel(rep_ref, grad_ref, feed_ref, parts_ref, out_ref):
    replicas, half, _ = out_ref.shape
    rows = grad_ref.shape[0]
    rank = parts_ref.shape[0] // 3
    parts = parts_ref[...]
    groups = 8
    size = rows // replicas * groups

    for i in range(replicas // groups):
        at = slice(i * size, (i + 1) * size)
        total = native(grad_ref[at, :], parts, 1, 1) + native(feed_ref[at, :], parts, 1, 1)
        value = (total[:, 2 * rank :] + total[:, rank : 2 * rank]) + total[:, :rank]
        value = value.reshape(groups, 2, half, rank)
        out_ref[i * groups : (i + 1) * groups] = jnp.concatenate([value[:, 0], value[:, 1]], axis=-1)


def project(rep, gradient, feedback, parts, replicas):
    rank = parts.shape[0] // 3
    half = gradient.shape[0] // replicas // 2
    outs = [pltpu.VMEM((replicas, half, 2 * rank), F32)]
    return call(
        project_kernel, outs, (rep, gradient, feedback, parts), (10**9, 2_500_000), "project"
    )[0]


def inverse_kernel(rep_ref, gram_ref, factor_ref, inverse_ref, unit_ref, parts_ref):
    rank = gram_ref.shape[0]
    width = 8
    row = lax.broadcasted_iota(jnp.int32, (rank, rank), 0)
    column = lax.broadcasted_iota(jnp.int32, (rank, rank), 1)
    diagonal = row == column
    gram = gram_ref[...]
    trace = jnp.sum(jnp.where(diagonal, gram, 0.0))
    gram = gram + jnp.where(diagonal, ridge_rate * trace / rank, 0.0)
    table = jnp.concatenate([gram, jnp.where(diagonal, 1.0, 0.0)], axis=1)
    row = lax.broadcasted_iota(jnp.int32, table.shape, 0)
    pivots = jnp.ones(table.shape, F32)
    for k in range(0, rank, width):
        ahead = [jnp.broadcast_to(table[:, c : c + 1], table.shape) for c in range(k, k + width)]
        lines = [table[c : c + 1, :] for c in range(k, k + width)]
        for i in range(width):
            at = k + i
            pivot = ahead[i][at : at + 1, :]
            pivots = jnp.where(row == at, pivot, pivots)
            scale = jnp.where(row > at, ahead[i] * (1.0 / pivot), 0.0)
            for j in range(i + 1, width):
                entry = ahead[j][at : at + 1, :]
                ahead[j] = ahead[j] - scale * entry
                lines[j] = lines[j] - scale[k + j : k + j + 1, :] * lines[i]
            table = table - scale * lines[i]
    inverse = table[:, rank:] / jnp.sqrt(pivots[:, rank:])
    inverse_ref[...] = inverse
    unit = exact(inverse, factor_ref[...], 1, 0)
    unit_ref[...] = unit
    for i, part in enumerate(three_parts(unit)):
        parts_ref[2 * i * rank : (2 * i + 1) * rank, :] = part
        parts_ref[(2 * i + 1) * rank : (2 * i + 2) * rank, :] = part


def invert(rep, gram, factor_t):
    rank, columns = factor_t.shape
    outs = [
        pltpu.VMEM((rank, rank), F32),
        pltpu.VMEM((rank, columns), F32),
        pltpu.VMEM((6 * rank, columns), BF16),
    ]
    return call(inverse_kernel, outs, (rep, gram, factor_t), (2 * 10**9, 500_000), "invert")


def update_kernel(replicas, rep_ref, sum_ref, inverse_ref, unit_ref, master_ref, moment_ref,
                  second_ref, send_ref, master_out, moment_out, second_out):
    rank = inverse_ref.shape[0]
    columns = master_ref.shape[1]
    packed = sum_ref[...]
    own = jnp.concatenate([packed[:, :rank], packed[:, rank:]], axis=0)
    right = exact(own, inverse_ref[...], 1, 1) / replicas
    grad = exact(right, unit_ref[...], 1, 0)
    moment = beta_one * moment_ref[...] + (1.0 - beta_one) * grad
    second = beta_two * second_ref[...] + (1.0 - beta_two) * grad * grad
    master = master_ref[...]
    master = master - learn_rate * (
        moment / (jnp.sqrt(second) + adam_eps) + decay_rate * master
    )
    moment_out[...] = moment
    second_out[...] = second
    master_out[...] = master
    high = right.astype(BF16).astype(F32)
    send_ref[:, :columns] = master.astype(BF16)
    send_ref[:, columns:] = jnp.concatenate([high, right - high], axis=1).astype(BF16)


def update(replicas, rep, own_sum, inverse, unit_t, master, moment, second):
    rows, columns = master.shape
    rank = inverse.shape[0]
    block = pltpu.VMEM(master.shape, F32)
    outs = [pltpu.VMEM((rows, columns + 2 * rank), BF16), block, block, block]
    args = (rep, own_sum, inverse, unit_t, master, moment, second)
    kernel = lambda *refs: update_kernel(replicas, *refs)
    return call(kernel, outs, args, (5 * 10**7, 600_000), "update")


def new_rows(own_y, own_z, d, block, parts_ref, grad_ref, feed_ref, out_ref):
    columns = grad_ref.shape[1]
    groups, own_rows, width = block.shape
    right = block[:, :, columns:].reshape(groups * own_rows, width - columns)
    approx = native(jnp.concatenate([right] * 3, axis=1), parts_ref[...], 1, 0)
    first = (own_y ^ d) * (groups * own_rows)
    for j in range(groups):
        at = pl.multiple_of((own_z ^ j) * own_rows, own_rows)
        source = pl.ds(pl.multiple_of(first + at, own_rows), own_rows)
        merged = grad_ref[source, :].astype(F32) + feed_ref[source, :].astype(F32)
        piece = approx[j * own_rows : (j + 1) * own_rows]
        out_ref[pl.ds(at, own_rows), :] = (merged - piece).astype(BF16)


def finish_kernel(begins, ds, rep_ref, *refs):
    count = Y_SIZE if not begins else len(ds)
    blocks, (parts_ref, grad_ref, feed_ref) = refs[:count], refs[count : count + 3]
    rest = refs[count + 3 :] if begins else refs[count + 5 :]
    if begins:
        new_far, weights_far, new_near, sems = rest
    else:
        new_far, weights_far, right_ref, new_near, right_rows, sems = rest
    columns = grad_ref.shape[1]
    groups, own_rows, width = blocks[0].shape
    size = groups * own_rows
    rank = (width - columns) // 2
    own_y, own_z = rep_ref[0] // Z_SIZE, rep_ref[0] % Z_SIZE
    copies = []

    def send(source, target):
        copies.append(pltpu.make_async_copy(source, target, sems.at[len(copies)]))
        copies[-1].start()

    def rows_of(d, j):
        at = (own_y ^ d) * size + (own_z ^ j) * own_rows
        return pl.ds(pl.multiple_of(at, own_rows), own_rows)

    for i, d in enumerate(ds):
        for j in range(groups):
            send(blocks[d].at[j, :, pl.ds(0, columns)], weights_far.at[rows_of(d, j)])
        new_rows(own_y, own_z, d, blocks[d], parts_ref, grad_ref, feed_ref, new_near.at[i])
        target = pl.ds(pl.multiple_of((own_y ^ d) * size, size), size)
        send(new_near.at[i], new_far.at[target])
    if not begins:
        for d, block in enumerate(blocks):
            for j in range(groups):
                wide = block[j, :, columns:].astype(F32)
                right_rows[rows_of(d, j), :] = wide[:, :rank] + wide[:, rank:]
        right_ref[...] = right_rows[...].T
    for copy in copies:
        copy.wait()


def finish(begins, ds, rep, blocks, parts, gradient, feedback, begun=()):
    rows, columns = gradient.shape
    groups, own_rows, width = blocks[0].shape
    rank = (width - columns) // 2
    far = pl.BlockSpec(memory_space=pl.ANY)
    outs = [jax.ShapeDtypeStruct((rows, columns), BF16)] * 2
    out_specs = [far, far]
    scratch = [pltpu.VMEM((len(ds), groups * own_rows, columns), BF16)]
    if not begins:
        outs = outs + [jax.ShapeDtypeStruct((rank, rows), F32)]
        out_specs = out_specs + [whole((rank, rows))]
        scratch = scratch + [pltpu.VMEM((rows, rank), F32)]
    return call(
        lambda *refs: finish_kernel(begins, ds, *refs),
        outs,
        (rep, *blocks, parts, gradient, feedback),
        (len(ds) * 3 * 10**8, len(ds) * 1_500_000),
        "finish_own" if begins else "finish_rest",
        aliases={} if begins else {Y_SIZE + 4: 0, Y_SIZE + 5: 1},
        out_specs=out_specs,
        spare=begun,
        scratch=scratch + [pltpu.SemaphoreType.DMA((len(ds) * (groups + 1),))],
    )


def on_device(gradient, feedback, warm_start, master, moment, second):
    replicas = lax.axis_size("rep")
    gradient, feedback = gradient[0], feedback[0]
    rep = lax.axis_index("rep").astype(jnp.int32).reshape(1)

    pieces, gradient, feedback = local_factor(rep, warm_start.T, gradient, feedback)
    quarter = sum_four([pieces[0]] + [exchange(p, "rep", d) for p, d in zip(pieces[1:], Y_STEPS)])
    for distance in (1, 2, 4):
        quarter = quarter + exchange(quarter, "rep", distance)
    quarter = quarter / replicas
    quarters = [quarter] + [exchange(quarter, "rep", d) for d in Y_STEPS]
    factor_t, parts, gram_term = assemble(rep, quarters)

    gram_pair = gram_term + exchange(gram_term, "shard", 1)
    packed = project(rep, gradient, feedback, parts, replicas)
    gram_pair, packed = lax.optimization_barrier((gram_pair, packed))
    received = lax.all_to_all(packed, "rep", 0, 0, tiled=True)
    gram = sum_four([gram_pair] + [exchange(gram_pair, "shard", d) for d in X_STEPS])
    inverse, unit_t, unit_parts = invert(rep, gram, factor_t)
    received, inverse, unit_t, unit_parts = lax.optimization_barrier(
        (received, inverse, unit_t, unit_parts)
    )
    own_sum = shard_sum(received.sum(0))

    send, master_out, moment_out, second_out = update(
        replicas, rep, own_sum, inverse, unit_t, master, moment, second
    )
    pair = jnp.stack([send, exchange(send, "rep", 1)])
    column = jnp.concatenate([pair] + [exchange(pair, "rep", d) for d in (2, 4, 6)])
    others = [exchange(column, "rep", d) for d in Y_STEPS]
    begun = finish(True, (0,), rep, [column], unit_parts, gradient, feedback)
    blocks = [column] + others
    new_feedback, weights, right_t = finish(
        False, (1, 2, 3), rep, blocks, unit_parts, gradient, feedback, begun
    )
    return (new_feedback[None], weights, master_out, moment_out, second_out, right_t.T)


def solution(mesh):
    return jax.shard_map(
        on_device,
        mesh=mesh,
        in_specs=(
            P("rep", None, "shard"),
            P("rep", None, "shard"),
            P(),
            P("rep", "shard"),
            P("rep", "shard"),
            P("rep", "shard"),
        ),
        out_specs=(
            P("rep", None, "shard"),
            P(None, "shard"),
            P("rep", "shard"),
            P("rep", "shard"),
            P("rep", "shard"),
            P(),
        ),
        check_vma=False,
    )
```

```python
import jax
import jax.numpy as jnp
from jax import lax
from jax.experimental import pallas as pl
from jax.experimental.pallas import tpu as pltpu
from jax.sharding import PartitionSpec as P

HIGHEST = lax.Precision.HIGHEST
beta_one = 0.9
beta_two = 0.95
learn_rate = 0.02
decay_rate = 0.1
adam_eps = 1e-08
ridge_rate = 1e-06

F32 = jnp.float32
BF16 = jnp.bfloat16
Y_SIZE, Z_SIZE = 4, 8
Y_STEPS = (8, 16, 24)
X_STEPS = (2, 4, 6)
Z_SUM_STEPS = (1, 3, 7)
Z_PAIRS = (2, 5, 6)
Z_ORDER = tuple(pair ^ bit for pair in (0,) + Z_PAIRS for bit in (0, 1))
ROW_BLOCKS = 4


def exact(left, right, left_dim, right_dim):
    return lax.dot_general(
        left,
        right,
        (((left_dim,), (right_dim,)), ((), ())),
        precision=HIGHEST,
        preferred_element_type=F32,
    )


def native(left, right, left_dim, right_dim):
    return lax.dot_general(
        left, right, (((left_dim,), (right_dim,)), ((), ())), preferred_element_type=F32
    )


def three_parts(value):
    high = value.astype(BF16)
    rest = value - high.astype(F32)
    middle = rest.astype(BF16)
    return high, middle, (rest - middle.astype(F32)).astype(BF16)


def exchange(value, axis, distance):
    return lax.ppermute(value, axis, [(i, i ^ distance) for i in range(lax.axis_size(axis))])


def sum_four(terms):
    return (terms[0] + terms[1]) + (terms[2] + terms[3])


def shard_sum(value):
    value = value + exchange(value, "shard", 1)
    return sum_four([value] + [exchange(value, "shard", d) for d in X_STEPS])


def whole(shape):
    return pl.BlockSpec(shape, lambda *_: (0,) * len(shape))


def call(kernel, outs, args, cost, name, aliases=None, grid=None, out_specs=None, spare=(),
         scratch=()):
    specs = [pl.BlockSpec(memory_space=pltpu.VMEM)] * (len(args) - 1)
    specs += [pl.BlockSpec(memory_space=pl.ANY)] * len(spare)
    flops, traffic = cost
    return pl.pallas_call(
        kernel,
        out_shape=outs,
        grid_spec=pltpu.PrefetchScalarGridSpec(
            num_scalar_prefetch=1,
            grid=grid or (1,),
            in_specs=specs,
            out_specs=out_specs or [pl.BlockSpec(memory_space=pltpu.VMEM)] * len(outs),
            scratch_shapes=scratch,
        ),
        input_output_aliases=aliases or {},
        compiler_params=pltpu.CompilerParams(vmem_limit_bytes=16 * 2**20),
        cost_estimate=pl.CostEstimate(flops=flops, bytes_accessed=traffic, transcendentals=0),
        name=name,
    )(
        args[0],
        *[pltpu.with_memory_space_constraint(v, pltpu.VMEM) for v in args[1:]],
        *spare,
    )


def factor_kernel(rep_ref, warm_far, grad_far, feed_far, *refs):
    outs, (grad_ref, feed_ref, warm_ref, parts_ref, total_ref, sems) = refs[:Y_SIZE], refs[Y_SIZE:]
    rank, rows = warm_ref.shape
    quarter = outs[0].shape[1]
    size = rows // ROW_BLOCKS
    warm_copy = pltpu.make_async_copy(warm_far, warm_ref, sems.at[2 * ROW_BLOCKS])
    warm_copy.start()
    copies = []
    for i in range(ROW_BLOCKS):
        at = pl.ds(i * size, size)
        for k, (far, ref) in enumerate([(grad_far, grad_ref), (feed_far, feed_ref)]):
            copies.append(pltpu.make_async_copy(far.at[at], ref.at[at], sems.at[2 * i + k]))
            copies[-1].start()
    warm_copy.wait()
    for i, part in enumerate(three_parts(warm_ref[...])):
        parts_ref[i * rank : (i + 1) * rank, :] = part
    total = None
    for i in range(ROW_BLOCKS):
        at = slice(i * size, (i + 1) * size)
        copies[2 * i].wait()
        copies[2 * i + 1].wait()
        parts = parts_ref[:, at]
        term = native(parts, grad_ref[at, :], 1, 0) + native(parts, feed_ref[at, :], 1, 0)
        total = term if total is None else total + term
    total_ref[...] = (total[2 * rank :] + total[rank : 2 * rank]) + total[:rank]
    own = rep_ref[0] // Z_SIZE
    for d, out in enumerate(outs):
        out[...] = total_ref[:, pl.ds(pl.multiple_of((own ^ d) * quarter, quarter), quarter)]


def local_factor(rep, warm_t, gradient, feedback):
    rank, rows = warm_t.shape
    columns = gradient.shape[1]
    near = pltpu.VMEM((rows, columns), BF16)
    args = [pltpu.with_memory_space_constraint(v, pltpu.HBM) for v in (warm_t, gradient, feedback)]
    outs = pl.pallas_call(
        factor_kernel,
        out_shape=[pltpu.VMEM((rank, columns // Y_SIZE), F32)] * Y_SIZE + [near] * 2,
        grid_spec=pltpu.PrefetchScalarGridSpec(
            num_scalar_prefetch=1,
            grid=(1,),
            in_specs=[pl.BlockSpec(memory_space=pl.ANY)] * 3,
            out_specs=[pl.BlockSpec(memory_space=pltpu.VMEM)] * (Y_SIZE + 2),
            scratch_shapes=[
                pltpu.VMEM((rank, rows), F32),
                pltpu.VMEM((3 * rank, rows), BF16),
                pltpu.VMEM((rank, columns), F32),
                pltpu.SemaphoreType.DMA((2 * ROW_BLOCKS + 1,)),
            ],
        ),
        compiler_params=pltpu.CompilerParams(vmem_limit_bytes=16 * 2**20),
        cost_estimate=pl.CostEstimate(flops=10**9, bytes_accessed=2_500_000, transcendentals=0),
        name="local_factor",
    )(rep, *args)
    return outs[:Y_SIZE], outs[Y_SIZE], outs[Y_SIZE + 1]


def assemble_kernel(rep_ref, *refs):
    quarters, (factor_ref, parts_ref, gram_ref) = refs[:Y_SIZE], refs[Y_SIZE:]
    rank, quarter = quarters[0].shape
    own = rep_ref[0] // Z_SIZE
    for d, block in enumerate(quarters):
        at = pl.ds(pl.multiple_of((own ^ d) * quarter, quarter), quarter)
        factor_ref[:, at] = block[...]
    factor = factor_ref[...]
    for i, part in enumerate(three_parts(factor)):
        parts_ref[i * rank : (i + 1) * rank, :] = part
    gram_ref[...] = exact(factor, factor, 1, 1)


def assemble(rep, quarters):
    rank, quarter = quarters[0].shape
    columns = quarter * Y_SIZE
    outs = [
        pltpu.VMEM((rank, columns), F32),
        pltpu.VMEM((3 * rank, columns), BF16),
        pltpu.VMEM((rank, rank), F32),
    ]
    return call(assemble_kernel, outs, (rep, *quarters), (10**8, 500_000), "assemble_factor")


def project_kernel(rep_ref, grad_ref, feed_ref, parts_ref, out_ref):
    replicas, half, _ = out_ref.shape
    rows = grad_ref.shape[0]
    rank = parts_ref.shape[0] // 3
    parts = parts_ref[...]
    groups = 8
    size = rows // replicas * groups

    for i in range(replicas // groups):
        at = slice(i * size, (i + 1) * size)
        total = native(grad_ref[at, :], parts, 1, 1) + native(feed_ref[at, :], parts, 1, 1)
        value = (total[:, 2 * rank :] + total[:, rank : 2 * rank]) + total[:, :rank]
        value = value.reshape(groups, 2, half, rank)
        out_ref[i * groups : (i + 1) * groups] = jnp.concatenate([value[:, 0], value[:, 1]], axis=-1)


def project(rep, gradient, feedback, parts, replicas):
    rank = parts.shape[0] // 3
    half = gradient.shape[0] // replicas // 2
    outs = [pltpu.VMEM((replicas, half, 2 * rank), F32)]
    return call(
        project_kernel, outs, (rep, gradient, feedback, parts), (10**9, 2_500_000), "project"
    )[0]


def inverse_kernel(rep_ref, gram_ref, factor_ref, inverse_ref, unit_ref, parts_ref):
    rank = gram_ref.shape[0]
    width = 8
    row = lax.broadcasted_iota(jnp.int32, (rank, rank), 0)
    column = lax.broadcasted_iota(jnp.int32, (rank, rank), 1)
    diagonal = row == column
    gram = gram_ref[...]
    trace = jnp.sum(jnp.where(diagonal, gram, 0.0))
    gram = gram + jnp.where(diagonal, ridge_rate * trace / rank, 0.0)
    table = jnp.concatenate([gram, jnp.where(diagonal, 1.0, 0.0)], axis=1)
    row = lax.broadcasted_iota(jnp.int32, table.shape, 0)
    pivots = jnp.ones(table.shape, F32)
    for k in range(0, rank, width):
        ahead = [jnp.broadcast_to(table[:, c : c + 1], table.shape) for c in range(k, k + width)]
        lines = [table[c : c + 1, :] for c in range(k, k + width)]
        for i in range(width):
            at = k + i
            pivot = ahead[i][at : at + 1, :]
            pivots = jnp.where(row == at, pivot, pivots)
            scale = jnp.where(row > at, ahead[i] * (1.0 / pivot), 0.0)
            for j in range(i + 1, width):
                entry = ahead[j][at : at + 1, :]
                ahead[j] = ahead[j] - scale * entry
                lines[j] = lines[j] - scale[k + j : k + j + 1, :] * lines[i]
            table = table - scale * lines[i]
    inverse = table[:, rank:] / jnp.sqrt(pivots[:, rank:])
    inverse_ref[...] = inverse
    unit = exact(inverse, factor_ref[...], 1, 0)
    unit_ref[...] = unit
    for i, part in enumerate(three_parts(unit)):
        parts_ref[2 * i * rank : (2 * i + 1) * rank, :] = part
        parts_ref[(2 * i + 1) * rank : (2 * i + 2) * rank, :] = part


def invert(rep, gram, factor_t):
    rank, columns = factor_t.shape
    outs = [
        pltpu.VMEM((rank, rank), F32),
        pltpu.VMEM((rank, columns), F32),
        pltpu.VMEM((6 * rank, columns), BF16),
    ]
    return call(inverse_kernel, outs, (rep, gram, factor_t), (2 * 10**9, 500_000), "invert")


def update_kernel(replicas, rep_ref, sum_ref, inverse_ref, unit_ref, master_ref, moment_ref,
                  second_ref, send_ref, master_out, moment_out, second_out):
    rank = inverse_ref.shape[0]
    columns = master_ref.shape[1]
    packed = sum_ref[...]
    own = jnp.concatenate([packed[:, :rank], packed[:, rank:]], axis=0)
    right = exact(own, inverse_ref[...], 1, 1) / replicas
    grad = exact(right, unit_ref[...], 1, 0)
    moment = beta_one * moment_ref[...] + (1.0 - beta_one) * grad
    second = beta_two * second_ref[...] + (1.0 - beta_two) * grad * grad
    master = master_ref[...]
    master = master - learn_rate * (
        moment / (jnp.sqrt(second) + adam_eps) + decay_rate * master
    )
    moment_out[...] = moment
    second_out[...] = second
    master_out[...] = master
    high = right.astype(BF16).astype(F32)
    send_ref[:, :columns] = master.astype(BF16)
    send_ref[:, columns:] = jnp.concatenate([high, right - high], axis=1).astype(BF16)


def update(replicas, rep, own_sum, inverse, unit_t, master, moment, second):
    rows, columns = master.shape
    rank = inverse.shape[0]
    block = pltpu.VMEM(master.shape, F32)
    outs = [pltpu.VMEM((rows, columns + 2 * rank), BF16), block, block, block]
    args = (rep, own_sum, inverse, unit_t, master, moment, second)
    kernel = lambda *refs: update_kernel(replicas, *refs)
    return call(kernel, outs, args, (5 * 10**7, 600_000), "update")


def new_rows(own_y, own_z, d, block, parts_ref, grad_ref, feed_ref, out_ref):
    columns = grad_ref.shape[1]
    groups, own_rows, width = block.shape
    right = block[:, :, columns:].reshape(groups * own_rows, width - columns)
    approx = native(jnp.concatenate([right] * 3, axis=1), parts_ref[...], 1, 0)
    first = (own_y ^ d) * (groups * own_rows)
    for j in range(groups):
        at = pl.multiple_of((own_z ^ Z_ORDER[j]) * own_rows, own_rows)
        source = pl.ds(pl.multiple_of(first + at, own_rows), own_rows)
        merged = grad_ref[source, :].astype(F32) + feed_ref[source, :].astype(F32)
        piece = approx[j * own_rows : (j + 1) * own_rows]
        out_ref[pl.ds(at, own_rows), :] = (merged - piece).astype(BF16)


def finish_kernel(begins, ds, rep_ref, *refs):
    count = Y_SIZE if not begins else len(ds)
    blocks, (parts_ref, grad_ref, feed_ref) = refs[:count], refs[count : count + 3]
    rest = refs[count + 3 :] if begins else refs[count + 5 :]
    if begins:
        new_far, weights_far, new_near, sems = rest
    else:
        new_far, weights_far, right_ref, new_near, right_rows, sems = rest
    columns = grad_ref.shape[1]
    groups, own_rows, width = blocks[0].shape
    size = groups * own_rows
    rank = (width - columns) // 2
    own_y, own_z = rep_ref[0] // Z_SIZE, rep_ref[0] % Z_SIZE
    copies = []

    def send(source, target):
        copies.append(pltpu.make_async_copy(source, target, sems.at[len(copies)]))
        copies[-1].start()

    def rows_of(d, j):
        at = (own_y ^ d) * size + (own_z ^ Z_ORDER[j]) * own_rows
        return pl.ds(pl.multiple_of(at, own_rows), own_rows)

    for i, d in enumerate(ds):
        for j in range(groups):
            send(blocks[d].at[j, :, pl.ds(0, columns)], weights_far.at[rows_of(d, j)])
        new_rows(own_y, own_z, d, blocks[d], parts_ref, grad_ref, feed_ref, new_near.at[i])
        target = pl.ds(pl.multiple_of((own_y ^ d) * size, size), size)
        send(new_near.at[i], new_far.at[target])
    if not begins:
        for d, block in enumerate(blocks):
            for j in range(groups):
                wide = block[j, :, columns:].astype(F32)
                right_rows[rows_of(d, j), :] = wide[:, :rank] + wide[:, rank:]
        right_ref[...] = right_rows[...].T
    for copy in copies:
        copy.wait()


def finish(begins, ds, rep, blocks, parts, gradient, feedback, begun=()):
    rows, columns = gradient.shape
    groups, own_rows, width = blocks[0].shape
    rank = (width - columns) // 2
    far = pl.BlockSpec(memory_space=pl.ANY)
    outs = [jax.ShapeDtypeStruct((rows, columns), BF16)] * 2
    out_specs = [far, far]
    scratch = [pltpu.VMEM((len(ds), groups * own_rows, columns), BF16)]
    if not begins:
        outs = outs + [jax.ShapeDtypeStruct((rank, rows), F32)]
        out_specs = out_specs + [whole((rank, rows))]
        scratch = scratch + [pltpu.VMEM((rows, rank), F32)]
    return call(
        lambda *refs: finish_kernel(begins, ds, *refs),
        outs,
        (rep, *blocks, parts, gradient, feedback),
        (len(ds) * 3 * 10**8, len(ds) * 1_500_000),
        "finish_own" if begins else "finish_rest",
        aliases={} if begins else {Y_SIZE + 4: 0, Y_SIZE + 5: 1},
        out_specs=out_specs,
        spare=begun,
        scratch=scratch + [pltpu.SemaphoreType.DMA((len(ds) * (groups + 1),))],
    )


def on_device(gradient, feedback, warm_start, master, moment, second):
    replicas = lax.axis_size("rep")
    gradient, feedback = gradient[0], feedback[0]
    rep = lax.axis_index("rep").astype(jnp.int32).reshape(1)

    pieces, gradient, feedback = local_factor(rep, warm_start.T, gradient, feedback)
    quarter = sum_four([pieces[0]] + [exchange(p, "rep", d) for p, d in zip(pieces[1:], Y_STEPS)])
    for distance in Z_SUM_STEPS:
        quarter = quarter + exchange(quarter, "rep", distance)
    quarter = quarter / replicas
    quarters = [quarter] + [exchange(quarter, "rep", d) for d in Y_STEPS]
    factor_t, parts, gram_term = assemble(rep, quarters)

    gram_pair = gram_term + exchange(gram_term, "shard", 1)
    packed = project(rep, gradient, feedback, parts, replicas)
    gram_pair, packed = lax.optimization_barrier((gram_pair, packed))
    received = lax.all_to_all(packed, "rep", 0, 0, tiled=True)
    gram = sum_four([gram_pair] + [exchange(gram_pair, "shard", d) for d in X_STEPS])
    inverse, unit_t, unit_parts = invert(rep, gram, factor_t)
    received, inverse, unit_t, unit_parts = lax.optimization_barrier(
        (received, inverse, unit_t, unit_parts)
    )
    own_sum = shard_sum(received.sum(0))

    send, master_out, moment_out, second_out = update(
        replicas, rep, own_sum, inverse, unit_t, master, moment, second
    )
    pair = jnp.stack([send, exchange(send, "rep", 1)])
    column = jnp.concatenate([pair] + [exchange(pair, "rep", d) for d in Z_PAIRS])
    others = [exchange(column, "rep", d) for d in Y_STEPS]
    begun = finish(True, (0,), rep, [column], unit_parts, gradient, feedback)
    blocks = [column] + others
    new_feedback, weights, right_t = finish(
        False, (1, 2, 3), rep, blocks, unit_parts, gradient, feedback, begun
    )
    return (new_feedback[None], weights, master_out, moment_out, second_out, right_t.T)


def solution(mesh):
    return jax.shard_map(
        on_device,
        mesh=mesh,
        in_specs=(
            P("rep", None, "shard"),
            P("rep", None, "shard"),
            P(),
            P("rep", "shard"),
            P("rep", "shard"),
            P("rep", "shard"),
        ),
        out_specs=(
            P("rep", None, "shard"),
            P(None, "shard"),
            P("rep", "shard"),
            P("rep", "shard"),
            P("rep", "shard"),
            P(),
        ),
        check_vma=False,
    )
```

```python
import jax
import jax.numpy as jnp
from jax import lax
from jax.experimental import pallas as pl
from jax.experimental.pallas import tpu as pltpu
from jax.sharding import PartitionSpec as P

HIGHEST = lax.Precision.HIGHEST
beta_one = 0.9
beta_two = 0.95
learn_rate = 0.02
decay_rate = 0.1
adam_eps = 1e-08
ridge_rate = 1e-06

F32 = jnp.float32
BF16 = jnp.bfloat16
Y_SIZE, Z_SIZE = 4, 8
Y_STEPS = (8, 16, 24)
X_STEPS = (2, 4, 6)
Z_SUM_STEPS = (1, 3, 7)
Z_PAIRS = (2, 5, 6)
Z_ORDER = tuple(pair ^ bit for pair in (0,) + Z_PAIRS for bit in (0, 1))
ROW_BLOCKS = 4


def exact(left, right, left_dim, right_dim):
    return lax.dot_general(
        left,
        right,
        (((left_dim,), (right_dim,)), ((), ())),
        precision=HIGHEST,
        preferred_element_type=F32,
    )


def native(left, right, left_dim, right_dim):
    return lax.dot_general(
        left, right, (((left_dim,), (right_dim,)), ((), ())), preferred_element_type=F32
    )


def three_parts(value):
    high = value.astype(BF16)
    rest = value - high.astype(F32)
    middle = rest.astype(BF16)
    return high, middle, (rest - middle.astype(F32)).astype(BF16)


def exchange(value, axis, distance):
    return lax.ppermute(value, axis, [(i, i ^ distance) for i in range(lax.axis_size(axis))])


def sum_four(terms):
    return (terms[0] + terms[1]) + (terms[2] + terms[3])


def shard_sum(value):
    value = value + exchange(value, "shard", 1)
    return sum_four([value] + [exchange(value, "shard", d) for d in X_STEPS])


def call(kernel, outs, args, cost, name, aliases=None, out_specs=None, spare=(), scratch=()):
    specs = [pl.BlockSpec(memory_space=pltpu.VMEM)] * len(args)
    specs += [pl.BlockSpec(memory_space=pl.ANY)] * len(spare)
    flops, traffic = cost
    return pl.pallas_call(
        kernel,
        out_shape=outs,
        in_specs=specs,
        out_specs=out_specs or [pl.BlockSpec(memory_space=pltpu.VMEM)] * len(outs),
        scratch_shapes=scratch,
        input_output_aliases=aliases or {},
        compiler_params=pltpu.CompilerParams(vmem_limit_bytes=16 * 2**20),
        cost_estimate=pl.CostEstimate(flops=flops, bytes_accessed=traffic, transcendentals=0),
        name=name,
    )(*[pltpu.with_memory_space_constraint(v, pltpu.VMEM) for v in args], *spare)


def factor_kernel(warm_far, grad_far, feed_far, *refs):
    outs, (grad_ref, feed_ref, warm_ref, parts_ref, total_ref, sems) = refs[:Y_SIZE], refs[Y_SIZE:]
    rank, rows = warm_ref.shape
    quarter = outs[0].shape[1]
    size = rows // ROW_BLOCKS
    warm_copy = pltpu.make_async_copy(warm_far, warm_ref, sems.at[2 * ROW_BLOCKS])
    warm_copy.start()
    copies = []
    for i in range(ROW_BLOCKS):
        at = pl.ds(i * size, size)
        for k, (far, ref) in enumerate([(grad_far, grad_ref), (feed_far, feed_ref)]):
            copies.append(pltpu.make_async_copy(far.at[at], ref.at[at], sems.at[2 * i + k]))
            copies[-1].start()
    warm_copy.wait()
    for i, part in enumerate(three_parts(warm_ref[...])):
        parts_ref[i * rank : (i + 1) * rank, :] = part
    total = None
    for i in range(ROW_BLOCKS):
        at = slice(i * size, (i + 1) * size)
        copies[2 * i].wait()
        copies[2 * i + 1].wait()
        parts = parts_ref[:, at]
        term = native(parts, grad_ref[at, :], 1, 0) + native(parts, feed_ref[at, :], 1, 0)
        total = term if total is None else total + term
    total_ref[...] = (total[2 * rank :] + total[rank : 2 * rank]) + total[:rank]
    own = lax.axis_index("rep") // Z_SIZE
    for d, out in enumerate(outs):
        out[...] = total_ref[:, pl.ds(pl.multiple_of((own ^ d) * quarter, quarter), quarter)]


def local_factor(warm_t, gradient, feedback):
    rank, rows = warm_t.shape
    columns = gradient.shape[1]
    near = pltpu.VMEM((rows, columns), BF16)
    args = [pltpu.with_memory_space_constraint(v, pltpu.HBM) for v in (warm_t, gradient, feedback)]
    outs = pl.pallas_call(
        factor_kernel,
        out_shape=[pltpu.VMEM((rank, columns // Y_SIZE), F32)] * Y_SIZE + [near] * 2,
        in_specs=[pl.BlockSpec(memory_space=pl.ANY)] * 3,
        out_specs=[pl.BlockSpec(memory_space=pltpu.VMEM)] * (Y_SIZE + 2),
        scratch_shapes=[
            pltpu.VMEM((rank, rows), F32),
            pltpu.VMEM((3 * rank, rows), BF16),
            pltpu.VMEM((rank, columns), F32),
            pltpu.SemaphoreType.DMA((2 * ROW_BLOCKS + 1,)),
        ],
        compiler_params=pltpu.CompilerParams(vmem_limit_bytes=16 * 2**20),
        cost_estimate=pl.CostEstimate(flops=10**9, bytes_accessed=2_500_000, transcendentals=0),
        name="local_factor",
    )(*args)
    return outs[:Y_SIZE], outs[Y_SIZE], outs[Y_SIZE + 1]


def assemble_kernel(*refs):
    quarters, (factor_ref, parts_ref, gram_ref) = refs[:Y_SIZE], refs[Y_SIZE:]
    rank, quarter = quarters[0].shape
    own = lax.axis_index("rep") // Z_SIZE
    for d, block in enumerate(quarters):
        at = pl.ds(pl.multiple_of((own ^ d) * quarter, quarter), quarter)
        factor_ref[:, at] = block[...]
    factor = factor_ref[...]
    for i, part in enumerate(three_parts(factor)):
        parts_ref[i * rank : (i + 1) * rank, :] = part
    gram_ref[...] = exact(factor, factor, 1, 1)


def assemble(quarters):
    rank, quarter = quarters[0].shape
    columns = quarter * Y_SIZE
    outs = [
        pltpu.VMEM((rank, columns), F32),
        pltpu.VMEM((3 * rank, columns), BF16),
        pltpu.VMEM((rank, rank), F32),
    ]
    return call(assemble_kernel, outs, tuple(quarters), (10**8, 500_000), "assemble_factor")


def project_kernel(grad_ref, feed_ref, parts_ref, out_ref):
    replicas, half, _ = out_ref.shape
    rows = grad_ref.shape[0]
    rank = parts_ref.shape[0] // 3
    parts = parts_ref[...]
    groups = 8
    size = rows // replicas * groups

    for i in range(replicas // groups):
        at = slice(i * size, (i + 1) * size)
        total = native(grad_ref[at, :], parts, 1, 1) + native(feed_ref[at, :], parts, 1, 1)
        value = (total[:, 2 * rank :] + total[:, rank : 2 * rank]) + total[:, :rank]
        value = value.reshape(groups, 2, half, rank)
        out_ref[i * groups : (i + 1) * groups] = jnp.concatenate([value[:, 0], value[:, 1]], axis=-1)


def project(gradient, feedback, parts, replicas):
    rank = parts.shape[0] // 3
    half = gradient.shape[0] // replicas // 2
    outs = [pltpu.VMEM((replicas, half, 2 * rank), F32)]
    return call(
        project_kernel, outs, (gradient, feedback, parts), (10**9, 2_500_000), "project"
    )[0]


def inverse_kernel(gram_ref, factor_ref, inverse_ref, unit_ref, parts_ref):
    rank = gram_ref.shape[0]
    width = 8
    row = lax.broadcasted_iota(jnp.int32, (rank, rank), 0)
    column = lax.broadcasted_iota(jnp.int32, (rank, rank), 1)
    diagonal = row == column
    gram = gram_ref[...]
    trace = jnp.sum(jnp.where(diagonal, gram, 0.0))
    gram = gram + jnp.where(diagonal, ridge_rate * trace / rank, 0.0)
    table = jnp.concatenate([gram, jnp.where(diagonal, 1.0, 0.0)], axis=1)
    row = lax.broadcasted_iota(jnp.int32, table.shape, 0)
    pivots = jnp.ones(table.shape, F32)
    for k in range(0, rank, width):
        ahead = [jnp.broadcast_to(table[:, c : c + 1], table.shape) for c in range(k, k + width)]
        lines = [table[c : c + 1, :] for c in range(k, k + width)]
        for i in range(width):
            at = k + i
            pivot = ahead[i][at : at + 1, :]
            pivots = jnp.where(row == at, pivot, pivots)
            scale = jnp.where(row > at, ahead[i] * (1.0 / pivot), 0.0)
            for j in range(i + 1, width):
                entry = ahead[j][at : at + 1, :]
                ahead[j] = ahead[j] - scale * entry
                lines[j] = lines[j] - scale[k + j : k + j + 1, :] * lines[i]
            table = table - scale * lines[i]
    inverse = table[:, rank:] / jnp.sqrt(pivots[:, rank:])
    inverse_ref[...] = inverse
    unit = exact(inverse, factor_ref[...], 1, 0)
    unit_ref[...] = unit
    for i, part in enumerate(three_parts(unit)):
        parts_ref[2 * i * rank : (2 * i + 1) * rank, :] = part
        parts_ref[(2 * i + 1) * rank : (2 * i + 2) * rank, :] = part


def invert(gram, factor_t):
    rank, columns = factor_t.shape
    outs = [
        pltpu.VMEM((rank, rank), F32),
        pltpu.VMEM((rank, columns), F32),
        pltpu.VMEM((6 * rank, columns), BF16),
    ]
    return call(inverse_kernel, outs, (gram, factor_t), (2 * 10**9, 500_000), "invert")


def update_kernel(replicas, sum_ref, inverse_ref, unit_ref, master_ref, moment_ref,
                  second_ref, send_ref, master_out, moment_out, second_out):
    rank = inverse_ref.shape[0]
    columns = master_ref.shape[1]
    packed = sum_ref[...]
    own = jnp.concatenate([packed[:, :rank], packed[:, rank:]], axis=0)
    right = exact(own, inverse_ref[...], 1, 1) / replicas
    grad = exact(right, unit_ref[...], 1, 0)
    moment = beta_one * moment_ref[...] + (1.0 - beta_one) * grad
    second = beta_two * second_ref[...] + (1.0 - beta_two) * grad * grad
    master = master_ref[...]
    master = master - learn_rate * (
        moment / (jnp.sqrt(second) + adam_eps) + decay_rate * master
    )
    moment_out[...] = moment
    second_out[...] = second
    master_out[...] = master
    high = right.astype(BF16).astype(F32)
    send_ref[:, :columns] = master.astype(BF16)
    send_ref[:, columns:] = jnp.concatenate([high, right - high], axis=1).astype(BF16)


def update(replicas, own_sum, inverse, unit_t, master, moment, second):
    rows, columns = master.shape
    rank = inverse.shape[0]
    block = pltpu.VMEM(master.shape, F32)
    outs = [pltpu.VMEM((rows, columns + 2 * rank), BF16), block, block, block]
    args = (own_sum, inverse, unit_t, master, moment, second)
    kernel = lambda *refs: update_kernel(replicas, *refs)
    return call(kernel, outs, args, (5 * 10**7, 600_000), "update")


def finish_kernel(begins, ds, *refs):
    count = Y_SIZE if not begins else len(ds)
    blocks, (parts_ref, grad_ref, feed_ref) = refs[:count], refs[count : count + 3]
    rest = refs[count + 3 :] if begins else refs[count + 5 :]
    if begins:
        new_far, weights_far, new_near, sems = rest
    else:
        new_far, weights_far, right_far, new_near, right_near, sems = rest
    columns = grad_ref.shape[1]
    groups, own_rows, width = blocks[0].shape
    size = groups * own_rows
    rank = (width - columns) // 2
    own_y, own_z = lax.axis_index("rep") // Z_SIZE, lax.axis_index("rep") % Z_SIZE
    copies = []

    def send(source, target):
        copies.append(pltpu.make_async_copy(source, target, sems.at[len(copies)]))
        copies[-1].start()

    def piece_of(z):
        step = own_z ^ z
        return step ^ ((step >> 2) & (1 - ((step >> 1) & 1)))

    def rights_of(block):
        return jnp.concatenate([block[piece_of(z), :, columns:] for z in range(groups)], axis=0)

    def rows_of(d):
        return pl.ds(pl.multiple_of((own_y ^ d) * size, size), size)

    for d in ds:
        for j in range(groups):
            at = (own_y ^ d) * size + (own_z ^ Z_ORDER[j]) * own_rows
            target = weights_far.at[pl.ds(pl.multiple_of(at, own_rows), own_rows)]
            send(blocks[d].at[j, :, pl.ds(0, columns)], target)
    if not begins:
        row = lax.broadcasted_iota(jnp.int32, (rank, 2 * rank), 0)
        column = lax.broadcasted_iota(jnp.int32, (rank, 2 * rank), 1)
        both = jnp.where((row == column) | (row + rank == column), 1.0, 0.0).astype(BF16)
        for d, block in enumerate(blocks):
            right_near[:, rows_of(d)] = native(both, rights_of(block), 1, 1)
        send(right_near, right_far)
    for i, d in enumerate(ds):
        right = rights_of(blocks[d])
        approx = native(jnp.concatenate([right] * 3, axis=1), parts_ref[...], 1, 0)
        merged = grad_ref[rows_of(d), :].astype(F32) + feed_ref[rows_of(d), :].astype(F32)
        new_near[i] = (merged - approx).astype(BF16)
        send(new_near.at[i], new_far.at[rows_of(d)])
    for copy in copies:
        copy.wait()


def finish(begins, ds, blocks, parts, gradient, feedback, begun=()):
    rows, columns = gradient.shape
    groups, own_rows, width = blocks[0].shape
    rank = (width - columns) // 2
    far = pl.BlockSpec(memory_space=pl.ANY)
    outs = [jax.ShapeDtypeStruct((rows, columns), BF16)] * 2
    out_specs = [far, far]
    scratch = [pltpu.VMEM((len(ds), groups * own_rows, columns), BF16)]
    if not begins:
        outs = outs + [jax.ShapeDtypeStruct((rank, rows), F32)]
        out_specs = out_specs + [far]
        scratch = scratch + [pltpu.VMEM((rank, rows), F32)]
    return call(
        lambda *refs: finish_kernel(begins, ds, *refs),
        outs,
        (*blocks, parts, gradient, feedback),
        (len(ds) * 3 * 10**8, len(ds) * 1_500_000),
        "finish_own" if begins else "finish_rest",
        aliases={} if begins else {Y_SIZE + 3: 0, Y_SIZE + 4: 1},
        out_specs=out_specs,
        spare=begun,
        scratch=scratch + [pltpu.SemaphoreType.DMA((len(ds) * (groups + 1) + 1,))],
    )


def on_device(gradient, feedback, warm_start, master, moment, second):
    replicas = lax.axis_size("rep")
    gradient, feedback = gradient[0], feedback[0]

    pieces, gradient, feedback = local_factor(warm_start.T, gradient, feedback)
    quarter = sum_four([pieces[0]] + [exchange(p, "rep", d) for p, d in zip(pieces[1:], Y_STEPS)])
    for distance in Z_SUM_STEPS:
        quarter = quarter + exchange(quarter, "rep", distance)
    quarter = quarter / replicas
    quarters = [quarter] + [exchange(quarter, "rep", d) for d in Y_STEPS]
    factor_t, parts, gram_term = assemble(quarters)

    gram_pair = gram_term + exchange(gram_term, "shard", 1)
    packed = project(gradient, feedback, parts, replicas)
    gram_pair, packed = lax.optimization_barrier((gram_pair, packed))
    received = lax.all_to_all(packed, "rep", 0, 0, tiled=True)
    gram = sum_four([gram_pair] + [exchange(gram_pair, "shard", d) for d in X_STEPS])
    inverse, unit_t, unit_parts = invert(gram, factor_t)
    received, inverse, unit_t, unit_parts = lax.optimization_barrier(
        (received, inverse, unit_t, unit_parts)
    )
    own_sum = shard_sum(received.sum(0))

    send, master_out, moment_out, second_out = update(
        replicas, own_sum, inverse, unit_t, master, moment, second
    )
    pair = jnp.stack([send, exchange(send, "rep", 1)])
    column = jnp.concatenate([pair] + [exchange(pair, "rep", d) for d in Z_PAIRS])
    others = [exchange(column, "rep", d) for d in Y_STEPS]
    begun = finish(True, (0,), [column], unit_parts, gradient, feedback)
    blocks = [column] + others
    new_feedback, weights, right_t = finish(
        False, (1, 2, 3), blocks, unit_parts, gradient, feedback, begun
    )
    return (new_feedback[None], weights, master_out, moment_out, second_out, right_t.T)


def solution(mesh):
    return jax.shard_map(
        on_device,
        mesh=mesh,
        in_specs=(
            P("rep", None, "shard"),
            P("rep", None, "shard"),
            P(),
            P("rep", "shard"),
            P("rep", "shard"),
            P("rep", "shard"),
        ),
        out_specs=(
            P("rep", None, "shard"),
            P(None, "shard"),
            P("rep", "shard"),
            P("rep", "shard"),
            P("rep", "shard"),
            P(),
        ),
        check_vma=False,
    )
```

```python
import jax
import jax.numpy as jnp
from jax import lax
from jax.experimental import pallas as pl
from jax.experimental.pallas import tpu as pltpu
from jax.sharding import PartitionSpec as P

HIGHEST = lax.Precision.HIGHEST
beta_one = 0.9
beta_two = 0.95
learn_rate = 0.02
decay_rate = 0.1
adam_eps = 1e-08
ridge_rate = 1e-06

F32 = jnp.float32
BF16 = jnp.bfloat16
Y_SIZE, Z_SIZE = 4, 8
Y_STEPS = (8, 16, 24)
X_STEPS = (2, 4, 6)
Z_SUM_STEPS = (1, 3, 7)
Z_PAIRS = (2, 5, 6)
Z_ORDER = tuple(pair ^ bit for pair in (0,) + Z_PAIRS for bit in (0, 1))
ROW_BLOCKS = 4


def exact(left, right, left_dim, right_dim):
    return lax.dot_general(
        left,
        right,
        (((left_dim,), (right_dim,)), ((), ())),
        precision=HIGHEST,
        preferred_element_type=F32,
    )


def native(left, right, left_dim, right_dim):
    return lax.dot_general(
        left, right, (((left_dim,), (right_dim,)), ((), ())), preferred_element_type=F32
    )


def three_parts(value):
    high = value.astype(BF16)
    rest = value - high.astype(F32)
    middle = rest.astype(BF16)
    return high, middle, (rest - middle.astype(F32)).astype(BF16)


def exchange(value, axis, distance):
    return lax.ppermute(value, axis, [(i, i ^ distance) for i in range(lax.axis_size(axis))])


def sum_four(terms):
    return (terms[0] + terms[1]) + (terms[2] + terms[3])


def call(kernel, outs, args, cost, name, aliases=None, out_specs=None, spare=(), scratch=()):
    specs = [pl.BlockSpec(memory_space=pltpu.VMEM)] * len(args)
    specs += [pl.BlockSpec(memory_space=pl.ANY)] * len(spare)
    flops, traffic = cost
    return pl.pallas_call(
        kernel,
        out_shape=outs,
        in_specs=specs,
        out_specs=out_specs or [pl.BlockSpec(memory_space=pltpu.VMEM)] * len(outs),
        scratch_shapes=scratch,
        input_output_aliases=aliases or {},
        compiler_params=pltpu.CompilerParams(vmem_limit_bytes=16 * 2**20),
        cost_estimate=pl.CostEstimate(flops=flops, bytes_accessed=traffic, transcendentals=0),
        name=name,
    )(*[pltpu.with_memory_space_constraint(v, pltpu.VMEM) for v in args], *spare)


def factor_kernel(warm_far, grad_far, feed_far, *refs):
    states_far, outs = refs[:3], refs[3 : 3 + Y_SIZE]
    grad_ref, feed_ref, state_ref, warm_ref, parts_ref, total_ref, sems = refs[3 + Y_SIZE :]
    rank, rows = warm_ref.shape
    quarter = outs[0].shape[1]
    size = rows // ROW_BLOCKS
    warm_copy = pltpu.make_async_copy(warm_far, warm_ref, sems.at[2 * ROW_BLOCKS])
    warm_copy.start()
    copies = []
    for i in range(ROW_BLOCKS):
        at = pl.ds(i * size, size)
        for k, (far, ref) in enumerate([(grad_far, grad_ref), (feed_far, feed_ref)]):
            copies.append(pltpu.make_async_copy(far.at[at], ref.at[at], sems.at[2 * i + k]))
            copies[-1].start()
    states = []
    for i, far in enumerate(states_far):
        sem = sems.at[2 * ROW_BLOCKS + 1 + i]
        states.append(pltpu.make_async_copy(far, state_ref.at[i], sem))
        states[-1].start()
    warm_copy.wait()
    for i, part in enumerate(three_parts(warm_ref[...])):
        parts_ref[i * rank : (i + 1) * rank, :] = part
    total = None
    for i in range(ROW_BLOCKS):
        at = slice(i * size, (i + 1) * size)
        copies[2 * i].wait()
        copies[2 * i + 1].wait()
        parts = parts_ref[:, at]
        term = native(parts, grad_ref[at, :], 1, 0) + native(parts, feed_ref[at, :], 1, 0)
        total = term if total is None else total + term
    total_ref[...] = (total[2 * rank :] + total[rank : 2 * rank]) + total[:rank]
    own = lax.axis_index("rep") // Z_SIZE
    for d, out in enumerate(outs):
        out[...] = total_ref[:, pl.ds(pl.multiple_of((own ^ d) * quarter, quarter), quarter)]
    for copy in states:
        copy.wait()


def local_factor(warm_t, gradient, feedback, states):
    rank, rows = warm_t.shape
    columns = gradient.shape[1]
    near = pltpu.VMEM((rows, columns), BF16)
    far = (warm_t, gradient, feedback, *states)
    args = [pltpu.with_memory_space_constraint(v, pltpu.HBM) for v in far]
    outs = pl.pallas_call(
        factor_kernel,
        out_shape=[pltpu.VMEM((rank, columns // Y_SIZE), F32)] * Y_SIZE
        + [near, near, pltpu.VMEM((3, *states[0].shape), F32)],
        in_specs=[pl.BlockSpec(memory_space=pl.ANY)] * 6,
        out_specs=[pl.BlockSpec(memory_space=pltpu.VMEM)] * (Y_SIZE + 3),
        scratch_shapes=[
            pltpu.VMEM((rank, rows), F32),
            pltpu.VMEM((3 * rank, rows), BF16),
            pltpu.VMEM((rank, columns), F32),
            pltpu.SemaphoreType.DMA((2 * ROW_BLOCKS + 4,)),
        ],
        compiler_params=pltpu.CompilerParams(vmem_limit_bytes=16 * 2**20),
        cost_estimate=pl.CostEstimate(flops=10**9, bytes_accessed=2_500_000, transcendentals=0),
        name="local_factor",
    )(*args)
    return outs[:Y_SIZE], *outs[Y_SIZE:]


def assemble_kernel(*refs):
    quarters, (factor_ref, parts_ref, gram_ref) = refs[:Y_SIZE], refs[Y_SIZE:]
    rank, quarter = quarters[0].shape
    own = lax.axis_index("rep") // Z_SIZE
    for d, block in enumerate(quarters):
        at = pl.ds(pl.multiple_of((own ^ d) * quarter, quarter), quarter)
        factor_ref[:, at] = block[...]
    factor = factor_ref[...]
    for i, part in enumerate(three_parts(factor)):
        parts_ref[i * rank : (i + 1) * rank, :] = part
    gram_ref[...] = exact(factor, factor, 1, 1)


def assemble(quarters):
    rank, quarter = quarters[0].shape
    columns = quarter * Y_SIZE
    outs = [
        pltpu.VMEM((rank, columns), F32),
        pltpu.VMEM((3 * rank, columns), BF16),
        pltpu.VMEM((rank, rank), F32),
    ]
    return call(assemble_kernel, outs, tuple(quarters), (10**8, 500_000), "assemble_factor")


def project_kernel(which, grad_ref, feed_ref, parts_ref, out_ref):
    replicas, quarter, _ = out_ref.shape
    own_rows = grad_ref.shape[0] // replicas
    rank = parts_ref.shape[0] // 3
    parts = parts_ref[...]
    groups = replicas // 2
    first = (lax.axis_index("shard") % 2 ^ which) * (2 * quarter)

    def rows_of(ref, i):
        pieces = []
        for r in range(i * groups, (i + 1) * groups):
            at = pl.multiple_of(r * own_rows + first, 2 * quarter)
            pieces.append(ref[pl.ds(at, 2 * quarter), :])
        return jnp.concatenate(pieces, axis=0)

    for i in range(2):
        total = native(rows_of(grad_ref, i), parts, 1, 1)
        total = total + native(rows_of(feed_ref, i), parts, 1, 1)
        value = (total[:, 2 * rank :] + total[:, rank : 2 * rank]) + total[:, :rank]
        value = value.reshape(groups, 2, quarter, rank)
        out_ref[i * groups : (i + 1) * groups] = jnp.concatenate([value[:, 0], value[:, 1]], axis=-1)


def project(which, gradient, feedback, parts, replicas):
    rank = parts.shape[0] // 3
    quarter = gradient.shape[0] // replicas // 4
    return call(
        lambda *refs: project_kernel(which, *refs),
        [pltpu.VMEM((replicas, quarter, 2 * rank), F32)],
        (gradient, feedback, parts),
        (5 * 10**8, 1_300_000),
        "project_send" if which else "project_keep",
    )[0]


def pair_kernel(keep_ref, other_ref, out_ref):
    for r in range(keep_ref.shape[0]):
        total = keep_ref[r] + other_ref[r]
        out_ref[r, 0] = total
        out_ref[r ^ 1, 1] = total


def pair_up(keep, other):
    replicas, quarter, lanes = keep.shape
    outs = [jax.ShapeDtypeStruct((replicas, 2, quarter, lanes), F32)]
    return call(pair_kernel, outs, (keep, other), (10**6, 500_000), "pair_up")[0]


def inverse_kernel(gram_ref, factor_ref, inverse_ref, unit_ref, parts_ref):
    rank = gram_ref.shape[0]
    width = 8
    row = lax.broadcasted_iota(jnp.int32, (rank, rank), 0)
    column = lax.broadcasted_iota(jnp.int32, (rank, rank), 1)
    diagonal = row == column
    gram = gram_ref[...]
    trace = jnp.sum(jnp.where(diagonal, gram, 0.0))
    gram = gram + jnp.where(diagonal, ridge_rate * trace / rank, 0.0)
    table = jnp.concatenate([gram, jnp.where(diagonal, 1.0, 0.0)], axis=1)
    row = lax.broadcasted_iota(jnp.int32, table.shape, 0)
    pivots = jnp.ones(table.shape, F32)
    for k in range(0, rank, width):
        ahead = [jnp.broadcast_to(table[:, c : c + 1], table.shape) for c in range(k, k + width)]
        lines = [table[c : c + 1, :] for c in range(k, k + width)]
        for i in range(width):
            at = k + i
            pivot = ahead[i][at : at + 1, :]
            pivots = jnp.where(row == at, pivot, pivots)
            scale = jnp.where(row > at, ahead[i] * (1.0 / pivot), 0.0)
            for j in range(i + 1, width):
                entry = ahead[j][at : at + 1, :]
                ahead[j] = ahead[j] - scale * entry
                lines[j] = lines[j] - scale[k + j : k + j + 1, :] * lines[i]
            table = table - scale * lines[i]
    inverse = table[:, rank:] / jnp.sqrt(pivots[:, rank:])
    inverse_ref[...] = inverse
    unit = exact(inverse, factor_ref[...], 1, 0)
    unit_ref[...] = unit
    for i, part in enumerate(three_parts(unit)):
        parts_ref[2 * i * rank : (2 * i + 1) * rank, :] = part
        parts_ref[(2 * i + 1) * rank : (2 * i + 2) * rank, :] = part


def invert(gram, factor_t):
    rank, columns = factor_t.shape
    outs = [
        pltpu.VMEM((rank, rank), F32),
        pltpu.VMEM((rank, columns), F32),
        pltpu.VMEM((6 * rank, columns), BF16),
    ]
    return call(inverse_kernel, outs, (gram, factor_t), (2 * 10**9, 500_000), "invert")


def update_kernel(replicas, half_ref, other_ref, inverse_ref, unit_ref, state_ref, neighbour_ref,
                  send_ref, master_out, moment_out, second_out):
    rank = inverse_ref.shape[0]
    columns = unit_ref.shape[1]
    first_core = lax.axis_index("shard") % 2 == 0
    low = jnp.where(first_core, half_ref[...], other_ref[...])
    high = jnp.where(first_core, other_ref[...], half_ref[...])
    pieces = []
    for k in range(2):
        for half in (low[k], high[k]):
            pieces += [half[:, :rank], half[:, rank:]]
    sums = jnp.concatenate(pieces, axis=0)
    rights = exact(sums, inverse_ref[...], 1, 1) / replicas
    grads = exact(rights, unit_ref[...], 1, 0)
    own_rows = sums.shape[0] // 2
    for k, ref in enumerate([state_ref, neighbour_ref]):
        at = slice(k * own_rows, (k + 1) * own_rows)
        right, grad = rights[at], grads[at]
        master, moment, second = ref[0], ref[1], ref[2]
        moment = beta_one * moment + (1.0 - beta_one) * grad
        second = beta_two * second + (1.0 - beta_two) * grad * grad
        master = master - learn_rate * (
            moment / (jnp.sqrt(second) + adam_eps) + decay_rate * master
        )
        if k == 0:
            master_out[...] = master
            moment_out[...] = moment
            second_out[...] = second
        upper = right.astype(BF16).astype(F32)
        send_ref[k, :, :columns] = master.astype(BF16)
        send_ref[k, :, columns:] = jnp.concatenate([upper, right - upper], axis=1).astype(BF16)


def update(replicas, half_sum, other_sum, inverse, unit_t, state, neighbour):
    _, rows, columns = state.shape
    rank = inverse.shape[0]
    block = pltpu.VMEM((rows, columns), F32)
    outs = [pltpu.VMEM((2, rows, columns + 2 * rank), BF16), block, block, block]
    args = (half_sum, other_sum, inverse, unit_t, state, neighbour)
    kernel = lambda *refs: update_kernel(replicas, *refs)
    return call(kernel, outs, args, (10**8, 1_000_000), "update")


def finish_kernel(begins, ds, *refs):
    count = Y_SIZE if not begins else len(ds)
    blocks, (parts_ref, grad_ref, feed_ref) = refs[:count], refs[count : count + 3]
    rest = refs[count + 3 :] if begins else refs[count + 5 :]
    if begins:
        new_far, weights_far, new_near, sems = rest
    else:
        new_far, weights_far, right_far, new_near, right_near, sems = rest
    columns = grad_ref.shape[1]
    groups, own_rows, width = blocks[0].shape
    size = groups * own_rows
    rank = (width - columns) // 2
    own_y, own_z = lax.axis_index("rep") // Z_SIZE, lax.axis_index("rep") % Z_SIZE
    copies = []

    def send(source, target):
        copies.append(pltpu.make_async_copy(source, target, sems.at[len(copies)]))
        copies[-1].start()

    def piece_of(z):
        step = own_z ^ z
        return step ^ ((step >> 2) & (1 - ((step >> 1) & 1)))

    def rights_of(block):
        return jnp.concatenate([block[piece_of(z), :, columns:] for z in range(groups)], axis=0)

    def rows_of(d):
        return pl.ds(pl.multiple_of((own_y ^ d) * size, size), size)

    for d in ds:
        for j in range(groups):
            at = (own_y ^ d) * size + (own_z ^ Z_ORDER[j]) * own_rows
            target = weights_far.at[pl.ds(pl.multiple_of(at, own_rows), own_rows)]
            send(blocks[d].at[j, :, pl.ds(0, columns)], target)
    if not begins:
        row = lax.broadcasted_iota(jnp.int32, (rank, 2 * rank), 0)
        column = lax.broadcasted_iota(jnp.int32, (rank, 2 * rank), 1)
        both = jnp.where((row == column) | (row + rank == column), 1.0, 0.0).astype(BF16)
        for d, block in enumerate(blocks):
            right_near[:, rows_of(d)] = native(both, rights_of(block), 1, 1)
        send(right_near, right_far)
    for i, d in enumerate(ds):
        right = rights_of(blocks[d])
        approx = native(jnp.concatenate([right] * 3, axis=1), parts_ref[...], 1, 0)
        merged = grad_ref[rows_of(d), :].astype(F32) + feed_ref[rows_of(d), :].astype(F32)
        new_near[i] = (merged - approx).astype(BF16)
        send(new_near.at[i], new_far.at[rows_of(d)])
    for copy in copies:
        copy.wait()


def finish(begins, ds, blocks, parts, gradient, feedback, begun=()):
    rows, columns = gradient.shape
    groups, own_rows, width = blocks[0].shape
    rank = (width - columns) // 2
    far = pl.BlockSpec(memory_space=pl.ANY)
    outs = [jax.ShapeDtypeStruct((rows, columns), BF16)] * 2
    out_specs = [far, far]
    scratch = [pltpu.VMEM((len(ds), groups * own_rows, columns), BF16)]
    if not begins:
        outs = outs + [jax.ShapeDtypeStruct((rank, rows), F32)]
        out_specs = out_specs + [far]
        scratch = scratch + [pltpu.VMEM((rank, rows), F32)]
    return call(
        lambda *refs: finish_kernel(begins, ds, *refs),
        outs,
        (*blocks, parts, gradient, feedback),
        (len(ds) * 3 * 10**8, len(ds) * 1_500_000),
        "finish_own" if begins else "finish_rest",
        aliases={} if begins else {Y_SIZE + 3: 0, Y_SIZE + 4: 1},
        out_specs=out_specs,
        spare=begun,
        scratch=scratch + [pltpu.SemaphoreType.DMA((len(ds) * (groups + 1) + 1,))],
    )


def on_device(gradient, feedback, warm_start, master, moment, second):
    replicas = lax.axis_size("rep")

    pieces, gradient, feedback, state = local_factor(
        warm_start.T, gradient[0], feedback[0], (master, moment, second)
    )
    quarter = sum_four([pieces[0]] + [exchange(p, "rep", d) for p, d in zip(pieces[1:], Y_STEPS)])
    for distance in Z_SUM_STEPS:
        quarter = quarter + exchange(quarter, "rep", distance)
    quarter = quarter / replicas
    quarter, state = lax.optimization_barrier((quarter, state))
    quarters = [quarter] + [exchange(quarter, "rep", d) for d in Y_STEPS]
    neighbour = exchange(state, "rep", 1)
    factor_t, parts, gram_term = assemble(quarters)

    gram_pair = gram_term + exchange(gram_term, "shard", 1)
    other_half = exchange(project(1, gradient, feedback, parts, replicas), "shard", 1)
    packed = pair_up(project(0, gradient, feedback, parts, replicas), other_half)
    gram_pair, packed = lax.optimization_barrier((gram_pair, packed))
    received = lax.all_to_all(packed, "rep", 0, 0, tiled=True)
    gram = sum_four([gram_pair] + [exchange(gram_pair, "shard", d) for d in X_STEPS])
    inverse, unit_t, unit_parts = invert(gram, factor_t)
    received, inverse, unit_t, unit_parts, neighbour = lax.optimization_barrier(
        (received, inverse, unit_t, unit_parts, neighbour)
    )
    half_sum = received.sum(0)
    half_sum = sum_four([half_sum] + [exchange(half_sum, "shard", d) for d in X_STEPS])

    pair, master_out, moment_out, second_out = update(
        replicas, half_sum, exchange(half_sum, "shard", 1), inverse, unit_t, state, neighbour
    )
    column = jnp.concatenate([pair] + [exchange(pair, "rep", d) for d in Z_PAIRS])
    others = [exchange(column, "rep", d) for d in Y_STEPS]
    begun = finish(True, (0,), [column], unit_parts, gradient, feedback)
    blocks = [column] + others
    new_feedback, weights, right_t = finish(
        False, (1, 2, 3), blocks, unit_parts, gradient, feedback, begun
    )
    return (new_feedback[None], weights, master_out, moment_out, second_out, right_t.T)


def solution(mesh):
    return jax.shard_map(
        on_device,
        mesh=mesh,
        in_specs=(
            P("rep", None, "shard"),
            P("rep", None, "shard"),
            P(),
            P("rep", "shard"),
            P("rep", "shard"),
            P("rep", "shard"),
        ),
        out_specs=(
            P("rep", None, "shard"),
            P(None, "shard"),
            P("rep", "shard"),
            P("rep", "shard"),
            P("rep", "shard"),
            P(),
        ),
        check_vma=False,
    )
```

```python
import jax
import jax.numpy as jnp
from jax import lax
from jax.experimental import pallas as pl
from jax.experimental.pallas import tpu as pltpu
from jax.sharding import PartitionSpec as P

HIGHEST = lax.Precision.HIGHEST
beta_one = 0.9
beta_two = 0.95
learn_rate = 0.02
decay_rate = 0.1
adam_eps = 1e-08
ridge_rate = 1e-06

F32 = jnp.float32
BF16 = jnp.bfloat16
Y_SIZE, Z_SIZE = 4, 8
Y_STEPS = (8, 16, 24)
X_STEPS = (2, 4, 6)
Z_SUM_STEPS = (1, 3, 7)
Z_PAIRS = (2, 5, 6)
Y_ORDER, Z_ORDER = (0,) + Y_STEPS, (0,) + Z_PAIRS
ROW_BLOCKS = 4


def exact(left, right, left_dim, right_dim):
    return lax.dot_general(
        left,
        right,
        (((left_dim,), (right_dim,)), ((), ())),
        precision=HIGHEST,
        preferred_element_type=F32,
    )


def native(left, right, left_dim, right_dim):
    return lax.dot_general(
        left, right, (((left_dim,), (right_dim,)), ((), ())), preferred_element_type=F32
    )


def three_parts(value):
    high = value.astype(BF16)
    rest = value - high.astype(F32)
    middle = rest.astype(BF16)
    return high, middle, (rest - middle.astype(F32)).astype(BF16)


def exchange(value, axis, distance):
    return lax.ppermute(value, axis, [(i, i ^ distance) for i in range(lax.axis_size(axis))])


def exchange_by_core(value, first_distance, second_distance):
    cores = lax.axis_size("shard")
    pairs = []
    for i in range(lax.axis_size("rep")):
        for j in range(cores):
            other = i ^ (second_distance if j % 2 else first_distance)
            pairs.append((i * cores + j, other * cores + j))
    return lax.ppermute(value, ("rep", "shard"), pairs)


def sum_four(terms):
    return (terms[0] + terms[1]) + (terms[2] + terms[3])


def shard_sum(value):
    value = value + exchange(value, "shard", 1)
    return sum_four([value] + [exchange(value, "shard", d) for d in X_STEPS])


def call(kernel, outs, args, cost, name, aliases=None, out_specs=None, spare=(), scratch=()):
    specs = [pl.BlockSpec(memory_space=pltpu.VMEM)] * len(args)
    specs += [pl.BlockSpec(memory_space=pl.ANY)] * len(spare)
    flops, traffic = cost
    return pl.pallas_call(
        kernel,
        out_shape=outs,
        in_specs=specs,
        out_specs=out_specs or [pl.BlockSpec(memory_space=pltpu.VMEM)] * len(outs),
        scratch_shapes=scratch,
        input_output_aliases=aliases or {},
        compiler_params=pltpu.CompilerParams(vmem_limit_bytes=16 * 2**20),
        cost_estimate=pl.CostEstimate(flops=flops, bytes_accessed=traffic, transcendentals=0),
        name=name,
    )(*[pltpu.with_memory_space_constraint(v, pltpu.VMEM) for v in args], *spare)


def factor_kernel(warm_far, grad_far, feed_far, *refs):
    outs, (grad_ref, feed_ref, warm_ref, parts_ref, total_ref, sems) = refs[:Y_SIZE], refs[Y_SIZE:]
    rank, rows = warm_ref.shape
    quarter = outs[0].shape[1]
    size = rows // ROW_BLOCKS
    warm_copy = pltpu.make_async_copy(warm_far, warm_ref, sems.at[2 * ROW_BLOCKS])
    warm_copy.start()
    copies = []
    for i in range(ROW_BLOCKS):
        at = pl.ds(i * size, size)
        for k, (far, ref) in enumerate([(grad_far, grad_ref), (feed_far, feed_ref)]):
            copies.append(pltpu.make_async_copy(far.at[at], ref.at[at], sems.at[2 * i + k]))
            copies[-1].start()
    warm_copy.wait()
    for i, part in enumerate(three_parts(warm_ref[...])):
        parts_ref[i * rank : (i + 1) * rank, :] = part
    total = None
    for i in range(ROW_BLOCKS):
        at = slice(i * size, (i + 1) * size)
        copies[2 * i].wait()
        copies[2 * i + 1].wait()
        parts = parts_ref[:, at]
        term = native(parts, grad_ref[at, :], 1, 0) + native(parts, feed_ref[at, :], 1, 0)
        total = term if total is None else total + term
    total_ref[...] = (total[2 * rank :] + total[rank : 2 * rank]) + total[:rank]
    own = lax.axis_index("rep") // Z_SIZE
    for d, out in enumerate(outs):
        out[...] = total_ref[:, pl.ds(pl.multiple_of((own ^ d) * quarter, quarter), quarter)]


def local_factor(warm_t, gradient, feedback):
    rank, rows = warm_t.shape
    columns = gradient.shape[1]
    near = pltpu.VMEM((rows, columns), BF16)
    args = [pltpu.with_memory_space_constraint(v, pltpu.HBM) for v in (warm_t, gradient, feedback)]
    outs = pl.pallas_call(
        factor_kernel,
        out_shape=[pltpu.VMEM((rank, columns // Y_SIZE), F32)] * Y_SIZE + [near] * 2,
        in_specs=[pl.BlockSpec(memory_space=pl.ANY)] * 3,
        out_specs=[pl.BlockSpec(memory_space=pltpu.VMEM)] * (Y_SIZE + 2),
        scratch_shapes=[
            pltpu.VMEM((rank, rows), F32),
            pltpu.VMEM((3 * rank, rows), BF16),
            pltpu.VMEM((rank, columns), F32),
            pltpu.SemaphoreType.DMA((2 * ROW_BLOCKS + 1,)),
        ],
        compiler_params=pltpu.CompilerParams(vmem_limit_bytes=16 * 2**20),
        cost_estimate=pl.CostEstimate(flops=10**9, bytes_accessed=2_500_000, transcendentals=0),
        name="local_factor",
    )(*args)
    return outs[:Y_SIZE], outs[Y_SIZE], outs[Y_SIZE + 1]


def assemble_kernel(*refs):
    quarters, (factor_ref, parts_ref, gram_ref) = refs[:Y_SIZE], refs[Y_SIZE:]
    rank, quarter = quarters[0].shape
    own = lax.axis_index("rep") // Z_SIZE
    for d, block in enumerate(quarters):
        at = pl.ds(pl.multiple_of((own ^ d) * quarter, quarter), quarter)
        factor_ref[:, at] = block[...]
    factor = factor_ref[...]
    for i, part in enumerate(three_parts(factor)):
        parts_ref[i * rank : (i + 1) * rank, :] = part
    gram_ref[...] = exact(factor, factor, 1, 1)


def assemble(quarters):
    rank, quarter = quarters[0].shape
    columns = quarter * Y_SIZE
    outs = [
        pltpu.VMEM((rank, columns), F32),
        pltpu.VMEM((3 * rank, columns), BF16),
        pltpu.VMEM((rank, rank), F32),
    ]
    return call(assemble_kernel, outs, tuple(quarters), (10**8, 500_000), "assemble_factor")


def project_kernel(grad_ref, feed_ref, parts_ref, out_ref):
    replicas, half, _ = out_ref.shape
    rows = grad_ref.shape[0]
    rank = parts_ref.shape[0] // 3
    parts = parts_ref[...]
    groups = 8
    size = rows // replicas * groups

    for i in range(replicas // groups):
        at = slice(i * size, (i + 1) * size)
        total = native(grad_ref[at, :], parts, 1, 1) + native(feed_ref[at, :], parts, 1, 1)
        value = (total[:, 2 * rank :] + total[:, rank : 2 * rank]) + total[:, :rank]
        value = value.reshape(groups, 2, half, rank)
        out_ref[i * groups : (i + 1) * groups] = jnp.concatenate([value[:, 0], value[:, 1]], axis=-1)


def project(gradient, feedback, parts, replicas):
    rank = parts.shape[0] // 3
    half = gradient.shape[0] // replicas // 2
    outs = [pltpu.VMEM((replicas, half, 2 * rank), F32)]
    return call(
        project_kernel, outs, (gradient, feedback, parts), (10**9, 2_500_000), "project"
    )[0]


def inverse_kernel(gram_ref, factor_ref, inverse_ref, unit_ref, parts_ref):
    rank = gram_ref.shape[0]
    width = 8
    row = lax.broadcasted_iota(jnp.int32, (rank, rank), 0)
    column = lax.broadcasted_iota(jnp.int32, (rank, rank), 1)
    diagonal = row == column
    gram = gram_ref[...]
    trace = jnp.sum(jnp.where(diagonal, gram, 0.0))
    gram = gram + jnp.where(diagonal, ridge_rate * trace / rank, 0.0)
    table = jnp.concatenate([gram, jnp.where(diagonal, 1.0, 0.0)], axis=1)
    row = lax.broadcasted_iota(jnp.int32, table.shape, 0)
    pivots = jnp.ones(table.shape, F32)
    for k in range(0, rank, width):
        ahead = [jnp.broadcast_to(table[:, c : c + 1], table.shape) for c in range(k, k + width)]
        lines = [table[c : c + 1, :] for c in range(k, k + width)]
        for i in range(width):
            at = k + i
            pivot = ahead[i][at : at + 1, :]
            pivots = jnp.where(row == at, pivot, pivots)
            scale = jnp.where(row > at, ahead[i] * (1.0 / pivot), 0.0)
            for j in range(i + 1, width):
                entry = ahead[j][at : at + 1, :]
                ahead[j] = ahead[j] - scale * entry
                lines[j] = lines[j] - scale[k + j : k + j + 1, :] * lines[i]
            table = table - scale * lines[i]
    inverse = table[:, rank:] / jnp.sqrt(pivots[:, rank:])
    inverse_ref[...] = inverse
    unit = exact(inverse, factor_ref[...], 1, 0)
    unit_ref[...] = unit
    for i, part in enumerate(three_parts(unit)):
        parts_ref[2 * i * rank : (2 * i + 1) * rank, :] = part
        parts_ref[(2 * i + 1) * rank : (2 * i + 2) * rank, :] = part


def invert(gram, factor_t):
    rank, columns = factor_t.shape
    outs = [
        pltpu.VMEM((rank, rank), F32),
        pltpu.VMEM((rank, columns), F32),
        pltpu.VMEM((6 * rank, columns), BF16),
    ]
    return call(inverse_kernel, outs, (gram, factor_t), (2 * 10**9, 500_000), "invert")


def update_kernel(replicas, sum_ref, inverse_ref, unit_ref, master_ref, moment_ref,
                  second_ref, send_ref, master_out, moment_out, second_out):
    rank = inverse_ref.shape[0]
    columns = master_ref.shape[1]
    packed = sum_ref[...]
    own = jnp.concatenate([packed[:, :rank], packed[:, rank:]], axis=0)
    right = exact(own, inverse_ref[...], 1, 1) / replicas
    grad = exact(right, unit_ref[...], 1, 0)
    moment = beta_one * moment_ref[...] + (1.0 - beta_one) * grad
    second = beta_two * second_ref[...] + (1.0 - beta_two) * grad * grad
    master = master_ref[...]
    master = master - learn_rate * (
        moment / (jnp.sqrt(second) + adam_eps) + decay_rate * master
    )
    moment_out[...] = moment
    second_out[...] = second
    master_out[...] = master
    high = right.astype(BF16).astype(F32)
    send_ref[:, :columns] = master.astype(BF16)
    send_ref[:, columns:] = jnp.concatenate([high, right - high], axis=1).astype(BF16)


def update(replicas, own_sum, inverse, unit_t, master, moment, second):
    rows, columns = master.shape
    rank = inverse.shape[0]
    block = pltpu.VMEM(master.shape, F32)
    outs = [pltpu.VMEM((rows, columns + 2 * rank), BF16), block, block, block]
    args = (own_sum, inverse, unit_t, master, moment, second)
    kernel = lambda *refs: update_kernel(replicas, *refs)
    return call(kernel, outs, args, (5 * 10**7, 600_000), "update")


def finish_kernel(begins, ds, *refs):
    count = Y_SIZE if not begins else len(ds)
    blocks, (parts_ref, grad_ref, feed_ref) = refs[:count], refs[count : count + 3]
    rest = refs[count + 3 :] if begins else refs[count + 5 :]
    if begins:
        new_far, weights_far, new_near, sems = rest
    else:
        new_far, weights_far, right_far, new_near, right_near, rights, sems = rest
    columns = grad_ref.shape[1]
    groups, own_rows, width = blocks[0].shape
    rank = (width - columns) // 2
    own = lax.axis_index("rep")
    core = lax.axis_index("shard") % 2
    copies = []

    def send(source, target):
        copies.append(pltpu.make_async_copy(source, target, sems.at[len(copies)]))
        copies[-1].start()

    def replica(d, k):
        first, second = Y_ORDER[d] ^ Z_ORDER[k], Y_ORDER[k] ^ Z_ORDER[d]
        return own ^ (first + core * (second - first))

    def rows_of(d, j):
        at = (replica(d, j // 2) ^ (j % 2)) * own_rows
        return pl.ds(pl.multiple_of(at, own_rows), own_rows)

    for d in ds:
        for j in range(groups):
            send(blocks[d].at[j, :, pl.ds(0, columns)], weights_far.at[rows_of(d, j)])
    if not begins:
        for d, block in enumerate(blocks):
            for j in range(groups):
                rights[rows_of(d, j), :] = block[j, :, columns:]
        row = lax.broadcasted_iota(jnp.int32, (rank, 2 * rank), 0)
        column = lax.broadcasted_iota(jnp.int32, (rank, 2 * rank), 1)
        both = jnp.where((row == column) | (row + rank == column), 1.0, 0.0).astype(BF16)
        right_near[...] = native(both, rights[...], 1, 1)
        send(right_near, right_far)
    for i, d in enumerate(ds):
        right = blocks[d][:, :, columns:].reshape(groups * own_rows, width - columns)
        approx = native(jnp.concatenate([right] * 3, axis=1), parts_ref[...], 1, 0)
        for k in range(groups // 2):
            for j in (2 * k, 2 * k + 1):
                rows = rows_of(d, j)
                merged = grad_ref[rows, :].astype(F32) + feed_ref[rows, :].astype(F32)
                piece = (merged - approx[j * own_rows : (j + 1) * own_rows]).astype(BF16)
                place = k * 2 * own_rows + ((replica(d, k) ^ j) % 2) * own_rows
                new_near[i, pl.ds(pl.multiple_of(place, own_rows), own_rows), :] = piece
            near = pl.ds(k * 2 * own_rows, 2 * own_rows)
            at = (replica(d, k) // 2) * (2 * own_rows)
            far = pl.ds(pl.multiple_of(at, 2 * own_rows), 2 * own_rows)
            send(new_near.at[i, near], new_far.at[far])
    for copy in copies:
        copy.wait()


def finish(begins, ds, blocks, parts, gradient, feedback, begun=()):
    rows, columns = gradient.shape
    groups, own_rows, width = blocks[0].shape
    rank = (width - columns) // 2
    far = pl.BlockSpec(memory_space=pl.ANY)
    outs = [jax.ShapeDtypeStruct((rows, columns), BF16)] * 2
    out_specs = [far, far]
    scratch = [pltpu.VMEM((len(ds), groups * own_rows, columns), BF16)]
    if not begins:
        outs = outs + [jax.ShapeDtypeStruct((rank, rows), F32)]
        out_specs = out_specs + [far]
        scratch = scratch + [pltpu.VMEM((rank, rows), F32), pltpu.VMEM((rows, 2 * rank), BF16)]
    return call(
        lambda *refs: finish_kernel(begins, ds, *refs),
        outs,
        (*blocks, parts, gradient, feedback),
        (len(ds) * 3 * 10**8, len(ds) * 1_500_000),
        "finish_own" if begins else "finish_rest",
        aliases={} if begins else {Y_SIZE + 3: 0, Y_SIZE + 4: 1},
        out_specs=out_specs,
        spare=begun,
        scratch=scratch + [pltpu.SemaphoreType.DMA((len(ds) * (groups + groups // 2) + 1,))],
    )


def on_device(gradient, feedback, warm_start, master, moment, second):
    replicas = lax.axis_size("rep")
    gradient, feedback = gradient[0], feedback[0]

    pieces, gradient, feedback = local_factor(warm_start.T, gradient, feedback)
    quarter = sum_four([pieces[0]] + [exchange(p, "rep", d) for p, d in zip(pieces[1:], Y_STEPS)])
    for distance in Z_SUM_STEPS:
        quarter = quarter + exchange(quarter, "rep", distance)
    quarter = quarter / replicas
    quarters = [quarter] + [exchange(quarter, "rep", d) for d in Y_STEPS]
    factor_t, parts, gram_term = assemble(quarters)

    gram_pair = gram_term + exchange(gram_term, "shard", 1)
    packed = project(gradient, feedback, parts, replicas)
    gram_pair, packed = lax.optimization_barrier((gram_pair, packed))
    received = lax.all_to_all(packed, "rep", 0, 0, tiled=True)
    gram = sum_four([gram_pair] + [exchange(gram_pair, "shard", d) for d in X_STEPS])
    inverse, unit_t, unit_parts = invert(gram, factor_t)
    received, inverse, unit_t, unit_parts = lax.optimization_barrier(
        (received, inverse, unit_t, unit_parts)
    )
    own_sum = shard_sum(received.sum(0))

    send, master_out, moment_out, second_out = update(
        replicas, own_sum, inverse, unit_t, master, moment, second
    )
    pair = jnp.stack([send, exchange(send, "rep", 1)])
    column = jnp.concatenate(
        [pair] + [exchange_by_core(pair, z, y) for y, z in zip(Y_STEPS, Z_PAIRS)]
    )
    others = [exchange_by_core(column, y, z) for y, z in zip(Y_STEPS, Z_PAIRS)]
    begun = finish(True, (0,), [column], unit_parts, gradient, feedback)
    blocks = [column] + others
    new_feedback, weights, right_t = finish(
        False, (1, 2, 3), blocks, unit_parts, gradient, feedback, begun
    )
    return (new_feedback[None], weights, master_out, moment_out, second_out, right_t.T)


def solution(mesh):
    return jax.shard_map(
        on_device,
        mesh=mesh,
        in_specs=(
            P("rep", None, "shard"),
            P("rep", None, "shard"),
            P(),
            P("rep", "shard"),
            P("rep", "shard"),
            P("rep", "shard"),
        ),
        out_specs=(
            P("rep", None, "shard"),
            P(None, "shard"),
            P("rep", "shard"),
            P("rep", "shard"),
            P("rep", "shard"),
            P(),
        ),
        check_vma=False,
    )
```

```python
import jax
import jax.numpy as jnp
from jax import lax
from jax.experimental import pallas as pl
from jax.experimental.pallas import tpu as pltpu
from jax.sharding import PartitionSpec as P

HIGHEST = lax.Precision.HIGHEST
beta_one = 0.9
beta_two = 0.95
learn_rate = 0.02
decay_rate = 0.1
adam_eps = 1e-08
ridge_rate = 1e-06

F32 = jnp.float32
BF16 = jnp.bfloat16
Y_SIZE, Z_SIZE = 4, 8
Y_STEPS = (8, 16, 24)
X_STEPS = (2, 4, 6)
Z_SUM_STEPS = (1, 3, 7)
Z_PAIRS = (2, 5, 6)
Z_ORDER = tuple(pair ^ bit for pair in (0,) + Z_PAIRS for bit in (0, 1))
LAST_STEPS = (0, 1, 3, 2)
ROW_BLOCKS = 4


def exact(left, right, left_dim, right_dim):
    return lax.dot_general(
        left,
        right,
        (((left_dim,), (right_dim,)), ((), ())),
        precision=HIGHEST,
        preferred_element_type=F32,
    )


def native(left, right, left_dim, right_dim):
    return lax.dot_general(
        left, right, (((left_dim,), (right_dim,)), ((), ())), preferred_element_type=F32
    )


def three_parts(value):
    high = value.astype(BF16)
    rest = value - high.astype(F32)
    middle = rest.astype(BF16)
    return high, middle, (rest - middle.astype(F32)).astype(BF16)


def exchange(value, axis, distance):
    return lax.ppermute(value, axis, [(i, i ^ distance) for i in range(lax.axis_size(axis))])


def sum_four(terms):
    return (terms[0] + terms[1]) + (terms[2] + terms[3])


def shard_sum(value):
    value = value + exchange(value, "shard", 1)
    return sum_four([value] + [exchange(value, "shard", d) for d in X_STEPS])


def call(kernel, outs, args, cost, name, aliases=None, out_specs=None, spare=(), scratch=()):
    specs = [pl.BlockSpec(memory_space=pltpu.VMEM)] * len(args)
    specs += [pl.BlockSpec(memory_space=pl.ANY)] * len(spare)
    flops, traffic = cost
    return pl.pallas_call(
        kernel,
        out_shape=outs,
        in_specs=specs,
        out_specs=out_specs or [pl.BlockSpec(memory_space=pltpu.VMEM)] * len(outs),
        scratch_shapes=scratch,
        input_output_aliases=aliases or {},
        compiler_params=pltpu.CompilerParams(vmem_limit_bytes=16 * 2**20),
        cost_estimate=pl.CostEstimate(flops=flops, bytes_accessed=traffic, transcendentals=0),
        name=name,
    )(*[pltpu.with_memory_space_constraint(v, pltpu.VMEM) for v in args], *spare)


def factor_kernel(warm_far, grad_far, feed_far, *refs):
    outs, (grad_ref, feed_ref, warm_ref, parts_ref, total_ref, sems) = refs[:Y_SIZE], refs[Y_SIZE:]
    rank, rows = warm_ref.shape
    quarter = outs[0].shape[1]
    size = rows // ROW_BLOCKS
    warm_copy = pltpu.make_async_copy(warm_far, warm_ref, sems.at[2 * ROW_BLOCKS])
    warm_copy.start()
    copies = []
    for i in range(ROW_BLOCKS):
        at = pl.ds(i * size, size)
        for k, (far, ref) in enumerate([(grad_far, grad_ref), (feed_far, feed_ref)]):
            copies.append(pltpu.make_async_copy(far.at[at], ref.at[at], sems.at[2 * i + k]))
            copies[-1].start()
    warm_copy.wait()
    for i, part in enumerate(three_parts(warm_ref[...])):
        parts_ref[i * rank : (i + 1) * rank, :] = part
    total = None
    for i in range(ROW_BLOCKS):
        at = slice(i * size, (i + 1) * size)
        copies[2 * i].wait()
        copies[2 * i + 1].wait()
        parts = parts_ref[:, at]
        term = native(parts, grad_ref[at, :], 1, 0) + native(parts, feed_ref[at, :], 1, 0)
        total = term if total is None else total + term
    total_ref[...] = (total[2 * rank :] + total[rank : 2 * rank]) + total[:rank]
    own = lax.axis_index("rep") // Z_SIZE
    for d, out in enumerate(outs):
        out[...] = total_ref[:, pl.ds(pl.multiple_of((own ^ d) * quarter, quarter), quarter)]


def local_factor(warm_t, gradient, feedback):
    rank, rows = warm_t.shape
    columns = gradient.shape[1]
    near = pltpu.VMEM((rows, columns), BF16)
    args = [pltpu.with_memory_space_constraint(v, pltpu.HBM) for v in (warm_t, gradient, feedback)]
    outs = pl.pallas_call(
        factor_kernel,
        out_shape=[pltpu.VMEM((rank, columns // Y_SIZE), F32)] * Y_SIZE + [near] * 2,
        in_specs=[pl.BlockSpec(memory_space=pl.ANY)] * 3,
        out_specs=[pl.BlockSpec(memory_space=pltpu.VMEM)] * (Y_SIZE + 2),
        scratch_shapes=[
            pltpu.VMEM((rank, rows), F32),
            pltpu.VMEM((3 * rank, rows), BF16),
            pltpu.VMEM((rank, columns), F32),
            pltpu.SemaphoreType.DMA((2 * ROW_BLOCKS + 1,)),
        ],
        compiler_params=pltpu.CompilerParams(vmem_limit_bytes=16 * 2**20),
        cost_estimate=pl.CostEstimate(flops=10**9, bytes_accessed=2_500_000, transcendentals=0),
        name="local_factor",
    )(*args)
    return outs[:Y_SIZE], outs[Y_SIZE], outs[Y_SIZE + 1]


def assemble_kernel(*refs):
    quarters, (factor_ref, parts_ref, gram_ref) = refs[:Y_SIZE], refs[Y_SIZE:]
    rank, quarter = quarters[0].shape
    own = lax.axis_index("rep") // Z_SIZE
    for d, block in enumerate(quarters):
        at = pl.ds(pl.multiple_of((own ^ d) * quarter, quarter), quarter)
        factor_ref[:, at] = block[...]
    factor = factor_ref[...]
    for i, part in enumerate(three_parts(factor)):
        parts_ref[i * rank : (i + 1) * rank, :] = part
    gram_ref[...] = exact(factor, factor, 1, 1)


def assemble(quarters):
    rank, quarter = quarters[0].shape
    columns = quarter * Y_SIZE
    outs = [
        pltpu.VMEM((rank, columns), F32),
        pltpu.VMEM((3 * rank, columns), BF16),
        pltpu.VMEM((rank, rank), F32),
    ]
    return call(assemble_kernel, outs, tuple(quarters), (10**8, 500_000), "assemble_factor")


def project_kernel(grad_ref, feed_ref, parts_ref, out_ref):
    replicas, half, _ = out_ref.shape
    rows = grad_ref.shape[0]
    rank = parts_ref.shape[0] // 3
    parts = parts_ref[...]
    groups = 8
    size = rows // replicas * groups

    for i in range(replicas // groups):
        at = slice(i * size, (i + 1) * size)
        total = native(grad_ref[at, :], parts, 1, 1) + native(feed_ref[at, :], parts, 1, 1)
        value = (total[:, 2 * rank :] + total[:, rank : 2 * rank]) + total[:, :rank]
        value = value.reshape(groups, 2, half, rank)
        out_ref[i * groups : (i + 1) * groups] = jnp.concatenate([value[:, 0], value[:, 1]], axis=-1)


def project(gradient, feedback, parts, replicas):
    rank = parts.shape[0] // 3
    half = gradient.shape[0] // replicas // 2
    outs = [pltpu.VMEM((replicas, half, 2 * rank), F32)]
    return call(
        project_kernel, outs, (gradient, feedback, parts), (10**9, 2_500_000), "project"
    )[0]


def inverse_kernel(gram_ref, factor_ref, inverse_ref, unit_ref, parts_ref):
    rank = gram_ref.shape[0]
    width = 8
    row = lax.broadcasted_iota(jnp.int32, (rank, rank), 0)
    column = lax.broadcasted_iota(jnp.int32, (rank, rank), 1)
    diagonal = row == column
    gram = gram_ref[...]
    trace = jnp.sum(jnp.where(diagonal, gram, 0.0))
    gram = gram + jnp.where(diagonal, ridge_rate * trace / rank, 0.0)
    table = jnp.concatenate([gram, jnp.where(diagonal, 1.0, 0.0)], axis=1)
    row = lax.broadcasted_iota(jnp.int32, table.shape, 0)
    pivots = jnp.ones(table.shape, F32)
    for k in range(0, rank, width):
        ahead = [jnp.broadcast_to(table[:, c : c + 1], table.shape) for c in range(k, k + width)]
        lines = [table[c : c + 1, :] for c in range(k, k + width)]
        for i in range(width):
            at = k + i
            pivot = ahead[i][at : at + 1, :]
            pivots = jnp.where(row == at, pivot, pivots)
            scale = jnp.where(row > at, ahead[i] * (1.0 / pivot), 0.0)
            for j in range(i + 1, width):
                entry = ahead[j][at : at + 1, :]
                ahead[j] = ahead[j] - scale * entry
                lines[j] = lines[j] - scale[k + j : k + j + 1, :] * lines[i]
            table = table - scale * lines[i]
    inverse = table[:, rank:] / jnp.sqrt(pivots[:, rank:])
    inverse_ref[...] = inverse
    unit = exact(inverse, factor_ref[...], 1, 0)
    unit_ref[...] = unit
    for i, part in enumerate(three_parts(unit)):
        parts_ref[2 * i * rank : (2 * i + 1) * rank, :] = part
        parts_ref[(2 * i + 1) * rank : (2 * i + 2) * rank, :] = part


def invert(gram, factor_t):
    rank, columns = factor_t.shape
    outs = [
        pltpu.VMEM((rank, rank), F32),
        pltpu.VMEM((rank, columns), F32),
        pltpu.VMEM((6 * rank, columns), BF16),
    ]
    return call(inverse_kernel, outs, (gram, factor_t), (2 * 10**9, 500_000), "invert")


def update_kernel(replicas, sum_ref, inverse_ref, unit_ref, master_ref, moment_ref,
                  second_ref, send_ref, master_out, moment_out, second_out):
    rank = inverse_ref.shape[0]
    columns = master_ref.shape[1]
    packed = sum_ref[...]
    own = jnp.concatenate([packed[:, :rank], packed[:, rank:]], axis=0)
    right = exact(own, inverse_ref[...], 1, 1) / replicas
    grad = exact(right, unit_ref[...], 1, 0)
    moment = beta_one * moment_ref[...] + (1.0 - beta_one) * grad
    second = beta_two * second_ref[...] + (1.0 - beta_two) * grad * grad
    master = master_ref[...]
    master = master - learn_rate * (
        moment / (jnp.sqrt(second) + adam_eps) + decay_rate * master
    )
    moment_out[...] = moment
    second_out[...] = second
    master_out[...] = master
    high = right.astype(BF16).astype(F32)
    send_ref[:, :columns] = master.astype(BF16)
    send_ref[:, columns:] = jnp.concatenate([high, right - high], axis=1).astype(BF16)


def update(replicas, own_sum, inverse, unit_t, master, moment, second):
    rows, columns = master.shape
    rank = inverse.shape[0]
    block = pltpu.VMEM(master.shape, F32)
    outs = [pltpu.VMEM((rows, columns + 2 * rank), BF16), block, block, block]
    args = (own_sum, inverse, unit_t, master, moment, second)
    kernel = lambda *refs: update_kernel(replicas, *refs)
    return call(kernel, outs, args, (5 * 10**7, 600_000), "update")


def finish_kernel(begins, ds, *refs):
    count = Y_SIZE if not begins else len(ds)
    blocks, (parts_ref, grad_ref, feed_ref) = refs[:count], refs[count : count + 3]
    rest = refs[count + 3 :] if begins else refs[count + 5 :]
    if begins:
        new_far, weights_far, new_near, sems = rest
    else:
        new_far, weights_far, right_far, new_near, right_near, sems = rest
    columns = grad_ref.shape[1]
    groups, own_rows, width = blocks[0].shape
    size = groups * own_rows
    rank = (width - columns) // 2
    own_y, own_z = lax.axis_index("rep") // Z_SIZE, lax.axis_index("rep") % Z_SIZE
    copies = []

    def send(source, target):
        copies.append(pltpu.make_async_copy(source, target, sems.at[len(copies)]))
        copies[-1].start()

    def piece_of(z):
        step = own_z ^ z
        return step ^ ((step >> 2) & (1 - ((step >> 1) & 1)))

    def rights_of(block):
        return jnp.concatenate([block[piece_of(z), :, columns:] for z in range(groups)], axis=0)

    def rows_of(d):
        return pl.ds(pl.multiple_of((own_y ^ LAST_STEPS[d]) * size, size), size)

    for d in ds:
        for j in range(groups):
            at = (own_y ^ LAST_STEPS[d]) * size + (own_z ^ Z_ORDER[j]) * own_rows
            target = weights_far.at[pl.ds(pl.multiple_of(at, own_rows), own_rows)]
            send(blocks[d].at[j, :, pl.ds(0, columns)], target)
    if not begins:
        row = lax.broadcasted_iota(jnp.int32, (rank, 2 * rank), 0)
        column = lax.broadcasted_iota(jnp.int32, (rank, 2 * rank), 1)
        both = jnp.where((row == column) | (row + rank == column), 1.0, 0.0).astype(BF16)
        for d, block in enumerate(blocks):
            right_near[:, rows_of(d)] = native(both, rights_of(block), 1, 1)
        send(right_near, right_far)
    for i, d in enumerate(ds):
        right = rights_of(blocks[d])
        approx = native(jnp.concatenate([right] * 3, axis=1), parts_ref[...], 1, 0)
        merged = grad_ref[rows_of(d), :].astype(F32) + feed_ref[rows_of(d), :].astype(F32)
        new_near[i] = (merged - approx).astype(BF16)
        send(new_near.at[i], new_far.at[rows_of(d)])
    for copy in copies:
        copy.wait()


def finish(begins, ds, blocks, parts, gradient, feedback, begun=()):
    rows, columns = gradient.shape
    groups, own_rows, width = blocks[0].shape
    rank = (width - columns) // 2
    far = pl.BlockSpec(memory_space=pl.ANY)
    outs = [jax.ShapeDtypeStruct((rows, columns), BF16)] * 2
    out_specs = [far, far]
    scratch = [pltpu.VMEM((len(ds), groups * own_rows, columns), BF16)]
    if not begins:
        outs = outs + [jax.ShapeDtypeStruct((rank, rows), F32)]
        out_specs = out_specs + [far]
        scratch = scratch + [pltpu.VMEM((rank, rows), F32)]
    return call(
        lambda *refs: finish_kernel(begins, ds, *refs),
        outs,
        (*blocks, parts, gradient, feedback),
        (len(ds) * 3 * 10**8, len(ds) * 1_500_000),
        "finish_own" if begins else "finish_rest",
        aliases={} if begins else {Y_SIZE + 3: 0, Y_SIZE + 4: 1},
        out_specs=out_specs,
        spare=begun,
        scratch=scratch + [pltpu.SemaphoreType.DMA((len(ds) * (groups + 1) + 1,))],
    )


def on_device(gradient, feedback, warm_start, master, moment, second):
    replicas = lax.axis_size("rep")
    gradient, feedback = gradient[0], feedback[0]

    pieces, gradient, feedback = local_factor(warm_start.T, gradient, feedback)
    quarter = sum_four([pieces[0]] + [exchange(p, "rep", d) for p, d in zip(pieces[1:], Y_STEPS)])
    for distance in Z_SUM_STEPS:
        quarter = quarter + exchange(quarter, "rep", distance)
    quarter = quarter / replicas
    quarters = [quarter] + [exchange(quarter, "rep", d) for d in Y_STEPS]
    factor_t, parts, gram_term = assemble(quarters)

    gram_pair = gram_term + exchange(gram_term, "shard", 1)
    packed = project(gradient, feedback, parts, replicas)
    gram_pair, packed = lax.optimization_barrier((gram_pair, packed))
    received = lax.all_to_all(packed, "rep", 0, 0, tiled=True)
    gram = sum_four([gram_pair] + [exchange(gram_pair, "shard", d) for d in X_STEPS])
    inverse, unit_t, unit_parts = invert(gram, factor_t)
    received, inverse, unit_t, unit_parts = lax.optimization_barrier(
        (received, inverse, unit_t, unit_parts)
    )
    own_sum = shard_sum(received.sum(0))

    send, master_out, moment_out, second_out = update(
        replicas, own_sum, inverse, unit_t, master, moment, second
    )
    pair = jnp.stack([send, exchange(send, "rep", 1)])
    column = jnp.concatenate([pair] + [exchange(pair, "rep", d) for d in Z_PAIRS])
    others = [exchange(column, "rep", Z_SIZE * d) for d in LAST_STEPS[1:]]
    begun = finish(True, (0,), [column], unit_parts, gradient, feedback)
    blocks = [column] + others
    new_feedback, weights, right_t = finish(
        False, (1, 2, 3), blocks, unit_parts, gradient, feedback, begun
    )
    return (new_feedback[None], weights, master_out, moment_out, second_out, right_t.T)


def solution(mesh):
    return jax.shard_map(
        on_device,
        mesh=mesh,
        in_specs=(
            P("rep", None, "shard"),
            P("rep", None, "shard"),
            P(),
            P("rep", "shard"),
            P("rep", "shard"),
            P("rep", "shard"),
        ),
        out_specs=(
            P("rep", None, "shard"),
            P(None, "shard"),
            P("rep", "shard"),
            P("rep", "shard"),
            P("rep", "shard"),
            P(),
        ),
        check_vma=False,
    )
```

```python
import jax
import jax.numpy as jnp
from jax import lax
from jax.experimental import pallas as pl
from jax.experimental.pallas import tpu as pltpu
from jax.sharding import PartitionSpec as P

HIGHEST = lax.Precision.HIGHEST
beta_one = 0.9
beta_two = 0.95
learn_rate = 0.02
decay_rate = 0.1
adam_eps = 1e-08
ridge_rate = 1e-06

F32 = jnp.float32
BF16 = jnp.bfloat16
Y_SIZE, Z_SIZE = 4, 8
Y_STEPS = (8, 16, 24)
X_STEPS = (2, 4, 6)
Z_SUM_STEPS = (1, 3, 7)
Z_PAIRS = (2, 5, 6)
Z_ORDER = tuple(pair ^ bit for pair in (0,) + Z_PAIRS for bit in (0, 1))
LAST_STEPS = (0, 1, 3, 2)
ROW_BLOCKS = 4


def exact(left, right, left_dim, right_dim):
    return lax.dot_general(
        left,
        right,
        (((left_dim,), (right_dim,)), ((), ())),
        precision=HIGHEST,
        preferred_element_type=F32,
    )


def native(left, right, left_dim, right_dim):
    return lax.dot_general(
        left, right, (((left_dim,), (right_dim,)), ((), ())), preferred_element_type=F32
    )


def three_parts(value):
    high = value.astype(BF16)
    rest = value - high.astype(F32)
    middle = rest.astype(BF16)
    return high, middle, (rest - middle.astype(F32)).astype(BF16)


def exchange(value, axis, distance):
    return lax.ppermute(value, axis, [(i, i ^ distance) for i in range(lax.axis_size(axis))])


def sum_four(terms):
    return (terms[0] + terms[1]) + (terms[2] + terms[3])


def shard_sum(value):
    value = value + exchange(value, "shard", 1)
    return sum_four([value] + [exchange(value, "shard", d) for d in X_STEPS])


def call(kernel, outs, args, cost, name, aliases=None, out_specs=None, spare=(), scratch=()):
    specs = [pl.BlockSpec(memory_space=pltpu.VMEM)] * len(args)
    specs += [pl.BlockSpec(memory_space=pl.ANY)] * len(spare)
    flops, traffic = cost
    return pl.pallas_call(
        kernel,
        out_shape=outs,
        in_specs=specs,
        out_specs=out_specs or [pl.BlockSpec(memory_space=pltpu.VMEM)] * len(outs),
        scratch_shapes=scratch,
        input_output_aliases=aliases or {},
        compiler_params=pltpu.CompilerParams(vmem_limit_bytes=16 * 2**20),
        cost_estimate=pl.CostEstimate(flops=flops, bytes_accessed=traffic, transcendentals=0),
        name=name,
    )(*[pltpu.with_memory_space_constraint(v, pltpu.VMEM) for v in args], *spare)


def factor_kernel(warm_far, grad_far, feed_far, *refs):
    outs, (grad_ref, feed_ref, warm_ref, parts_ref, total_ref, sems) = refs[:Y_SIZE], refs[Y_SIZE:]
    rank, rows = warm_ref.shape
    quarter = outs[0].shape[1]
    size = rows // ROW_BLOCKS
    warm_copy = pltpu.make_async_copy(warm_far, warm_ref, sems.at[2 * ROW_BLOCKS])
    warm_copy.start()
    copies = []
    for i in range(ROW_BLOCKS):
        at = pl.ds(i * size, size)
        for k, (far, ref) in enumerate([(grad_far, grad_ref), (feed_far, feed_ref)]):
            copies.append(pltpu.make_async_copy(far.at[at], ref.at[at], sems.at[2 * i + k]))
            copies[-1].start()
    warm_copy.wait()
    for i, part in enumerate(three_parts(warm_ref[...])):
        parts_ref[i * rank : (i + 1) * rank, :] = part
    total = None
    for i in range(ROW_BLOCKS):
        at = slice(i * size, (i + 1) * size)
        copies[2 * i].wait()
        copies[2 * i + 1].wait()
        parts = parts_ref[:, at]
        term = native(parts, grad_ref[at, :], 1, 0) + native(parts, feed_ref[at, :], 1, 0)
        total = term if total is None else total + term
    total_ref[...] = (total[2 * rank :] + total[rank : 2 * rank]) + total[:rank]
    own = lax.axis_index("rep") // Z_SIZE
    for d, out in enumerate(outs):
        out[...] = total_ref[:, pl.ds(pl.multiple_of((own ^ d) * quarter, quarter), quarter)]


def local_factor(warm_t, gradient, feedback):
    rank, rows = warm_t.shape
    columns = gradient.shape[1]
    near = pltpu.VMEM((rows, columns), BF16)
    args = [pltpu.with_memory_space_constraint(v, pltpu.HBM) for v in (warm_t, gradient, feedback)]
    outs = pl.pallas_call(
        factor_kernel,
        out_shape=[pltpu.VMEM((rank, columns // Y_SIZE), F32)] * Y_SIZE + [near] * 2,
        in_specs=[pl.BlockSpec(memory_space=pl.ANY)] * 3,
        out_specs=[pl.BlockSpec(memory_space=pltpu.VMEM)] * (Y_SIZE + 2),
        scratch_shapes=[
            pltpu.VMEM((rank, rows), F32),
            pltpu.VMEM((3 * rank, rows), BF16),
            pltpu.VMEM((rank, columns), F32),
            pltpu.SemaphoreType.DMA((2 * ROW_BLOCKS + 1,)),
        ],
        compiler_params=pltpu.CompilerParams(vmem_limit_bytes=16 * 2**20),
        cost_estimate=pl.CostEstimate(flops=10**9, bytes_accessed=2_500_000, transcendentals=0),
        name="local_factor",
    )(*args)
    return outs[:Y_SIZE], outs[Y_SIZE], outs[Y_SIZE + 1]


def assemble_kernel(*refs):
    quarters, (factor_ref, parts_ref, gram_ref) = refs[:Y_SIZE], refs[Y_SIZE:]
    rank, quarter = quarters[0].shape
    own = lax.axis_index("rep") // Z_SIZE
    for d, block in enumerate(quarters):
        at = pl.ds(pl.multiple_of((own ^ d) * quarter, quarter), quarter)
        factor_ref[:, at] = block[...]
    factor = factor_ref[...]
    for i, part in enumerate(three_parts(factor)):
        parts_ref[i * rank : (i + 1) * rank, :] = part
    gram_ref[...] = exact(factor, factor, 1, 1)


def assemble(quarters):
    rank, quarter = quarters[0].shape
    columns = quarter * Y_SIZE
    outs = [
        pltpu.VMEM((rank, columns), F32),
        pltpu.VMEM((3 * rank, columns), BF16),
        pltpu.VMEM((rank, rank), F32),
    ]
    return call(assemble_kernel, outs, tuple(quarters), (10**8, 500_000), "assemble_factor")


def project_kernel(grad_ref, feed_ref, parts_ref, out_ref):
    replicas, half, _ = out_ref.shape
    rows = grad_ref.shape[0]
    rank = parts_ref.shape[0] // 3
    parts = parts_ref[...]
    groups = 8
    size = rows // replicas * groups

    for i in range(replicas // groups):
        at = slice(i * size, (i + 1) * size)
        total = native(grad_ref[at, :], parts, 1, 1) + native(feed_ref[at, :], parts, 1, 1)
        value = (total[:, 2 * rank :] + total[:, rank : 2 * rank]) + total[:, :rank]
        value = value.reshape(groups, 2, half, rank)
        out_ref[i * groups : (i + 1) * groups] = jnp.concatenate([value[:, 0], value[:, 1]], axis=-1)


def project(gradient, feedback, parts, replicas):
    rank = parts.shape[0] // 3
    half = gradient.shape[0] // replicas // 2
    outs = [pltpu.VMEM((replicas, half, 2 * rank), F32)]
    return call(
        project_kernel, outs, (gradient, feedback, parts), (10**9, 2_500_000), "project"
    )[0]


def inverse_kernel(gram_ref, factor_ref, inverse_ref, unit_ref, parts_ref):
    rank = gram_ref.shape[0]
    width = 8
    row = lax.broadcasted_iota(jnp.int32, (rank, rank), 0)
    column = lax.broadcasted_iota(jnp.int32, (rank, rank), 1)
    diagonal = row == column
    gram = gram_ref[...]
    trace = jnp.sum(jnp.where(diagonal, gram, 0.0))
    gram = gram + jnp.where(diagonal, ridge_rate * trace / rank, 0.0)
    table = jnp.concatenate([gram, jnp.where(diagonal, 1.0, 0.0)], axis=1)
    row = lax.broadcasted_iota(jnp.int32, table.shape, 0)
    pivots = jnp.ones(table.shape, F32)
    for k in range(0, rank, width):
        ahead = [jnp.broadcast_to(table[:, c : c + 1], table.shape) for c in range(k, k + width)]
        lines = [table[c : c + 1, :] for c in range(k, k + width)]
        for i in range(width):
            at = k + i
            pivot = ahead[i][at : at + 1, :]
            pivots = jnp.where(row == at, pivot, pivots)
            scale = jnp.where(row > at, ahead[i] * (1.0 / pivot), 0.0)
            for j in range(i + 1, width):
                entry = ahead[j][at : at + 1, :]
                ahead[j] = ahead[j] - scale * entry
                lines[j] = lines[j] - scale[k + j : k + j + 1, :] * lines[i]
            table = table - scale * lines[i]
    inverse = table[:, rank:] / jnp.sqrt(pivots[:, rank:])
    inverse_ref[...] = inverse
    unit = exact(inverse, factor_ref[...], 1, 0)
    unit_ref[...] = unit
    for i, part in enumerate(three_parts(unit)):
        parts_ref[2 * i * rank : (2 * i + 1) * rank, :] = part
        parts_ref[(2 * i + 1) * rank : (2 * i + 2) * rank, :] = part


def invert(gram, factor_t):
    rank, columns = factor_t.shape
    outs = [
        pltpu.VMEM((rank, rank), F32),
        pltpu.VMEM((rank, columns), F32),
        pltpu.VMEM((6 * rank, columns), BF16),
    ]
    return call(inverse_kernel, outs, (gram, factor_t), (2 * 10**9, 500_000), "invert")


def update_kernel(replicas, sum_ref, inverse_ref, unit_ref, master_ref, moment_ref,
                  second_ref, send_ref, master_out, moment_out, second_out):
    rank = inverse_ref.shape[0]
    columns = master_ref.shape[1]
    packed = sum_ref[...]
    own = jnp.concatenate([packed[:, :rank], packed[:, rank:]], axis=0)
    right = exact(own, inverse_ref[...], 1, 1) / replicas
    grad = exact(right, unit_ref[...], 1, 0)
    moment = beta_one * moment_ref[...] + (1.0 - beta_one) * grad
    second = beta_two * second_ref[...] + (1.0 - beta_two) * grad * grad
    master = master_ref[...]
    master = master - learn_rate * (
        moment / (jnp.sqrt(second) + adam_eps) + decay_rate * master
    )
    moment_out[...] = moment
    second_out[...] = second
    master_out[...] = master
    high = right.astype(BF16).astype(F32)
    send_ref[:, :columns] = master.astype(BF16)
    send_ref[:, columns:] = jnp.concatenate([high, right - high], axis=1).astype(BF16)


def update(replicas, own_sum, inverse, unit_t, master, moment, second):
    rows, columns = master.shape
    rank = inverse.shape[0]
    block = pltpu.VMEM(master.shape, F32)
    outs = [pltpu.VMEM((rows, columns + 2 * rank), BF16), block, block, block]
    args = (own_sum, inverse, unit_t, master, moment, second)
    kernel = lambda *refs: update_kernel(replicas, *refs)
    return call(kernel, outs, args, (5 * 10**7, 600_000), "update")


def finish_kernel(ds, begun, *refs):
    count = len(ds)
    blocks, (parts_ref, grad_ref, feed_ref) = refs[:count], refs[count : count + 3]
    new_far, weights_far, right_far, new_near, right_near, sems = refs[count + 3 + begun :]
    columns = grad_ref.shape[1]
    groups, own_rows, width = blocks[0].shape
    size = groups * own_rows
    rank = (width - columns) // 2
    own_y, own_z = lax.axis_index("rep") // Z_SIZE, lax.axis_index("rep") % Z_SIZE
    copies = []

    def send(source, target):
        copies.append(pltpu.make_async_copy(source, target, sems.at[len(copies)]))
        copies[-1].start()

    def piece_of(z):
        step = own_z ^ z
        return step ^ ((step >> 2) & (1 - ((step >> 1) & 1)))

    def rows_of(d):
        return pl.ds(pl.multiple_of((own_y ^ LAST_STEPS[d]) * size, size), size)

    for i, d in enumerate(ds):
        for j in range(groups):
            at = (own_y ^ LAST_STEPS[d]) * size + (own_z ^ Z_ORDER[j]) * own_rows
            target = weights_far.at[pl.ds(pl.multiple_of(at, own_rows), own_rows)]
            send(blocks[i].at[j, :, pl.ds(0, columns)], target)
    row = lax.broadcasted_iota(jnp.int32, (rank, 2 * rank), 0)
    column = lax.broadcasted_iota(jnp.int32, (rank, 2 * rank), 1)
    both = jnp.where((row == column) | (row + rank == column), 1.0, 0.0).astype(BF16)
    for i, d in enumerate(ds):
        pieces = [blocks[i][piece_of(z), :, columns:] for z in range(groups)]
        right = jnp.concatenate(pieces, axis=0)
        right_near[i] = native(both, right, 1, 1)
        send(right_near.at[i], right_far.at[:, rows_of(d)])
        approx = native(jnp.concatenate([right] * 3, axis=1), parts_ref[...], 1, 0)
        merged = grad_ref[rows_of(d), :].astype(F32) + feed_ref[rows_of(d), :].astype(F32)
        new_near[i] = (merged - approx).astype(BF16)
        send(new_near.at[i], new_far.at[rows_of(d)])
    for copy in copies:
        copy.wait()


def finish(name, ds, blocks, parts, gradient, feedback, begun=()):
    rows, columns = gradient.shape
    groups, own_rows, width = blocks[0].shape
    rank = (width - columns) // 2
    size = groups * own_rows
    count = len(ds)
    return call(
        lambda *refs: finish_kernel(ds, len(begun), *refs),
        [jax.ShapeDtypeStruct((rows, columns), BF16)] * 2
        + [jax.ShapeDtypeStruct((rank, rows), F32)],
        (*blocks, parts, gradient, feedback),
        (count * 3 * 10**8, count * 1_500_000),
        name,
        aliases={count + 3 + i: i for i in range(len(begun))},
        out_specs=[pl.BlockSpec(memory_space=pl.ANY)] * 3,
        spare=begun,
        scratch=[
            pltpu.VMEM((count, size, columns), BF16),
            pltpu.VMEM((count, rank, size), F32),
            pltpu.SemaphoreType.DMA((count * (groups + 2),)),
        ],
    )


def on_device(gradient, feedback, warm_start, master, moment, second):
    replicas = lax.axis_size("rep")
    gradient, feedback = gradient[0], feedback[0]

    pieces, gradient, feedback = local_factor(warm_start.T, gradient, feedback)
    quarter = sum_four([pieces[0]] + [exchange(p, "rep", d) for p, d in zip(pieces[1:], Y_STEPS)])
    for distance in Z_SUM_STEPS:
        quarter = quarter + exchange(quarter, "rep", distance)
    quarter = quarter / replicas
    quarters = [quarter] + [exchange(quarter, "rep", d) for d in Y_STEPS]
    factor_t, parts, gram_term = assemble(quarters)

    gram_pair = gram_term + exchange(gram_term, "shard", 1)
    packed = project(gradient, feedback, parts, replicas)
    gram_pair, packed = lax.optimization_barrier((gram_pair, packed))
    received = lax.all_to_all(packed, "rep", 0, 0, tiled=True)
    gram = sum_four([gram_pair] + [exchange(gram_pair, "shard", d) for d in X_STEPS])
    inverse, unit_t, unit_parts = invert(gram, factor_t)
    received, inverse, unit_t, unit_parts = lax.optimization_barrier(
        (received, inverse, unit_t, unit_parts)
    )
    own_sum = shard_sum(received.sum(0))

    send, master_out, moment_out, second_out = update(
        replicas, own_sum, inverse, unit_t, master, moment, second
    )
    pair = jnp.stack([send, exchange(send, "rep", 1)])
    column = jnp.concatenate([pair] + [exchange(pair, "rep", d) for d in Z_PAIRS])
    others = [exchange(column, "rep", Z_SIZE * d) for d in LAST_STEPS[1:]]
    rest = (unit_parts, gradient, feedback)
    begun = finish("finish_own", (0,), [column], *rest)
    begun = finish("finish_far", (3,), others[2:], *rest, begun)
    new_feedback, weights, right_t = finish("finish_near", (1, 2), others[:2], *rest, begun)
    return (new_feedback[None], weights, master_out, moment_out, second_out, right_t.T)


def solution(mesh):
    return jax.shard_map(
        on_device,
        mesh=mesh,
        in_specs=(
            P("rep", None, "shard"),
            P("rep", None, "shard"),
            P(),
            P("rep", "shard"),
            P("rep", "shard"),
            P("rep", "shard"),
        ),
        out_specs=(
            P("rep", None, "shard"),
            P(None, "shard"),
            P("rep", "shard"),
            P("rep", "shard"),
            P("rep", "shard"),
            P(),
        ),
        check_vma=False,
    )
```

```python
import jax
import jax.numpy as jnp
from jax import lax
from jax.experimental import pallas as pl
from jax.experimental.pallas import tpu as pltpu
from jax.sharding import PartitionSpec as P

HIGHEST = lax.Precision.HIGHEST
beta_one = 0.9
beta_two = 0.95
learn_rate = 0.02
decay_rate = 0.1
adam_eps = 1e-08
ridge_rate = 1e-06

F32 = jnp.float32
BF16 = jnp.bfloat16
Y_SIZE, Z_SIZE = 4, 8
Y_STEPS = (8, 16, 24)
X_STEPS = (2, 4, 6)
Z_SUM_STEPS = (1, 3, 7)
Z_PAIRS = (2, 5, 6)
Z_ORDER = tuple(pair ^ bit for pair in (0,) + Z_PAIRS for bit in (0, 1))
LAST_STEPS = (0, 1, 3, 2)
GATHER_STEPS = (0, 3, 2, 1)
ROW_BLOCKS = 4


def exact(left, right, left_dim, right_dim):
    return lax.dot_general(
        left,
        right,
        (((left_dim,), (right_dim,)), ((), ())),
        precision=HIGHEST,
        preferred_element_type=F32,
    )


def native(left, right, left_dim, right_dim):
    return lax.dot_general(
        left, right, (((left_dim,), (right_dim,)), ((), ())), preferred_element_type=F32
    )


def three_parts(value):
    high = value.astype(BF16)
    rest = value - high.astype(F32)
    middle = rest.astype(BF16)
    return high, middle, (rest - middle.astype(F32)).astype(BF16)


def exchange(value, axis, distance):
    return lax.ppermute(value, axis, [(i, i ^ distance) for i in range(lax.axis_size(axis))])


def sum_four(terms):
    return (terms[0] + terms[1]) + (terms[2] + terms[3])


def shard_sum(value):
    value = value + exchange(value, "shard", 1)
    return sum_four([value] + [exchange(value, "shard", d) for d in X_STEPS[::-1]])


def call(kernel, outs, args, cost, name, aliases=None, out_specs=None, spare=(), scratch=()):
    specs = [pl.BlockSpec(memory_space=pltpu.VMEM)] * len(args)
    specs += [pl.BlockSpec(memory_space=pl.ANY)] * len(spare)
    flops, traffic = cost
    return pl.pallas_call(
        kernel,
        out_shape=outs,
        in_specs=specs,
        out_specs=out_specs or [pl.BlockSpec(memory_space=pltpu.VMEM)] * len(outs),
        scratch_shapes=scratch,
        input_output_aliases=aliases or {},
        compiler_params=pltpu.CompilerParams(vmem_limit_bytes=16 * 2**20),
        cost_estimate=pl.CostEstimate(flops=flops, bytes_accessed=traffic, transcendentals=0),
        name=name,
    )(*[pltpu.with_memory_space_constraint(v, pltpu.VMEM) for v in args], *spare)


def factor_kernel(warm_far, grad_far, feed_far, *refs):
    outs, (grad_ref, feed_ref, warm_ref, parts_ref, total_ref, sems) = refs[:Y_SIZE], refs[Y_SIZE:]
    rank, rows = warm_ref.shape
    quarter = outs[0].shape[1]
    size = rows // ROW_BLOCKS
    warm_copy = pltpu.make_async_copy(warm_far, warm_ref, sems.at[2 * ROW_BLOCKS])
    warm_copy.start()
    copies = []
    for i in range(ROW_BLOCKS):
        at = pl.ds(i * size, size)
        for k, (far, ref) in enumerate([(grad_far, grad_ref), (feed_far, feed_ref)]):
            copies.append(pltpu.make_async_copy(far.at[at], ref.at[at], sems.at[2 * i + k]))
            copies[-1].start()
    warm_copy.wait()
    for i, part in enumerate(three_parts(warm_ref[...])):
        parts_ref[i * rank : (i + 1) * rank, :] = part
    total = None
    for i in range(ROW_BLOCKS):
        at = slice(i * size, (i + 1) * size)
        copies[2 * i].wait()
        copies[2 * i + 1].wait()
        parts = parts_ref[:, at]
        term = native(parts, grad_ref[at, :], 1, 0) + native(parts, feed_ref[at, :], 1, 0)
        total = term if total is None else total + term
    total_ref[...] = (total[2 * rank :] + total[rank : 2 * rank]) + total[:rank]
    own = lax.axis_index("rep") // Z_SIZE
    for d, out in enumerate(outs):
        out[...] = total_ref[:, pl.ds(pl.multiple_of((own ^ d) * quarter, quarter), quarter)]


def local_factor(warm_t, gradient, feedback):
    rank, rows = warm_t.shape
    columns = gradient.shape[1]
    near = pltpu.VMEM((rows, columns), BF16)
    args = [pltpu.with_memory_space_constraint(v, pltpu.HBM) for v in (warm_t, gradient, feedback)]
    outs = pl.pallas_call(
        factor_kernel,
        out_shape=[pltpu.VMEM((rank, columns // Y_SIZE), F32)] * Y_SIZE + [near] * 2,
        in_specs=[pl.BlockSpec(memory_space=pl.ANY)] * 3,
        out_specs=[pl.BlockSpec(memory_space=pltpu.VMEM)] * (Y_SIZE + 2),
        scratch_shapes=[
            pltpu.VMEM((rank, rows), F32),
            pltpu.VMEM((3 * rank, rows), BF16),
            pltpu.VMEM((rank, columns), F32),
            pltpu.SemaphoreType.DMA((2 * ROW_BLOCKS + 1,)),
        ],
        compiler_params=pltpu.CompilerParams(vmem_limit_bytes=16 * 2**20),
        cost_estimate=pl.CostEstimate(flops=10**9, bytes_accessed=2_500_000, transcendentals=0),
        name="local_factor",
    )(*args)
    return outs[:Y_SIZE], outs[Y_SIZE], outs[Y_SIZE + 1]


def assemble_kernel(*refs):
    quarters, (factor_ref, parts_ref, gram_ref) = refs[:Y_SIZE], refs[Y_SIZE:]
    rank, quarter = quarters[0].shape
    own = lax.axis_index("rep") // Z_SIZE
    for d, block in zip(GATHER_STEPS, quarters):
        at = pl.ds(pl.multiple_of((own ^ d) * quarter, quarter), quarter)
        factor_ref[:, at] = block[...]
    factor = factor_ref[...]
    for i, part in enumerate(three_parts(factor)):
        parts_ref[i * rank : (i + 1) * rank, :] = part
    gram_ref[...] = exact(factor, factor, 1, 1)


def assemble(quarters):
    rank, quarter = quarters[0].shape
    columns = quarter * Y_SIZE
    outs = [
        pltpu.VMEM((rank, columns), F32),
        pltpu.VMEM((3 * rank, columns), BF16),
        pltpu.VMEM((rank, rank), F32),
    ]
    return call(assemble_kernel, outs, tuple(quarters), (10**8, 500_000), "assemble_factor")


def project_kernel(grad_ref, feed_ref, parts_ref, out_ref):
    replicas, half, _ = out_ref.shape
    rows = grad_ref.shape[0]
    rank = parts_ref.shape[0] // 3
    parts = parts_ref[...]
    groups = 8
    size = rows // replicas * groups

    for i in range(replicas // groups):
        at = slice(i * size, (i + 1) * size)
        total = native(grad_ref[at, :], parts, 1, 1) + native(feed_ref[at, :], parts, 1, 1)
        value = (total[:, 2 * rank :] + total[:, rank : 2 * rank]) + total[:, :rank]
        value = value.reshape(groups, 2, half, rank)
        out_ref[i * groups : (i + 1) * groups] = jnp.concatenate([value[:, 0], value[:, 1]], axis=-1)


def project(gradient, feedback, parts, replicas):
    rank = parts.shape[0] // 3
    half = gradient.shape[0] // replicas // 2
    outs = [pltpu.VMEM((replicas, half, 2 * rank), F32)]
    return call(
        project_kernel, outs, (gradient, feedback, parts), (10**9, 2_500_000), "project"
    )[0]


def inverse_kernel(gram_ref, factor_ref, inverse_ref, unit_ref, parts_ref):
    rank = gram_ref.shape[0]
    width = 8
    row = lax.broadcasted_iota(jnp.int32, (rank, rank), 0)
    column = lax.broadcasted_iota(jnp.int32, (rank, rank), 1)
    diagonal = row == column
    gram = gram_ref[...]
    trace = jnp.sum(jnp.where(diagonal, gram, 0.0))
    gram = gram + jnp.where(diagonal, ridge_rate * trace / rank, 0.0)
    table = jnp.concatenate([gram, jnp.where(diagonal, 1.0, 0.0)], axis=1)
    row = lax.broadcasted_iota(jnp.int32, table.shape, 0)
    pivots = jnp.ones(table.shape, F32)
    for k in range(0, rank, width):
        ahead = [jnp.broadcast_to(table[:, c : c + 1], table.shape) for c in range(k, k + width)]
        lines = [table[c : c + 1, :] for c in range(k, k + width)]
        for i in range(width):
            at = k + i
            pivot = ahead[i][at : at + 1, :]
            pivots = jnp.where(row == at, pivot, pivots)
            scale = jnp.where(row > at, ahead[i] * (1.0 / pivot), 0.0)
            for j in range(i + 1, width):
                entry = ahead[j][at : at + 1, :]
                ahead[j] = ahead[j] - scale * entry
                lines[j] = lines[j] - scale[k + j : k + j + 1, :] * lines[i]
            table = table - scale * lines[i]
    inverse = table[:, rank:] / jnp.sqrt(pivots[:, rank:])
    inverse_ref[...] = inverse
    unit = exact(inverse, factor_ref[...], 1, 0)
    unit_ref[...] = unit
    for i, part in enumerate(three_parts(unit)):
        parts_ref[2 * i * rank : (2 * i + 1) * rank, :] = part
        parts_ref[(2 * i + 1) * rank : (2 * i + 2) * rank, :] = part


def invert(gram, factor_t):
    rank, columns = factor_t.shape
    outs = [
        pltpu.VMEM((rank, rank), F32),
        pltpu.VMEM((rank, columns), F32),
        pltpu.VMEM((6 * rank, columns), BF16),
    ]
    return call(inverse_kernel, outs, (gram, factor_t), (2 * 10**9, 500_000), "invert")


def update_kernel(replicas, sum_ref, inverse_ref, unit_ref, master_ref, moment_ref,
                  second_ref, send_ref, master_out, moment_out, second_out):
    rank = inverse_ref.shape[0]
    columns = master_ref.shape[1]
    packed = sum_ref[...]
    own = jnp.concatenate([packed[:, :rank], packed[:, rank:]], axis=0)
    right = exact(own, inverse_ref[...], 1, 1) / replicas
    grad = exact(right, unit_ref[...], 1, 0)
    moment = beta_one * moment_ref[...] + (1.0 - beta_one) * grad
    second = beta_two * second_ref[...] + (1.0 - beta_two) * grad * grad
    master = master_ref[...]
    master = master - learn_rate * (
        moment / (jnp.sqrt(second) + adam_eps) + decay_rate * master
    )
    moment_out[...] = moment
    second_out[...] = second
    master_out[...] = master
    high = right.astype(BF16).astype(F32)
    send_ref[:, :columns] = master.astype(BF16)
    send_ref[:, columns:] = jnp.concatenate([high, right - high], axis=1).astype(BF16)


def update(replicas, own_sum, inverse, unit_t, master, moment, second):
    rows, columns = master.shape
    rank = inverse.shape[0]
    block = pltpu.VMEM(master.shape, F32)
    outs = [pltpu.VMEM((rows, columns + 2 * rank), BF16), block, block, block]
    args = (own_sum, inverse, unit_t, master, moment, second)
    kernel = lambda *refs: update_kernel(replicas, *refs)
    return call(kernel, outs, args, (5 * 10**7, 600_000), "update")


def finish_kernel(ds, begun, *refs):
    count = len(ds)
    blocks, (parts_ref, grad_ref, feed_ref) = refs[:count], refs[count : count + 3]
    new_far, weights_far, right_far, new_near, right_near, sems = refs[count + 3 + begun :]
    columns = grad_ref.shape[1]
    groups, own_rows, width = blocks[0].shape
    size = groups * own_rows
    rank = (width - columns) // 2
    own_y, own_z = lax.axis_index("rep") // Z_SIZE, lax.axis_index("rep") % Z_SIZE
    copies = []

    def send(source, target):
        copies.append(pltpu.make_async_copy(source, target, sems.at[len(copies)]))
        copies[-1].start()

    def piece_of(z):
        step = own_z ^ z
        return step ^ ((step >> 2) & (1 - ((step >> 1) & 1)))

    def rows_of(d):
        return pl.ds(pl.multiple_of((own_y ^ LAST_STEPS[d]) * size, size), size)

    for i, d in enumerate(ds):
        for j in range(groups):
            at = (own_y ^ LAST_STEPS[d]) * size + (own_z ^ Z_ORDER[j]) * own_rows
            target = weights_far.at[pl.ds(pl.multiple_of(at, own_rows), own_rows)]
            send(blocks[i].at[j, :, pl.ds(0, columns)], target)
    row = lax.broadcasted_iota(jnp.int32, (rank, 2 * rank), 0)
    column = lax.broadcasted_iota(jnp.int32, (rank, 2 * rank), 1)
    both = jnp.where((row == column) | (row + rank == column), 1.0, 0.0).astype(BF16)
    for i, d in enumerate(ds):
        pieces = [blocks[i][piece_of(z), :, columns:] for z in range(groups)]
        right = jnp.concatenate(pieces, axis=0)
        right_near[i] = native(both, right, 1, 1)
        send(right_near.at[i], right_far.at[:, rows_of(d)])
        approx = native(jnp.concatenate([right] * 3, axis=1), parts_ref[...], 1, 0)
        merged = grad_ref[rows_of(d), :].astype(F32) + feed_ref[rows_of(d), :].astype(F32)
        new_near[i] = (merged - approx).astype(BF16)
        send(new_near.at[i], new_far.at[rows_of(d)])
    for copy in copies:
        copy.wait()


def finish(name, ds, blocks, parts, gradient, feedback, begun=()):
    rows, columns = gradient.shape
    groups, own_rows, width = blocks[0].shape
    rank = (width - columns) // 2
    size = groups * own_rows
    count = len(ds)
    return call(
        lambda *refs: finish_kernel(ds, len(begun), *refs),
        [jax.ShapeDtypeStruct((rows, columns), BF16)] * 2
        + [jax.ShapeDtypeStruct((rank, rows), F32)],
        (*blocks, parts, gradient, feedback),
        (count * 3 * 10**8, count * 1_500_000),
        name,
        aliases={count + 3 + i: i for i in range(len(begun))},
        out_specs=[pl.BlockSpec(memory_space=pl.ANY)] * 3,
        spare=begun,
        scratch=[
            pltpu.VMEM((count, size, columns), BF16),
            pltpu.VMEM((count, rank, size), F32),
            pltpu.SemaphoreType.DMA((count * (groups + 2),)),
        ],
    )


def on_device(gradient, feedback, warm_start, master, moment, second):
    replicas = lax.axis_size("rep")
    gradient, feedback = gradient[0], feedback[0]

    pieces, gradient, feedback = local_factor(warm_start.T, gradient, feedback)
    quarter = sum_four([pieces[0]] + [exchange(p, "rep", d) for p, d in zip(pieces[1:], Y_STEPS)])
    for distance in Z_SUM_STEPS:
        quarter = quarter + exchange(quarter, "rep", distance)
    quarter = quarter / replicas
    quarters = [quarter] + [exchange(quarter, "rep", Z_SIZE * d) for d in GATHER_STEPS[1:]]
    factor_t, parts, gram_term = assemble(quarters)

    gram_pair = gram_term + exchange(gram_term, "shard", 1)
    packed = project(gradient, feedback, parts, replicas)
    gram_pair, packed = lax.optimization_barrier((gram_pair, packed))
    received = lax.all_to_all(packed, "rep", 0, 0, tiled=True)
    gram = sum_four([gram_pair] + [exchange(gram_pair, "shard", d) for d in X_STEPS[::-1]])
    inverse, unit_t, unit_parts = invert(gram, factor_t)
    received, inverse, unit_t, unit_parts = lax.optimization_barrier(
        (received, inverse, unit_t, unit_parts)
    )
    own_sum = shard_sum(received.sum(0))

    send, master_out, moment_out, second_out = update(
        replicas, own_sum, inverse, unit_t, master, moment, second
    )
    pair = jnp.stack([send, exchange(send, "rep", 1)])
    column = jnp.concatenate([pair] + [exchange(pair, "rep", d) for d in Z_PAIRS])
    others = [exchange(column, "rep", Z_SIZE * d) for d in LAST_STEPS[1:]]
    rest = (unit_parts, gradient, feedback)
    begun = finish("finish_own", (0,), [column], *rest)
    begun = finish("finish_far", (3,), others[2:], *rest, begun)
    new_feedback, weights, right_t = finish("finish_near", (1, 2), others[:2], *rest, begun)
    return (new_feedback[None], weights, master_out, moment_out, second_out, right_t.T)


def solution(mesh):
    return jax.shard_map(
        on_device,
        mesh=mesh,
        in_specs=(
            P("rep", None, "shard"),
            P("rep", None, "shard"),
            P(),
            P("rep", "shard"),
            P("rep", "shard"),
            P("rep", "shard"),
        ),
        out_specs=(
            P("rep", None, "shard"),
            P(None, "shard"),
            P("rep", "shard"),
            P("rep", "shard"),
            P("rep", "shard"),
            P(),
        ),
        check_vma=False,
    )
```

```python
import jax
import jax.numpy as jnp
from jax import lax
from jax.experimental import pallas as pl
from jax.experimental.pallas import tpu as pltpu
from jax.sharding import PartitionSpec as P

HIGHEST = lax.Precision.HIGHEST
beta_one = 0.9
beta_two = 0.95
learn_rate = 0.02
decay_rate = 0.1
adam_eps = 1e-08
ridge_rate = 1e-06

F32 = jnp.float32
BF16 = jnp.bfloat16
Y_SIZE, Z_SIZE = 4, 8
Y_STEPS = (8, 16, 24)
X_STEPS = (2, 4, 6)
Z_SUM_STEPS = (1, 3, 7)
Z_PAIRS = (6, 5, 2)
Z_ORDER = tuple(pair ^ bit for pair in (0,) + Z_PAIRS for bit in (0, 1))
LAST_STEPS = (0, 3, 1, 2)
GATHER_STEPS = (0, 3, 2, 1)
ROW_BLOCKS = 4


def exact(left, right, left_dim, right_dim):
    return lax.dot_general(
        left,
        right,
        (((left_dim,), (right_dim,)), ((), ())),
        precision=HIGHEST,
        preferred_element_type=F32,
    )


def native(left, right, left_dim, right_dim):
    return lax.dot_general(
        left, right, (((left_dim,), (right_dim,)), ((), ())), preferred_element_type=F32
    )


def three_parts(value):
    high = value.astype(BF16)
    rest = value - high.astype(F32)
    middle = rest.astype(BF16)
    return high, middle, (rest - middle.astype(F32)).astype(BF16)


def exchange(value, axis, distance):
    return lax.ppermute(value, axis, [(i, i ^ distance) for i in range(lax.axis_size(axis))])


def sum_four(terms):
    return (terms[0] + terms[1]) + (terms[2] + terms[3])


def shard_sum(value):
    value = value + exchange(value, "shard", 1)
    return sum_four([value] + [exchange(value, "shard", d) for d in X_STEPS[::-1]])


def call(kernel, outs, args, cost, name, aliases=None, out_specs=None, spare=(), scratch=()):
    specs = [pl.BlockSpec(memory_space=pltpu.VMEM)] * len(args)
    specs += [pl.BlockSpec(memory_space=pl.ANY)] * len(spare)
    flops, traffic = cost
    return pl.pallas_call(
        kernel,
        out_shape=outs,
        in_specs=specs,
        out_specs=out_specs or [pl.BlockSpec(memory_space=pltpu.VMEM)] * len(outs),
        scratch_shapes=scratch,
        input_output_aliases=aliases or {},
        compiler_params=pltpu.CompilerParams(vmem_limit_bytes=16 * 2**20),
        cost_estimate=pl.CostEstimate(flops=flops, bytes_accessed=traffic, transcendentals=0),
        name=name,
    )(*[pltpu.with_memory_space_constraint(v, pltpu.VMEM) for v in args], *spare)


def factor_kernel(warm_far, grad_far, feed_far, *refs):
    outs, (grad_ref, feed_ref, warm_ref, parts_ref, total_ref, sems) = refs[:Y_SIZE], refs[Y_SIZE:]
    rank, rows = warm_ref.shape
    quarter = outs[0].shape[1]
    size = rows // ROW_BLOCKS
    warm_copy = pltpu.make_async_copy(warm_far, warm_ref, sems.at[2 * ROW_BLOCKS])
    warm_copy.start()
    copies = []
    for i in range(ROW_BLOCKS):
        at = pl.ds(i * size, size)
        for k, (far, ref) in enumerate([(grad_far, grad_ref), (feed_far, feed_ref)]):
            copies.append(pltpu.make_async_copy(far.at[at], ref.at[at], sems.at[2 * i + k]))
            copies[-1].start()
    warm_copy.wait()
    for i, part in enumerate(three_parts(warm_ref[...])):
        parts_ref[i * rank : (i + 1) * rank, :] = part
    total = None
    for i in range(ROW_BLOCKS):
        at = slice(i * size, (i + 1) * size)
        copies[2 * i].wait()
        copies[2 * i + 1].wait()
        parts = parts_ref[:, at]
        term = native(parts, grad_ref[at, :], 1, 0) + native(parts, feed_ref[at, :], 1, 0)
        total = term if total is None else total + term
    total_ref[...] = (total[2 * rank :] + total[rank : 2 * rank]) + total[:rank]
    own = lax.axis_index("rep") // Z_SIZE
    for d, out in enumerate(outs):
        out[...] = total_ref[:, pl.ds(pl.multiple_of((own ^ d) * quarter, quarter), quarter)]


def local_factor(warm_t, gradient, feedback):
    rank, rows = warm_t.shape
    columns = gradient.shape[1]
    near = pltpu.VMEM((rows, columns), BF16)
    args = [pltpu.with_memory_space_constraint(v, pltpu.HBM) for v in (warm_t, gradient, feedback)]
    outs = pl.pallas_call(
        factor_kernel,
        out_shape=[pltpu.VMEM((rank, columns // Y_SIZE), F32)] * Y_SIZE + [near] * 2,
        in_specs=[pl.BlockSpec(memory_space=pl.ANY)] * 3,
        out_specs=[pl.BlockSpec(memory_space=pltpu.VMEM)] * (Y_SIZE + 2),
        scratch_shapes=[
            pltpu.VMEM((rank, rows), F32),
            pltpu.VMEM((3 * rank, rows), BF16),
            pltpu.VMEM((rank, columns), F32),
            pltpu.SemaphoreType.DMA((2 * ROW_BLOCKS + 1,)),
        ],
        compiler_params=pltpu.CompilerParams(vmem_limit_bytes=16 * 2**20),
        cost_estimate=pl.CostEstimate(flops=10**9, bytes_accessed=2_500_000, transcendentals=0),
        name="local_factor",
    )(*args)
    return outs[:Y_SIZE], outs[Y_SIZE], outs[Y_SIZE + 1]


def assemble_kernel(*refs):
    quarters, (factor_ref, parts_ref, gram_ref) = refs[:Y_SIZE], refs[Y_SIZE:]
    rank, quarter = quarters[0].shape
    own = lax.axis_index("rep") // Z_SIZE
    for d, block in zip(GATHER_STEPS, quarters):
        at = pl.ds(pl.multiple_of((own ^ d) * quarter, quarter), quarter)
        factor_ref[:, at] = block[...]
    factor = factor_ref[...]
    for i, part in enumerate(three_parts(factor)):
        parts_ref[i * rank : (i + 1) * rank, :] = part
    gram_ref[...] = exact(factor, factor, 1, 1)


def assemble(quarters):
    rank, quarter = quarters[0].shape
    columns = quarter * Y_SIZE
    outs = [
        pltpu.VMEM((rank, columns), F32),
        pltpu.VMEM((3 * rank, columns), BF16),
        pltpu.VMEM((rank, rank), F32),
    ]
    return call(assemble_kernel, outs, tuple(quarters), (10**8, 500_000), "assemble_factor")


def project_kernel(grad_ref, feed_ref, parts_ref, out_ref):
    replicas, half, _ = out_ref.shape
    rows = grad_ref.shape[0]
    rank = parts_ref.shape[0] // 3
    parts = parts_ref[...]
    groups = 8
    size = rows // replicas * groups

    for i in range(replicas // groups):
        at = slice(i * size, (i + 1) * size)
        total = native(grad_ref[at, :], parts, 1, 1) + native(feed_ref[at, :], parts, 1, 1)
        value = (total[:, 2 * rank :] + total[:, rank : 2 * rank]) + total[:, :rank]
        value = value.reshape(groups, 2, half, rank)
        out_ref[i * groups : (i + 1) * groups] = jnp.concatenate([value[:, 0], value[:, 1]], axis=-1)


def project(gradient, feedback, parts, replicas):
    rank = parts.shape[0] // 3
    half = gradient.shape[0] // replicas // 2
    outs = [pltpu.VMEM((replicas, half, 2 * rank), F32)]
    return call(
        project_kernel, outs, (gradient, feedback, parts), (10**9, 2_500_000), "project"
    )[0]


def inverse_kernel(gram_ref, factor_ref, inverse_ref, unit_ref, parts_ref):
    rank = gram_ref.shape[0]
    width = 8
    row = lax.broadcasted_iota(jnp.int32, (rank, rank), 0)
    column = lax.broadcasted_iota(jnp.int32, (rank, rank), 1)
    diagonal = row == column
    gram = gram_ref[...]
    trace = jnp.sum(jnp.where(diagonal, gram, 0.0))
    gram = gram + jnp.where(diagonal, ridge_rate * trace / rank, 0.0)
    table = jnp.concatenate([gram, jnp.where(diagonal, 1.0, 0.0)], axis=1)
    row = lax.broadcasted_iota(jnp.int32, table.shape, 0)
    pivots = jnp.ones(table.shape, F32)
    for k in range(0, rank, width):
        ahead = [jnp.broadcast_to(table[:, c : c + 1], table.shape) for c in range(k, k + width)]
        lines = [table[c : c + 1, :] for c in range(k, k + width)]
        for i in range(width):
            at = k + i
            pivot = ahead[i][at : at + 1, :]
            pivots = jnp.where(row == at, pivot, pivots)
            scale = jnp.where(row > at, ahead[i] * (1.0 / pivot), 0.0)
            for j in range(i + 1, width):
                entry = ahead[j][at : at + 1, :]
                ahead[j] = ahead[j] - scale * entry
                lines[j] = lines[j] - scale[k + j : k + j + 1, :] * lines[i]
            table = table - scale * lines[i]
    inverse = table[:, rank:] / jnp.sqrt(pivots[:, rank:])
    inverse_ref[...] = inverse
    unit = exact(inverse, factor_ref[...], 1, 0)
    unit_ref[...] = unit
    for i, part in enumerate(three_parts(unit)):
        parts_ref[2 * i * rank : (2 * i + 1) * rank, :] = part
        parts_ref[(2 * i + 1) * rank : (2 * i + 2) * rank, :] = part


def invert(gram, factor_t):
    rank, columns = factor_t.shape
    outs = [
        pltpu.VMEM((rank, rank), F32),
        pltpu.VMEM((rank, columns), F32),
        pltpu.VMEM((6 * rank, columns), BF16),
    ]
    return call(inverse_kernel, outs, (gram, factor_t), (2 * 10**9, 500_000), "invert")


def update_kernel(replicas, sum_ref, inverse_ref, unit_ref, master_ref, moment_ref,
                  second_ref, send_ref, master_out, moment_out, second_out):
    rank = inverse_ref.shape[0]
    columns = master_ref.shape[1]
    packed = sum_ref[...]
    own = jnp.concatenate([packed[:, :rank], packed[:, rank:]], axis=0)
    right = exact(own, inverse_ref[...], 1, 1) / replicas
    grad = exact(right, unit_ref[...], 1, 0)
    moment = beta_one * moment_ref[...] + (1.0 - beta_one) * grad
    second = beta_two * second_ref[...] + (1.0 - beta_two) * grad * grad
    master = master_ref[...]
    master = master - learn_rate * (
        moment / (jnp.sqrt(second) + adam_eps) + decay_rate * master
    )
    moment_out[...] = moment
    second_out[...] = second
    master_out[...] = master
    high = right.astype(BF16).astype(F32)
    send_ref[:, :columns] = master.astype(BF16)
    send_ref[:, columns:] = jnp.concatenate([high, right - high], axis=1).astype(BF16)


def update(replicas, own_sum, inverse, unit_t, master, moment, second):
    rows, columns = master.shape
    rank = inverse.shape[0]
    block = pltpu.VMEM(master.shape, F32)
    outs = [pltpu.VMEM((rows, columns + 2 * rank), BF16), block, block, block]
    args = (own_sum, inverse, unit_t, master, moment, second)
    kernel = lambda *refs: update_kernel(replicas, *refs)
    return call(kernel, outs, args, (5 * 10**7, 600_000), "update")


def finish_kernel(ds, begun, *refs):
    count = len(ds)
    blocks, (parts_ref, grad_ref, feed_ref) = refs[:count], refs[count : count + 3]
    new_far, weights_far, right_far, new_near, right_near, sems = refs[count + 3 + begun :]
    columns = grad_ref.shape[1]
    groups, own_rows, width = blocks[0].shape
    size = groups * own_rows
    rank = (width - columns) // 2
    own_y, own_z = lax.axis_index("rep") // Z_SIZE, lax.axis_index("rep") % Z_SIZE
    copies = []

    def send(source, target):
        copies.append(pltpu.make_async_copy(source, target, sems.at[len(copies)]))
        copies[-1].start()

    def piece_of(z):
        step = own_z ^ z
        swapped = (step >> 2) & (1 - ((step >> 1) & 1))
        return ((4 - (step >> 1)) & 3) * 2 + ((step & 1) ^ swapped)

    def rows_of(d):
        return pl.ds(pl.multiple_of((own_y ^ LAST_STEPS[d]) * size, size), size)

    for i, d in enumerate(ds):
        for j in range(groups):
            at = (own_y ^ LAST_STEPS[d]) * size + (own_z ^ Z_ORDER[j]) * own_rows
            target = weights_far.at[pl.ds(pl.multiple_of(at, own_rows), own_rows)]
            send(blocks[i].at[j, :, pl.ds(0, columns)], target)
    row = lax.broadcasted_iota(jnp.int32, (rank, 2 * rank), 0)
    column = lax.broadcasted_iota(jnp.int32, (rank, 2 * rank), 1)
    both = jnp.where((row == column) | (row + rank == column), 1.0, 0.0).astype(BF16)
    for i, d in enumerate(ds):
        pieces = [blocks[i][piece_of(z), :, columns:] for z in range(groups)]
        right = jnp.concatenate(pieces, axis=0)
        right_near[i] = native(both, right, 1, 1)
        send(right_near.at[i], right_far.at[:, rows_of(d)])
        approx = native(jnp.concatenate([right] * 3, axis=1), parts_ref[...], 1, 0)
        merged = grad_ref[rows_of(d), :].astype(F32) + feed_ref[rows_of(d), :].astype(F32)
        new_near[i] = (merged - approx).astype(BF16)
        send(new_near.at[i], new_far.at[rows_of(d)])
    for copy in copies:
        copy.wait()


def finish(name, ds, blocks, parts, gradient, feedback, begun=()):
    rows, columns = gradient.shape
    groups, own_rows, width = blocks[0].shape
    rank = (width - columns) // 2
    size = groups * own_rows
    count = len(ds)
    return call(
        lambda *refs: finish_kernel(ds, len(begun), *refs),
        [jax.ShapeDtypeStruct((rows, columns), BF16)] * 2
        + [jax.ShapeDtypeStruct((rank, rows), F32)],
        (*blocks, parts, gradient, feedback),
        (count * 3 * 10**8, count * 1_500_000),
        name,
        aliases={count + 3 + i: i for i in range(len(begun))},
        out_specs=[pl.BlockSpec(memory_space=pl.ANY)] * 3,
        spare=begun,
        scratch=[
            pltpu.VMEM((count, size, columns), BF16),
            pltpu.VMEM((count, rank, size), F32),
            pltpu.SemaphoreType.DMA((count * (groups + 2),)),
        ],
    )


def on_device(gradient, feedback, warm_start, master, moment, second):
    replicas = lax.axis_size("rep")
    gradient, feedback = gradient[0], feedback[0]

    pieces, gradient, feedback = local_factor(warm_start.T, gradient, feedback)
    quarter = sum_four([pieces[0]] + [exchange(p, "rep", d) for p, d in zip(pieces[1:], Y_STEPS)])
    for distance in Z_SUM_STEPS:
        quarter = quarter + exchange(quarter, "rep", distance)
    quarter = quarter / replicas
    quarters = [quarter] + [exchange(quarter, "rep", Z_SIZE * d) for d in GATHER_STEPS[1:]]
    factor_t, parts, gram_term = assemble(quarters)

    gram_pair = gram_term + exchange(gram_term, "shard", 1)
    packed = project(gradient, feedback, parts, replicas)
    gram_pair, packed = lax.optimization_barrier((gram_pair, packed))
    received = lax.all_to_all(packed, "rep", 0, 0, tiled=True)
    gram = sum_four([gram_pair] + [exchange(gram_pair, "shard", d) for d in X_STEPS[::-1]])
    inverse, unit_t, unit_parts = invert(gram, factor_t)
    received, inverse, unit_t, unit_parts = lax.optimization_barrier(
        (received, inverse, unit_t, unit_parts)
    )
    own_sum = shard_sum(received.sum(0))

    send, master_out, moment_out, second_out = update(
        replicas, own_sum, inverse, unit_t, master, moment, second
    )
    pair = jnp.stack([send, exchange(send, "rep", 1)])
    column = jnp.concatenate([pair] + [exchange(pair, "rep", d) for d in Z_PAIRS])
    others = [exchange(column, "rep", Z_SIZE * d) for d in LAST_STEPS[1:]]
    rest = (unit_parts, gradient, feedback)
    begun = finish("finish_own", (0,), [column], *rest)
    begun = finish("finish_far", (3,), others[2:], *rest, begun)
    new_feedback, weights, right_t = finish("finish_near", (1, 2), others[:2], *rest, begun)
    return (new_feedback[None], weights, master_out, moment_out, second_out, right_t.T)


def solution(mesh):
    return jax.shard_map(
        on_device,
        mesh=mesh,
        in_specs=(
            P("rep", None, "shard"),
            P("rep", None, "shard"),
            P(),
            P("rep", "shard"),
            P("rep", "shard"),
            P("rep", "shard"),
        ),
        out_specs=(
            P("rep", None, "shard"),
            P(None, "shard"),
            P("rep", "shard"),
            P("rep", "shard"),
            P("rep", "shard"),
            P(),
        ),
        check_vma=False,
    )
```

```python
import jax
import jax.numpy as jnp
from jax import lax
from jax.experimental import pallas as pl
from jax.experimental.pallas import tpu as pltpu
from jax.sharding import PartitionSpec as P

HIGHEST = lax.Precision.HIGHEST
beta_one = 0.9
beta_two = 0.95
learn_rate = 0.02
decay_rate = 0.1
adam_eps = 1e-08
ridge_rate = 1e-06

F32 = jnp.float32
BF16 = jnp.bfloat16
Y_SIZE, Z_SIZE = 4, 8
Y_STEPS = (8, 16, 24)
X_STEPS = (2, 4, 6)
Z_SUM_STEPS = (1, 3, 7)
Z_PAIRS = (6, 5, 2)
Z_ORDER = tuple(pair ^ bit for pair in (0,) + Z_PAIRS for bit in (0, 1))
LAST_STEPS = (0, 3, 1, 2)
GATHER_STEPS = (0, 3, 2, 1)
ROW_BLOCKS = 4


def exact(left, right, left_dim, right_dim):
    return lax.dot_general(
        left,
        right,
        (((left_dim,), (right_dim,)), ((), ())),
        precision=HIGHEST,
        preferred_element_type=F32,
    )


def native(left, right, left_dim, right_dim):
    return lax.dot_general(
        left, right, (((left_dim,), (right_dim,)), ((), ())), preferred_element_type=F32
    )


def three_parts(value):
    high = value.astype(BF16)
    rest = value - high.astype(F32)
    middle = rest.astype(BF16)
    return high, middle, (rest - middle.astype(F32)).astype(BF16)


def exchange(value, axis, distance):
    return lax.ppermute(value, axis, [(i, i ^ distance) for i in range(lax.axis_size(axis))])


def sum_four(terms):
    return (terms[0] + terms[1]) + (terms[2] + terms[3])


def shard_sum(value):
    value = value + exchange(value, "shard", 1)
    return sum_four([value] + [exchange(value, "shard", d) for d in X_STEPS[::-1]])


def call(kernel, outs, args, cost, name, aliases=None, out_specs=None, spare=(), scratch=()):
    specs = [pl.BlockSpec(memory_space=pltpu.VMEM)] * len(args)
    specs += [pl.BlockSpec(memory_space=pl.ANY)] * len(spare)
    flops, traffic = cost
    return pl.pallas_call(
        kernel,
        out_shape=outs,
        in_specs=specs,
        out_specs=out_specs or [pl.BlockSpec(memory_space=pltpu.VMEM)] * len(outs),
        scratch_shapes=scratch,
        input_output_aliases=aliases or {},
        compiler_params=pltpu.CompilerParams(vmem_limit_bytes=16 * 2**20),
        cost_estimate=pl.CostEstimate(flops=flops, bytes_accessed=traffic, transcendentals=0),
        name=name,
    )(*[pltpu.with_memory_space_constraint(v, pltpu.VMEM) for v in args], *spare)


def factor_kernel(warm_far, grad_far, feed_far, *refs):
    outs, (grad_ref, feed_ref, warm_ref, parts_ref, total_ref, sems) = refs[:Y_SIZE], refs[Y_SIZE:]
    rank, rows = warm_ref.shape
    quarter = outs[0].shape[1]
    size = rows // ROW_BLOCKS
    warm_copy = pltpu.make_async_copy(warm_far, warm_ref, sems.at[2 * ROW_BLOCKS])
    warm_copy.start()
    copies = []
    for i in range(ROW_BLOCKS):
        at = pl.ds(i * size, size)
        for k, (far, ref) in enumerate([(grad_far, grad_ref), (feed_far, feed_ref)]):
            copies.append(pltpu.make_async_copy(far.at[at], ref.at[at], sems.at[2 * i + k]))
            copies[-1].start()
    warm_copy.wait()
    for i, part in enumerate(three_parts(warm_ref[...])):
        parts_ref[i * rank : (i + 1) * rank, :] = part
    total = None
    for i in range(ROW_BLOCKS):
        at = slice(i * size, (i + 1) * size)
        copies[2 * i].wait()
        copies[2 * i + 1].wait()
        parts = parts_ref[:, at]
        term = native(parts, grad_ref[at, :], 1, 0) + native(parts, feed_ref[at, :], 1, 0)
        total = term if total is None else total + term
    total_ref[...] = (total[2 * rank :] + total[rank : 2 * rank]) + total[:rank]
    own = lax.axis_index("rep") // Z_SIZE
    for d, out in enumerate(outs):
        out[...] = total_ref[:, pl.ds(pl.multiple_of((own ^ d) * quarter, quarter), quarter)]


def local_factor(warm_t, gradient, feedback):
    rank, rows = warm_t.shape
    columns = gradient.shape[1]
    near = pltpu.VMEM((rows, columns), BF16)
    args = [pltpu.with_memory_space_constraint(v, pltpu.HBM) for v in (warm_t, gradient, feedback)]
    outs = pl.pallas_call(
        factor_kernel,
        out_shape=[pltpu.VMEM((rank, columns // Y_SIZE), F32)] * Y_SIZE + [near] * 2,
        in_specs=[pl.BlockSpec(memory_space=pl.ANY)] * 3,
        out_specs=[pl.BlockSpec(memory_space=pltpu.VMEM)] * (Y_SIZE + 2),
        scratch_shapes=[
            pltpu.VMEM((rank, rows), F32),
            pltpu.VMEM((3 * rank, rows), BF16),
            pltpu.VMEM((rank, columns), F32),
            pltpu.SemaphoreType.DMA((2 * ROW_BLOCKS + 1,)),
        ],
        compiler_params=pltpu.CompilerParams(vmem_limit_bytes=16 * 2**20),
        cost_estimate=pl.CostEstimate(flops=10**9, bytes_accessed=2_500_000, transcendentals=0),
        name="local_factor",
    )(*args)
    return outs[:Y_SIZE], outs[Y_SIZE], outs[Y_SIZE + 1]


def assemble_kernel(*refs):
    quarters, (factor_ref, parts_ref, gram_ref) = refs[:Y_SIZE], refs[Y_SIZE:]
    rank, quarter = quarters[0].shape
    own = lax.axis_index("rep") // Z_SIZE
    for d, block in zip(GATHER_STEPS, quarters):
        at = pl.ds(pl.multiple_of((own ^ d) * quarter, quarter), quarter)
        factor_ref[:, at] = block[...]
    factor = factor_ref[...]
    for i, part in enumerate(three_parts(factor)):
        parts_ref[i * rank : (i + 1) * rank, :] = part
    gram_ref[...] = exact(factor, factor, 1, 1)


def assemble(quarters):
    rank, quarter = quarters[0].shape
    columns = quarter * Y_SIZE
    outs = [
        pltpu.VMEM((rank, columns), F32),
        pltpu.VMEM((3 * rank, columns), BF16),
        pltpu.VMEM((rank, rank), F32),
    ]
    return call(assemble_kernel, outs, tuple(quarters), (10**8, 500_000), "assemble_factor")


def project_kernel(grad_ref, feed_ref, parts_ref, out_ref):
    replicas, half, _ = out_ref.shape
    rows = grad_ref.shape[0]
    rank = parts_ref.shape[0] // 3
    parts = parts_ref[...]
    groups = 8
    size = rows // replicas * groups

    for i in range(replicas // groups):
        at = slice(i * size, (i + 1) * size)
        total = native(grad_ref[at, :], parts, 1, 1) + native(feed_ref[at, :], parts, 1, 1)
        value = (total[:, 2 * rank :] + total[:, rank : 2 * rank]) + total[:, :rank]
        value = value.reshape(groups, 2, half, rank)
        out_ref[i * groups : (i + 1) * groups] = jnp.concatenate([value[:, 0], value[:, 1]], axis=-1)


def project(gradient, feedback, parts, replicas):
    rank = parts.shape[0] // 3
    half = gradient.shape[0] // replicas // 2
    outs = [pltpu.VMEM((replicas, half, 2 * rank), F32)]
    return call(
        project_kernel, outs, (gradient, feedback, parts), (10**9, 2_500_000), "project"
    )[0]


def inverse_kernel(gram_ref, factor_ref, inverse_ref, unit_ref, parts_ref):
    rank = gram_ref.shape[0]
    width = 8
    row = lax.broadcasted_iota(jnp.int32, (rank, rank), 0)
    column = lax.broadcasted_iota(jnp.int32, (rank, rank), 1)
    diagonal = row == column
    gram = gram_ref[...]
    trace = jnp.sum(jnp.where(diagonal, gram, 0.0))
    gram = gram + jnp.where(diagonal, ridge_rate * trace / rank, 0.0)
    table = jnp.concatenate([gram, jnp.where(diagonal, 1.0, 0.0)], axis=1)
    row = lax.broadcasted_iota(jnp.int32, table.shape, 0)
    pivots = jnp.ones(table.shape, F32)
    for k in range(0, rank, width):
        ahead = [jnp.broadcast_to(table[:, c : c + 1], table.shape) for c in range(k, k + width)]
        lines = [table[c : c + 1, :] for c in range(k, k + width)]
        for i in range(width):
            at = k + i
            pivot = ahead[i][at : at + 1, :]
            pivots = jnp.where(row == at, pivot, pivots)
            scale = jnp.where(row > at, ahead[i] * (1.0 / pivot), 0.0)
            for j in range(i + 1, width):
                entry = ahead[j][at : at + 1, :]
                ahead[j] = ahead[j] - scale * entry
                lines[j] = lines[j] - scale[k + j : k + j + 1, :] * lines[i]
            table = table - scale * lines[i]
    inverse = table[:, rank:] / jnp.sqrt(pivots[:, rank:])
    inverse_ref[...] = inverse
    unit = exact(inverse, factor_ref[...], 1, 0)
    unit_ref[...] = unit
    for i, part in enumerate(three_parts(unit)):
        parts_ref[2 * i * rank : (2 * i + 1) * rank, :] = part
        parts_ref[(2 * i + 1) * rank : (2 * i + 2) * rank, :] = part


def invert(gram, factor_t):
    rank, columns = factor_t.shape
    outs = [
        pltpu.VMEM((rank, rank), F32),
        pltpu.VMEM((rank, columns), F32),
        pltpu.VMEM((6 * rank, columns), BF16),
    ]
    return call(inverse_kernel, outs, (gram, factor_t), (2 * 10**9, 500_000), "invert")


def update_kernel(replicas, sum_ref, inverse_ref, unit_ref, master_ref, moment_ref,
                  second_ref, send_ref, master_out, moment_out, second_out):
    rank = inverse_ref.shape[0]
    columns = master_ref.shape[1]
    packed = sum_ref[...]
    own = jnp.concatenate([packed[:, :rank], packed[:, rank:]], axis=0)
    right = exact(own, inverse_ref[...], 1, 1) / replicas
    grad = exact(right, unit_ref[...], 1, 0)
    moment = beta_one * moment_ref[...] + (1.0 - beta_one) * grad
    second = beta_two * second_ref[...] + (1.0 - beta_two) * grad * grad
    master = master_ref[...]
    master = master - learn_rate * (
        moment / (jnp.sqrt(second) + adam_eps) + decay_rate * master
    )
    moment_out[...] = moment
    second_out[...] = second
    master_out[...] = master
    high = right.astype(BF16).astype(F32)
    send_ref[:, :columns] = master.astype(BF16)
    send_ref[:, columns:] = jnp.concatenate([high, right - high], axis=1).astype(BF16)


def update(replicas, own_sum, inverse, unit_t, master, moment, second):
    rows, columns = master.shape
    rank = inverse.shape[0]
    block = pltpu.VMEM(master.shape, F32)
    outs = [pltpu.VMEM((rows, columns + 2 * rank), BF16), block, block, block]
    args = (own_sum, inverse, unit_t, master, moment, second)
    kernel = lambda *refs: update_kernel(replicas, *refs)
    return call(kernel, outs, args, (5 * 10**7, 600_000), "update")


def finish_kernel(ds, begun, *refs):
    count = len(ds)
    blocks, (parts_ref, grad_ref, feed_ref) = refs[:count], refs[count : count + 3]
    new_far, weights_far, right_far, new_near, right_near, sems = refs[count + 3 + begun :]
    columns = grad_ref.shape[1]
    groups, own_rows, width = blocks[0].shape
    size = groups * own_rows
    rank = (width - columns) // 2
    own_y, own_z = lax.axis_index("rep") // Z_SIZE, lax.axis_index("rep") % Z_SIZE
    copies = []

    def send(source, target):
        copies.append(pltpu.make_async_copy(source, target, sems.at[len(copies)]))
        copies[-1].start()

    def piece_of(z):
        step = own_z ^ z
        swapped = (step >> 2) & (1 - ((step >> 1) & 1))
        return ((4 - (step >> 1)) & 3) * 2 + ((step & 1) ^ swapped)

    def rows_of(d):
        return pl.ds(pl.multiple_of((own_y ^ LAST_STEPS[d]) * size, size), size)

    for i, d in enumerate(ds):
        for j in range(groups):
            at = (own_y ^ LAST_STEPS[d]) * size + (own_z ^ Z_ORDER[j]) * own_rows
            target = weights_far.at[pl.ds(pl.multiple_of(at, own_rows), own_rows)]
            send(blocks[i].at[j, :, pl.ds(0, columns)], target)
    row = lax.broadcasted_iota(jnp.int32, (rank, 2 * rank), 0)
    column = lax.broadcasted_iota(jnp.int32, (rank, 2 * rank), 1)
    both = jnp.where((row == column) | (row + rank == column), 1.0, 0.0).astype(BF16)
    for i, d in enumerate(ds):
        pieces = [blocks[i][piece_of(z), :, columns:] for z in range(groups)]
        right = jnp.concatenate(pieces, axis=0)
        right_near[i] = native(both, right, 1, 1)
        send(right_near.at[i], right_far.at[:, rows_of(d)])
        approx = native(jnp.concatenate([right] * 3, axis=1), parts_ref[...], 1, 0)
        merged = grad_ref[rows_of(d), :].astype(F32) + feed_ref[rows_of(d), :].astype(F32)
        new_near[i] = (merged - approx).astype(BF16)
        send(new_near.at[i], new_far.at[rows_of(d)])
    for copy in copies:
        copy.wait()


def finish(name, ds, blocks, parts, gradient, feedback, begun=()):
    rows, columns = gradient.shape
    groups, own_rows, width = blocks[0].shape
    rank = (width - columns) // 2
    size = groups * own_rows
    count = len(ds)
    return call(
        lambda *refs: finish_kernel(ds, len(begun), *refs),
        [jax.ShapeDtypeStruct((rows, columns), BF16)] * 2
        + [jax.ShapeDtypeStruct((rank, rows), F32)],
        (*blocks, parts, gradient, feedback),
        (count * 3 * 10**8, count * 1_500_000),
        name,
        aliases={count + 3 + i: i for i in range(len(begun))},
        out_specs=[pl.BlockSpec(memory_space=pl.ANY)] * 3,
        spare=begun,
        scratch=[
            pltpu.VMEM((count, size, columns), BF16),
            pltpu.VMEM((count, rank, size), F32),
            pltpu.SemaphoreType.DMA((count * (groups + 2),)),
        ],
    )


def on_device(gradient, feedback, warm_start, master, moment, second):
    replicas = lax.axis_size("rep")
    gradient, feedback = gradient[0], feedback[0]

    pieces, gradient, feedback = local_factor(warm_start.T, gradient, feedback)
    quarter = sum_four(
        [pieces[0]] + [exchange(pieces[d], "rep", Z_SIZE * d) for d in GATHER_STEPS[1:]]
    )
    for distance in Z_SUM_STEPS:
        quarter = quarter + exchange(quarter, "rep", distance)
    quarter = quarter / replicas
    quarters = [quarter] + [exchange(quarter, "rep", Z_SIZE * d) for d in GATHER_STEPS[1:]]
    factor_t, parts, gram_term = assemble(quarters)

    gram_pair = gram_term + exchange(gram_term, "shard", 1)
    packed = project(gradient, feedback, parts, replicas)
    gram_pair, packed = lax.optimization_barrier((gram_pair, packed))
    received = lax.all_to_all(packed, "rep", 0, 0, tiled=True)
    gram = sum_four([gram_pair] + [exchange(gram_pair, "shard", d) for d in X_STEPS[::-1]])
    inverse, unit_t, unit_parts = invert(gram, factor_t)
    received, inverse, unit_t, unit_parts = lax.optimization_barrier(
        (received, inverse, unit_t, unit_parts)
    )
    own_sum = shard_sum(received.sum(0))

    send, master_out, moment_out, second_out = update(
        replicas, own_sum, inverse, unit_t, master, moment, second
    )
    pair = jnp.stack([send, exchange(send, "rep", 1)])
    column = jnp.concatenate([pair] + [exchange(pair, "rep", d) for d in Z_PAIRS])
    others = [exchange(column, "rep", Z_SIZE * d) for d in LAST_STEPS[1:]]
    rest = (unit_parts, gradient, feedback)
    begun = finish("finish_own", (0,), [column], *rest)
    begun = finish("finish_far", (3,), others[2:], *rest, begun)
    new_feedback, weights, right_t = finish("finish_near", (1, 2), others[:2], *rest, begun)
    return (new_feedback[None], weights, master_out, moment_out, second_out, right_t.T)


def solution(mesh):
    return jax.shard_map(
        on_device,
        mesh=mesh,
        in_specs=(
            P("rep", None, "shard"),
            P("rep", None, "shard"),
            P(),
            P("rep", "shard"),
            P("rep", "shard"),
            P("rep", "shard"),
        ),
        out_specs=(
            P("rep", None, "shard"),
            P(None, "shard"),
            P("rep", "shard"),
            P("rep", "shard"),
            P("rep", "shard"),
            P(),
        ),
        check_vma=False,
    )
```
